32 devices in a mesh: dp: 16 (over z, y, core), tensor: 2 (over x).
Axes of the slice: x: 2, y: 2, z: 4, core: 2. Of those that a mesh axis runs over, the one named last changes fastest.
Arguments:
- hidden_in: bfloat16 [32768, 768], P('dp'), may hold values from -6 to 6
- pair_lengths: int32 [64], P('dp'), may hold values from 64 to 512
- candidates: int32 [64], P('dp'), may hold values from 2 to 64
- qkv_weight: bfloat16 [3, 768, 768], P(None, None, 'tensor'), may hold values from -0.21875 to 0.21875
- qv_bias: float32 [2, 768], P(None, 'tensor'), may hold values from -3 to 3
- out_weight: bfloat16 [768, 768], P('tensor'), may hold values from -1.75 to 1.75
- out_bias: float32 [768], replicated, may hold values from -3 to 3
- norm1_gain: float32 [768], replicated, may hold values from 0.5 to 1.5
- norm1_shift: float32 [768], replicated, may hold values from -3 to 3
- up_weight: bfloat16 [768, 3072], P(None, 'tensor'), may hold values from -0.21875 to 0.21875
- up_bias: float32 [3072], P('tensor'), may hold values from -3 to 3
- down_weight: bfloat16 [3072, 768], P('tensor'), may hold values from -0.109375 to 0.109375
- down_bias: float32 [768], replicated, may hold values from -3 to 3
- norm2_gain: float32 [768], replicated, may hold values from 0.5 to 1.5
- norm2_shift: float32 [768], replicated, may hold values from -3 to 3
- out_cotangent: bfloat16 [32768, 768], P('dp'), may hold values from -48 to 48
Outputs:
- block_out: bfloat16 [32768, 768], P('dp')
- grad_in: bfloat16 [32768, 768], P('dp')
- grad_qkv_weight: float32 [3, 768, 768], P(None, 'dp', 'tensor')
- grad_qv_bias: float32 [2, 768], P(None, ('tensor', 'dp'))
- grad_out_weight: float32 [768, 768], P('tensor', 'dp')
- grad_out_bias: float32 [768], P('dp')
- grad_norm1_gain: float32 [768], P('dp')
- grad_norm1_shift: float32 [768], P('dp')
- grad_up_weight: float32 [768, 3072], P('dp', 'tensor')
- grad_up_bias: float32 [3072], P(('tensor', 'dp'))
- grad_down_weight: float32 [3072, 768], P('tensor', 'dp')
- grad_down_bias: float32 [768], P('dp')
- grad_norm2_gain: float32 [768], P('dp')
- grad_norm2_shift: float32 [768], P('dp')
The draws below stay inside these ranges and needn't reach their ends.
All inputs are finite; a program needn't handle non-finite values.
Results may differ from the reference program's by a relative error of at most 0.02.
The reference program's roundings to bfloat16 on the way count: a program that leaves them out, or rounds other values in their place, can miss the bound.
Values may be sent and summed in bfloat16 or wider, within the bound.
No kernel may reach another device: no remote copies, remote signals or barrier semaphores. Data moves between devices by JAX's collectives and lax.ppermute only.
A program may use at most 192 MiB of HBM per device.

```python
import jax
import jax.numpy as jnp
from jax import lax

D = 768
HEADS = 12
HEAD_DIM = 64
FF = 3072
LEN = 512
SEQ_DEV = 4
PAIRS = 64
TOKENS = 32768
N_DP = 16
N_TENSOR = 2


def plant(entries, own_key, least, top_value):
    place = [jax.random.randint(jax.random.fold_in(own_key, axis), (), 0, length) for axis, length in enumerate(entries.shape)]
    widest = entries.shape.index(max(entries.shape))
    neighbour = place[:widest] + [(place[widest] + 1) % entries.shape[widest]] + place[widest + 1:]
    return entries.at[tuple(place)].set(least).at[tuple(neighbour)].set(top_value)


def strengthened(result, own_key, source, target, parts, factor):
    owner, partner = [(jnp.arange(result.shape[position]) // (result.shape[position] // parts)).reshape([-1 if axis == position else 1 for axis in range(result.ndim)]) for position in (source, target)]
    chosen = jax.random.permutation(own_key, parts)[partner]
    strong = (owner == chosen) | (owner == (partner + parts // 2) % parts)
    return jnp.where(strong, factor * result, result)


def block_levels(key, shape, cuts, low, top_value):
    def one(dim, shards_of):
        heights = jax.random.uniform(jax.random.fold_in(jax.random.fold_in(key, 6), dim), (shards_of,), jnp.float32, low / len(cuts), top_value / len(cuts))
        return jnp.repeat(jnp.exp(heights), shape[dim] // shards_of).reshape((-1,) + (1,) * (len(shape) - dim - 1))

    loudness = one(*cuts[0])
    for cut in cuts[1:]:
        loudness = loudness * one(*cut)
    return loudness


def centred(rng, dims, scale, limit, cuts=(), held_as=jnp.bfloat16):
    values = scale * jax.random.normal(rng, dims, jnp.float32)
    if cuts:
        values = values * block_levels(rng, dims, cuts, -0.22, 0.18)
    return jnp.clip(values, -limit, limit).astype(held_as)


def gaussian_with(stream_key, extent, scale, reach, split, heavy, kind=jnp.bfloat16):
    drawn = scale * jax.random.normal(stream_key, extent, jnp.float32)
    if split:
        drawn = drawn * block_levels(stream_key, extent, split, -0.22, 0.18)
    return jnp.clip(strengthened(drawn, jax.random.fold_in(stream_key, 3), *heavy), -reach, reach).astype(kind)


def setup_inputs(seed: int = 0) -> dict:
    seeds = jax.random.split(jax.random.key(seed), 17)
    hidden_in = gaussian_with(seeds[0], (TOKENS, D), 1.0, 6.0, ((0, 16),), (0, 1, 16, 2.0))
    pair_lengths = plant(jax.random.randint(seeds[1], (PAIRS,), LEN // 8, LEN + 1), jax.random.fold_in(seeds[1], 1), LEN // 8, LEN).astype(jnp.int32)
    candidates = plant(jax.random.randint(seeds[2], (PAIRS,), 2, 65), jax.random.fold_in(seeds[2], 1), 2, 64).astype(jnp.int32)
    qkv_weight = centred(seeds[3], (3, D, D), D ** -0.5, 0.21875, ((2, 2),))
    qv_bias = centred(seeds[4], (2, D), 0.5, 3.0, ((1, 2),), jnp.float32)
    out_weight = centred(seeds[5], (D, D), (D // 64) ** -0.5, 1.75, ((0, 2),))
    out_bias = centred(seeds[6], (D,), 0.5, 3.0, (), jnp.float32)
    norm1_gain = jnp.clip(1.0 + 0.1 * jax.random.normal(seeds[7], (D,), jnp.float32), 0.5, 1.5)
    norm1_shift = centred(seeds[8], (D,), 0.5, 3.0, (), jnp.float32)
    up_weight = centred(seeds[9], (D, FF), D ** -0.5, 0.21875, ((1, 2),))
    up_bias = centred(seeds[10], (FF,), 0.5, 3.0, ((0, 2),), jnp.float32)
    down_weight = centred(seeds[11], (FF, D), FF ** -0.5, 0.109375, ((0, 2),))
    down_bias = centred(seeds[12], (D,), 0.5, 3.0, (), jnp.float32)
    norm2_gain = jnp.clip(1.0 + 0.1 * jax.random.normal(seeds[13], (D,), jnp.float32), 0.5, 1.5)
    norm2_shift = centred(seeds[14], (D,), 0.5, 3.0, (), jnp.float32)
    out_cotangent = gaussian_with(seeds[15], (TOKENS, D), 8.0, 48.0, ((0, 16),), (0, 1, 16, 2.0))
    return {"hidden_in": hidden_in, "pair_lengths": pair_lengths, "candidates": candidates, "qkv_weight": qkv_weight, "qv_bias": qv_bias, "out_weight": out_weight, "out_bias": out_bias, "norm1_gain": norm1_gain, "norm1_shift": norm1_shift, "up_weight": up_weight, "up_bias": up_bias, "down_weight": down_weight, "down_bias": down_bias, "norm2_gain": norm2_gain, "norm2_shift": norm2_shift, "out_cotangent": out_cotangent}


@jax.custom_vjp
def low(v):
    return lax.optimization_barrier(v.astype(jnp.bfloat16)).astype(jnp.float32)

@jax.custom_vjp
def low_back(v):
    return v

def low_keep(v):
    return (low(v), None)

def low_pass(kept, grad):
    return (grad,)

def back_keep(v):
    return (v, None)

def back_low(kept, grad):
    return (low(grad),)
low.defvjp(low_keep, low_pass)
low_back.defvjp(back_keep, back_low)
NORM_EPSILON = 1e-12
HALF_ROOT = 0.7071067811865476
PRECISE = lax.Precision.HIGHEST

def norm_rows(hidden, norm_gain, norm_shift):
    row_mean = lax.optimization_barrier(jnp.mean(hidden, axis=-1, keepdims=True))
    centered = hidden - row_mean
    variance = lax.optimization_barrier(jnp.mean(centered * centered, axis=-1, keepdims=True))
    return centered * lax.rsqrt(variance + NORM_EPSILON) * norm_gain + norm_shift

def gelu_exact(inputs):
    return 0.5 * inputs * (1.0 + lax.erf(inputs * HALF_ROOT))

def attend_pair(queries, key_rows, values, length):
    scores = jnp.einsum('qhe,khe->hqk', queries, key_rows, precision=PRECISE) * HEAD_DIM ** (-0.5)
    valid_keys = jnp.arange(key_rows.shape[0], dtype=jnp.int32) < length.astype(jnp.int32)
    scores = low_back(jnp.where(valid_keys[None, None, :], scores, -1000000000.0))
    row_peak = lax.optimization_barrier(jnp.max(scores, axis=-1, keepdims=True))
    exponent = jnp.exp(scores - row_peak)
    probs = exponent / lax.optimization_barrier(jnp.sum(exponent, axis=-1, keepdims=True))
    return jnp.einsum('hqk,khe->qhe', low(probs), values, precision=PRECISE)

def encoder_block(hidden, lengths, params):
    qkv_weight, qv_bias, out_weight, out_bias, norm1_gain, norm1_shift, up_weight, up_bias, down_weight, down_bias, norm2_gain, norm2_shift = params
    flat_rows = hidden.reshape(-1, D)
    pair_shape = (hidden.shape[0], LEN, HEADS, HEAD_DIM)
    queries = low_back(low(jnp.dot(flat_rows, qkv_weight[0], precision=PRECISE) + qv_bias[0]))
    key_rows = low_back(low(jnp.dot(flat_rows, qkv_weight[1], precision=PRECISE)))
    values = low_back(low(jnp.dot(flat_rows, qkv_weight[2], precision=PRECISE) + qv_bias[1]))
    attend = jax.checkpoint(attend_pair)

    def per_pair(pieces):
        return attend(pieces[0], pieces[1], pieces[2], pieces[3])
    context = lax.map(per_pair, (queries.reshape(pair_shape), key_rows.reshape(pair_shape), values.reshape(pair_shape), lengths))
    context = low_back(low(context.reshape(-1, D)))
    group_width = D // N_TENSOR
    attention_parts = jnp.einsum('ntc,tcd->tnd', context.reshape(-1, N_TENSOR, group_width), out_weight.reshape(N_TENSOR, group_width, D), precision=PRECISE)
    attention_out = low_back(lax.optimization_barrier(jnp.sum(low(attention_parts), axis=0))) + out_bias
    normed_one = norm_rows(flat_rows + attention_out, norm1_gain, norm1_shift)
    pre_activation = low_back(jnp.dot(low(normed_one), up_weight, precision=PRECISE) + up_bias)
    activation = low(gelu_exact(pre_activation))
    hidden_width = FF // N_TENSOR
    feedforward_parts = jnp.einsum('ntc,tcd->tnd', activation.reshape(-1, N_TENSOR, hidden_width), down_weight.reshape(N_TENSOR, hidden_width, D), precision=PRECISE)
    feedforward_out = low_back(lax.optimization_barrier(jnp.sum(low(feedforward_parts), axis=0))) + down_bias
    return norm_rows(normed_one + feedforward_out, norm2_gain, norm2_shift).reshape(hidden.shape)

def reference(hidden_in, pair_lengths, candidates, qkv_weight, qv_bias, out_weight, out_bias, norm1_gain, norm1_shift, up_weight, up_bias, down_weight, down_bias, norm2_gain, norm2_shift, out_cotangent):
    params = (qkv_weight.astype(jnp.float32), qv_bias.astype(jnp.float32), out_weight.astype(jnp.float32), out_bias.astype(jnp.float32), norm1_gain.astype(jnp.float32), norm1_shift.astype(jnp.float32), up_weight.astype(jnp.float32), up_bias.astype(jnp.float32), down_weight.astype(jnp.float32), down_bias.astype(jnp.float32), norm2_gain.astype(jnp.float32), norm2_shift.astype(jnp.float32))
    hidden = hidden_in.astype(jnp.float32).reshape(N_DP, SEQ_DEV, LEN, D)
    weighting = candidates.astype(jnp.float32).reshape(N_DP, SEQ_DEV, 1, 1)
    cotangent = out_cotangent.astype(jnp.float32).reshape(N_DP, SEQ_DEV, LEN, D) / weighting
    lengths = pair_lengths.astype(jnp.int32).reshape(N_DP, SEQ_DEV)
    zero_grads = jax.tree.map(jnp.zeros_like, params)

    def scan_step(summed, pieces):
        group_hidden, group_lengths, group_cotangent = pieces

        def forward(inputs, weights):
            return encoder_block(inputs, group_lengths, weights)
        layer_out, pullback = jax.vjp(forward, group_hidden, params)
        grad_hidden, grad_params = pullback(group_cotangent)
        return (jax.tree.map(jnp.add, summed, grad_params), (layer_out, grad_hidden))
    summed, outputs = lax.scan(scan_step, zero_grads, (hidden, lengths, cotangent))
    layer_out, grad_hidden = outputs
    return (layer_out.reshape(TOKENS, D).astype(jnp.bfloat16), grad_hidden.reshape(TOKENS, D).astype(jnp.bfloat16), summed[0], summed[1], summed[2], summed[3], summed[4], summed[5], summed[6], summed[7], summed[8], summed[9], summed[10], summed[11])
```

```python
import functools

import jax
import jax.numpy as jnp
from jax import lax
from jax.experimental import pallas as pl
from jax.experimental.pallas import tpu as pltpu
from jax.sharding import PartitionSpec as P

HEAD_DIM = 64
LANES = 128
VMEM_BYTES = 60 * 1024 * 1024
NORM_EPSILON = 1e-12
HALF_ROOT = 0.7071067811865476
INVERSE_ROOT_TWO_PI = 0.3989422804014327
SCORE_SCALE = HEAD_DIM ** (-0.5)
NT = (((1,), (1,)), ((), ()))
NN = (((1,), (0,)), ((), ()))
TN = (((0,), (0,)), ((), ()))
F32 = jnp.float32
BF16 = jnp.bfloat16


def product(left, right, dims):
    return lax.dot_general(left, right, dims, preferred_element_type=F32)


def head_halves(block):
    lane = lax.broadcasted_iota(jnp.int32, (1, LANES), 1)
    zero = jnp.zeros_like(block)
    return jnp.where(lane < HEAD_DIM, block, zero), jnp.where(lane < HEAD_DIM, zero, block)


def call(kernel, name, meta, grid, inputs, outputs, flops, moved, exps=0, scratch=()):
    return pl.pallas_call(
        kernel,
        out_shape=[jax.ShapeDtypeStruct(shape, dtype) for shape, dtype, spec in outputs],
        grid_spec=pltpu.PrefetchScalarGridSpec(
            num_scalar_prefetch=1,
            grid=grid,
            in_specs=[spec for array, spec in inputs],
            out_specs=[spec for shape, dtype, spec in outputs],
            scratch_shapes=list(scratch),
        ),
        cost_estimate=pl.CostEstimate(flops=flops, bytes_accessed=moved, transcendentals=exps),
        name=name,
    )(meta, *[array for array, spec in inputs])


def attend_kernel(meta_ref, length_ref, qkv_ref, context_ref, total_ref):
    length = length_ref[meta_ref[1] * pl.num_programs(0) + pl.program_id(0)]
    keys = qkv_ref[:, LANES : 2 * LANES] * SCORE_SCALE
    valid = lax.broadcasted_iota(jnp.int32, (keys.shape[0], 1), 0) < length
    heads = zip(head_halves(qkv_ref[:, :LANES]), head_halves(qkv_ref[:, 2 * LANES :]))
    flipped = None
    for head, (query, value) in enumerate(heads):
        scores = jnp.where(valid, product(keys, query, NT), -1000000000.0)
        peak = jnp.max(scores, axis=0, keepdims=True)
        exponent = jnp.exp(scores - peak)
        total = jnp.sum(exponent, axis=0, keepdims=True)
        probs_low = (exponent * (1.0 / total)).astype(BF16)
        part = product(value, probs_low, TN)
        flipped = part if flipped is None else flipped + part
        total_ref[0, 0, head : head + 1, :] = peak + jnp.log(total)
    context_ref[...] = flipped.T.astype(BF16)


def attend(meta, lengths, qkv, pairs):
    rows, columns = qkv.shape
    span, blocks = rows // pairs, columns // (3 * LANES)
    work = rows * span * blocks * LANES
    return call(
        attend_kernel,
        "attend",
        meta,
        (pairs, blocks),
        [
            (lengths, pl.BlockSpec(memory_space=pltpu.SMEM)),
            (qkv, pl.BlockSpec((span, 3 * LANES), lambda pair, lanes, meta: (pair, lanes))),
        ],
        [
            (
                (rows, blocks * LANES),
                BF16,
                pl.BlockSpec((span, LANES), lambda pair, lanes, meta: (pair, lanes)),
            ),
            (
                (pairs, blocks, 2, span),
                F32,
                pl.BlockSpec((1, 1, 2, span), lambda pair, lanes, meta: (pair, lanes, 0, 0)),
            ),
        ],
        flops=16 * work,
        moved=8 * rows * blocks * LANES,
        exps=work // HEAD_DIM,
    )


def attend_back_kernel(pair, pairs, meta_ref, length_ref, qkv_ref, grad_ref, total_ref, out_ref):
    length = length_ref[meta_ref[1] * pairs + pair]
    keys = qkv_ref[:, LANES : 2 * LANES] * SCORE_SCALE
    values = qkv_ref[:, 2 * LANES :]
    valid = lax.broadcasted_iota(jnp.int32, (keys.shape[0], 1), 0) < length
    heads = zip(head_halves(qkv_ref[:, :LANES]), head_halves(keys), head_halves(grad_ref[...]))
    sums = [None, None, None]
    for head, (query, key, grad) in enumerate(heads):
        scores = jnp.where(valid, product(keys, query, NT), -1000000000.0)
        probs = jnp.exp(scores - total_ref[0, 0, head : head + 1, :])
        grad_probs = product(values, grad, NT)
        weighted = probs * grad_probs
        inner = jnp.sum(weighted, axis=0, keepdims=True)
        grad_scores = (weighted - probs * inner).astype(BF16)
        parts = (
            product(grad_scores, key, TN),
            product(grad_scores, query, NN),
            product(probs.astype(BF16), grad, NN),
        )
        sums = [b if a is None else a + b for a, b in zip(sums, parts)]
    out_ref[:, :LANES] = sums[0].astype(BF16)
    out_ref[:, LANES : 2 * LANES] = (sums[1] * SCORE_SCALE).astype(BF16)
    out_ref[:, 2 * LANES :] = sums[2].astype(BF16)


def attend_back(meta, lengths, qkv, grad, totals, pair, pairs):
    rows, columns = qkv.shape
    span, blocks = rows // pairs, columns // (3 * LANES)
    work = span * span * blocks * LANES
    return call(
        functools.partial(attend_back_kernel, pair, pairs),
        "attend_back",
        meta,
        (blocks,),
        [
            (lengths, pl.BlockSpec(memory_space=pltpu.SMEM)),
            (qkv, pl.BlockSpec((span, 3 * LANES), lambda lanes, meta: (pair, lanes))),
            (grad, pl.BlockSpec((span, LANES), lambda lanes, meta: (pair, lanes))),
            (totals, pl.BlockSpec((1, 1, 2, span), lambda lanes, meta: (pair, lanes, 0, 0))),
        ],
        [((span, columns), BF16, pl.BlockSpec((span, 3 * LANES), lambda lanes, meta: (0, lanes)))],
        flops=28 * work,
        moved=14 * span * blocks * LANES,
        exps=work // HEAD_DIM,
    )[0]


def move_kernel(moves, source_count, meta_ref, *refs):
    sources = refs[:source_count]
    target_count = 1 + max(move[2] for move in moves)
    targets = refs[source_count : source_count + target_count]
    rest = refs[source_count + target_count :]
    buffers, arrived, left = rest[: len(moves)], rest[-2], rest[-1]
    incoming, outgoing = [], []
    for number, (source, start, target, place, rows) in enumerate(moves):
        into = sources[source].at[pl.ds(start(meta_ref), rows)]
        onto = targets[target].at[pl.ds(place(meta_ref), rows)]
        incoming.append(pltpu.make_async_copy(into, buffers[number], arrived.at[number]))
        outgoing.append(pltpu.make_async_copy(buffers[number], onto, left.at[number]))
    for copy in incoming:
        copy.start()
    for copy_in, copy_out in zip(incoming, outgoing):
        copy_in.wait()
        copy_out.start()
    for copy in outgoing:
        copy.wait()


def move(name, meta, sources, targets, moves):
    moved = sum(entry[4] * sources[entry[0]].shape[1] * 4 for entry in moves)
    return call(
        functools.partial(move_kernel, moves, len(sources)),
        name,
        meta,
        (1,),
        [(source, pl.BlockSpec(memory_space=pl.ANY)) for source in sources],
        [(shape, BF16, pl.BlockSpec(memory_space=pl.ANY)) for shape in targets],
        flops=0,
        moved=moved,
        scratch=[pltpu.VMEM((entry[4], sources[entry[0]].shape[1]), BF16) for entry in moves]
        + [pltpu.SemaphoreType.DMA((len(moves),))] * 2,
    )


def first_row(meta_ref):
    return 0


def by_place(entry, rows, other=False):
    def start(meta_ref):
        place = 1 - meta_ref[entry] if other else meta_ref[entry]
        return pl.multiple_of(place * rows, 16) if rows % 16 == 0 else place * rows

    return start


def pack(meta, weights):
    halves = [weight.shape[0] // 2 for weight in weights]
    return move(
        "pack",
        meta,
        weights,
        [(half, weight.shape[1]) for half, weight in zip(halves, weights)],
        [(i, by_place(0, half), i, first_row, half) for i, half in enumerate(halves)],
    )


def join(meta, entry, mine, other, name):
    rows = mine[0].shape[0]
    count = len(mine)
    moves = []
    for own, which in ((0, True), (1, False)):
        base = by_place(entry, rows * count, other=bool(own))
        for i in range(count):
            start = lambda meta_ref, base=base, i=i: pl.multiple_of(base(meta_ref) + i * rows, 16)
            moves.append((own * count + i, first_row, 0, start, rows))
    return move(name, meta, [*mine, *other], [(2 * count * rows, mine[0].shape[1])], moves)[0]


def normalized(rows):
    row_mean = jnp.mean(rows, axis=-1, keepdims=True)
    centered = rows - row_mean
    variance = jnp.mean(centered * centered, axis=-1, keepdims=True)
    scale = lax.rsqrt(variance + NORM_EPSILON)
    return centered * scale, scale


def norm_back(grad, xhat, scale, gain):
    inner = grad * gain
    mean = jnp.mean(inner, axis=-1, keepdims=True)
    along = jnp.mean(inner * xhat, axis=-1, keepdims=True)
    return scale * (inner - mean - xhat * along)


def low(value):
    return value.astype(BF16).astype(F32)


def gelu_pair(value):
    cdf = 0.5 + 0.5 * lax.erf(value * HALF_ROOT)
    slope = cdf + value * (jnp.exp(-0.5 * value * value) * INVERSE_ROOT_TWO_PI)
    return (value * cdf).astype(BF16), slope.astype(BF16)


def by_lane_pair(weight):
    count, rows, columns = weight.shape
    return weight.reshape(count, rows, -1, LANES).transpose(1, 2, 0, 3).reshape(rows, -1)


def swap_tensor(block):
    return lax.ppermute(block, "tensor", [(0, 1), (1, 0)])


def swap_dp(block, devices, stride):
    return lax.ppermute(block, "dp", [(place, place ^ stride) for place in range(devices)])


def boundary(*values):
    return lax.optimization_barrier(values)


class Reduction:
    def __init__(self, local, remote, devices, plan):
        self.devices = devices
        self.plan = list(plan)
        self.left = list(range(devices.bit_length() - 2, -1, -1))
        self.sides = [[side.reshape(devices, -1, side.shape[1])] for side in (local, remote)]
        self.prepare()

    def total(self, terms):
        total = terms[0].astype(F32)
        for term in terms[1:]:
            total = total + term.astype(F32)
        return total

    def prepare(self):
        self.stage = stage = self.plan.pop(0)
        if stage == "x":
            self.send = self.total(self.sides[1]).astype(BF16)
            self.sides = [[self.total(self.sides[0])]]
            return
        where = self.left.index(stage)
        self.left.remove(stage)
        before, behind = 2**where, 2 ** (len(self.left) - where)
        here = lax.axis_index("dp") // 2**stage % 2

        def pick(terms, index):
            parts = []
            for term in terms:
                cut = term.reshape(before, 2, behind, *term.shape[1:])
                part = lax.dynamic_index_in_dim(cut, index, 1, keepdims=False)
                parts.append(part.reshape(before * behind, *term.shape[1:]))
            return self.total(parts)

        self.send = jnp.stack([pick(terms, 1 - here).astype(BF16) for terms in self.sides])
        self.sides = [[pick(terms, here)] for terms in self.sides]

    def start(self):
        if self.stage == "x":
            self.received = swap_tensor(self.send)
        else:
            self.received = swap_dp(self.send, self.devices, 2**self.stage)

    def absorb(self):
        if self.stage == "x":
            self.sides[0].append(self.received)
        else:
            for number, terms in enumerate(self.sides):
                terms.append(self.received[number])

    def step(self):
        self.absorb()
        self.prepare()
        self.start()

    def finish(self):
        while self.plan:
            self.step()
        self.absorb()
        total = self.total(self.sides[0])
        return total.reshape(total.shape[-2:])


def body(
    hidden_in,
    pair_lengths,
    candidates,
    qkv_weight,
    qv_bias,
    out_weight,
    out_bias,
    norm1_gain,
    norm1_shift,
    up_weight,
    up_bias,
    down_weight,
    down_bias,
    norm2_gain,
    norm2_shift,
    out_cotangent,
    *,
    devices,
):
    pairs = pair_lengths.shape[0] // 2
    width = hidden_in.shape[1]
    local = qv_bias.shape[1]
    units = up_bias.shape[0]
    row_count = hidden_in.shape[0] // 2
    span = row_count // pairs
    place, tensor = lax.axis_index("dp"), lax.axis_index("tensor")
    meta = jnp.stack([place % 2, tensor]).astype(jnp.int32)
    bits = list(range(1, devices.bit_length() - 1))

    def own(array, size):
        return lax.dynamic_slice_in_dim(array, tensor * size, size, 0)

    qkv_local_weight = by_lane_pair(qkv_weight)
    (qkv_piece,) = pack(meta, [qkv_local_weight])
    qkv_mine = swap_tensor(qkv_piece)
    biases_other = swap_tensor(jnp.concatenate([qv_bias.reshape(-1), up_bias]))
    out_piece, up_piece, down_piece = pack(meta, [out_weight, up_weight, down_weight])
    rows = own(hidden_in, row_count)

    def project(weight, bias):
        bias = jnp.stack([bias[0], jnp.zeros_like(bias[0]), bias[1]]).reshape(3, 1, local)
        return (product(rows, weight, NN) + by_lane_pair(bias)).astype(BF16)

    qkv_local = project(qkv_local_weight, qv_bias)
    context_local, totals_local = attend(meta, pair_lengths, qkv_local, pairs)
    context_local, qkv_mine, out_piece = boundary(context_local, qkv_mine, out_piece)
    qkv_other = swap_dp(qkv_mine, devices, 1)
    out_mine = swap_tensor(out_piece)
    part_local = low(product(context_local, out_weight, NN))
    qkv_mine, qkv_other, part_local, up_piece = boundary(qkv_mine, qkv_other, part_local, up_piece)
    up_mine = swap_tensor(up_piece)
    qkv_remote_weight = join(meta, 0, [qkv_mine], [qkv_other], "join_qkv")
    qkv_remote = project(qkv_remote_weight, biases_other[: 2 * local].reshape(2, local))
    context_remote, totals_remote = attend(meta, pair_lengths, qkv_remote, pairs)
    context_remote, out_mine = boundary(context_remote, out_mine)
    out_other = swap_dp(out_mine, devices, 1)
    out_remote_weight = join(meta, 0, [out_mine], [out_other], "join_out")
    part_remote = low(product(context_remote, out_remote_weight, NN))
    residual = rows.astype(F32) + (part_local + part_remote) + out_bias
    xhat_one, scale_one = normalized(residual)
    normed_one = xhat_one * norm1_gain + norm1_shift
    normed = normed_one.astype(BF16)
    normed, up_mine, down_piece = boundary(normed, up_mine, down_piece)
    down_mine = swap_tensor(down_piece)
    up_other = swap_dp(up_mine, devices, 1)
    act_local, slope_local = gelu_pair(product(normed, up_weight, NN) + up_bias)
    ff_local = low(product(act_local, down_weight, NN))
    normed_again, up_mine, up_other, ff_local = boundary(normed, up_mine, up_other, ff_local)
    up_remote_weight = join(meta, 0, [up_mine], [up_other], "join_up")
    act_remote, slope_remote = gelu_pair(
        product(normed_again, up_remote_weight, NN) + biases_other[2 * local :]
    )
    act_remote, down_mine = boundary(act_remote, down_mine)
    down_other = swap_dp(down_mine, devices, 1)
    down_remote_weight = join(meta, 0, [down_mine], [down_other], "join_down")
    ff_remote = low(product(act_remote, down_remote_weight, NN))
    xhat, scale = normalized(normed_one + (ff_local + ff_remote) + down_bias)
    block_mine = (xhat * norm2_gain + norm2_shift).astype(BF16)

    counts = own(candidates, pairs).astype(F32)[:, None, None]
    grad_output = own(out_cotangent, row_count).astype(F32).reshape(pairs, span, width) / counts
    grad_output = grad_output.reshape(row_count, width)
    grad_two = norm_back(grad_output, xhat, scale, norm2_gain)
    grad_two_low = grad_two.astype(BF16)
    sums = [
        jnp.sum(grad_two, axis=0),
        jnp.sum(grad_output * xhat, axis=0),
        jnp.sum(grad_output, axis=0),
    ]
    grad_two_low, block_mine = boundary(grad_two_low, block_mine)
    block_other = swap_tensor(block_mine)

    def weight_grad(left, right):
        return product(left, right, TN).astype(BF16)

    down_sum = Reduction(
        weight_grad(grad_two_low, act_local),
        weight_grad(grad_two_low, act_remote),
        devices,
        [0] + bits + ["x"],
    )
    grad_two_low, down_sum.send = boundary(grad_two_low, down_sum.send)
    down_sum.start()
    grad_pre = []
    for weight, slope in ((down_weight, slope_local), (down_remote_weight, slope_remote)):
        grad_pre.append((product(grad_two_low, weight, NT) * slope.astype(F32)).astype(BF16))
    pre_local, pre_remote, down_sum.received = boundary(*grad_pre, down_sum.received)
    down_sum.step()
    up_bias_grads = [jnp.sum(grad, axis=0, dtype=F32) for grad in (pre_local, pre_remote)]
    grad_normed = (
        grad_two + product(pre_local, up_weight, NT) + product(pre_remote, up_remote_weight, NT)
    )
    grad_one = norm_back(grad_normed, xhat_one, scale_one, norm1_gain)
    sums += [
        jnp.sum(grad_one, axis=0),
        jnp.sum(grad_normed * xhat_one, axis=0),
        jnp.sum(grad_normed, axis=0),
    ]
    grad_one_low = grad_one.astype(BF16)
    back_local = product(grad_one_low, out_weight, NT).astype(BF16)
    back_remote = product(grad_one_low, out_remote_weight, NT).astype(BF16)
    up_sum = Reduction(
        weight_grad(normed, pre_local),
        weight_grad(normed, pre_remote),
        devices,
        [0, "x"] + bits,
    )
    back_local, up_sum.send, down_sum.received = boundary(back_local, up_sum.send, down_sum.received)
    up_sum.start()
    down_sum.step()
    grads = {}
    grads["local", 0] = attend_back(meta, pair_lengths, qkv_local, back_local, totals_local, 0, pairs)
    out_sum = Reduction(
        weight_grad(grad_one_low, context_local),
        weight_grad(grad_one_low, context_remote),
        devices,
        [0] + bits + ["x"],
    )
    back_remote, grads["local", 0], out_sum.send, up_sum.received, down_sum.received, block_other = boundary(
        back_remote, grads["local", 0], out_sum.send, up_sum.received, down_sum.received, block_other
    )
    up_sum.step()
    down_sum.step()
    block_out = join(meta, 1, [block_mine], [block_other], "join_block")
    out_sum.start()
    grads["remote", 0] = attend_back(
        meta, pair_lengths, qkv_remote, back_remote, totals_remote, 0, pairs
    )

    def input_grad(pair):
        part = product(grads["local", pair], qkv_local_weight, NT)
        part = part + product(grads["remote", pair], qkv_remote_weight, NT)
        return (grad_one[pair * span : (pair + 1) * span] + part).astype(BF16)

    grad_in = {}
    grad_in[0] = input_grad(0)
    back_local, grad_in[0], down_sum.received, out_sum.received = boundary(
        back_local, grad_in[0], down_sum.received, out_sum.received
    )
    down_sum.step()
    out_sum.step()
    other_in = {0: swap_tensor(grad_in[0])}
    for pair in range(1, pairs):
        grads["local", pair] = attend_back(
            meta, pair_lengths, qkv_local, back_local, totals_local, pair, pairs
        )
        back_remote, grads["local", pair], up_sum.received, down_sum.received, out_sum.received = boundary(
            back_remote, grads["local", pair], up_sum.received, down_sum.received, out_sum.received
        )
        if pair == 1:
            up_sum.step()
            out_sum.step()
        grads["remote", pair] = attend_back(
            meta, pair_lengths, qkv_remote, back_remote, totals_remote, pair, pairs
        )
        grad_in[pair] = input_grad(pair)
        grads["remote", pair], grad_in[pair], out_sum.received = boundary(
            grads["remote", pair], grad_in[pair], out_sum.received
        )
        other_in[pair] = swap_tensor(grad_in[pair])

    def qkv_grad(side):
        total = 0.0
        for pair in range(pairs):
            total += product(rows[pair * span : (pair + 1) * span], grads[side, pair], TN)
        return total.astype(BF16)

    qkv_sum = Reduction(
        qkv_grad("local"), qkv_grad("remote"), devices, [0] + bits[::-1] + ["x"]
    )
    qkv_sum.start()

    qv_rows = []
    for side in ("local", "remote"):
        total = sum(jnp.sum(grads[side, pair], axis=0, dtype=F32) for pair in range(pairs))
        total = total.reshape(-1, 3, LANES)
        qv_rows.append(jnp.concatenate([total[:, 0], total[:, 2]]).reshape(1, -1))
    ups = [grad.reshape(-1, width) for grad in up_bias_grads]
    small = jnp.concatenate([ups[0], qv_rows[0]] + [v.reshape(1, -1) for v in sums] + [ups[1], qv_rows[1]])
    up_rows = ups[0].shape[0]
    mine = up_rows + 1
    (small,) = boundary(small)
    got = swap_tensor(small[mine:])
    small = small[: mine + len(sums)] + jnp.concatenate([got[len(sums) :], got[: len(sums)]])
    for bit in [0] + bits:
        small = small + swap_dp(small, devices, 2**bit)

    share_down = down_sum.finish()
    share_out = out_sum.finish()
    share_up = up_sum.finish()
    share_qkv = qkv_sum.finish()
    here = lambda array: lax.dynamic_index_in_dim(array, place, 0, keepdims=False)
    vectors = here(small[mine:].reshape(len(sums), devices, -1).transpose(1, 0, 2))
    qv_share = here(small[up_rows].reshape(2, devices, -1).transpose(1, 0, 2))
    return (
        block_out,
        join(meta, 1, [grad_in[p] for p in range(pairs)], [other_in[p] for p in range(pairs)], "join_in"),
        share_qkv.reshape(-1, local // LANES, 3, LANES).transpose(2, 0, 1, 3).reshape(3, -1, local),
        qv_share,
        share_out.T,
        vectors[3],
        vectors[4],
        vectors[5],
        share_up,
        here(small[:up_rows].reshape(devices, -1)),
        share_down.T,
        vectors[0],
        vectors[1],
        vectors[2],
    )


def solution(mesh):
    devices = mesh.shape["dp"]
    in_specs = (
        P("dp", None),
        P("dp"),
        P("dp"),
        P(None, None, "tensor"),
        P(None, "tensor"),
        P("tensor", None),
        P(),
        P(),
        P(),
        P(None, "tensor"),
        P("tensor"),
        P("tensor", None),
        P(),
        P(),
        P(),
        P("dp", None),
    )
    out_specs = (
        P("dp", None),
        P("dp", None),
        P(None, "dp", "tensor"),
        P(None, ("tensor", "dp")),
        P("tensor", "dp"),
        P("dp"),
        P("dp"),
        P("dp"),
        P("dp", "tensor"),
        P(("tensor", "dp")),
        P("tensor", "dp"),
        P("dp"),
        P("dp"),
        P("dp"),
    )
    return jax.shard_map(
        functools.partial(body, devices=devices),
        mesh=mesh,
        in_specs=in_specs,
        out_specs=out_specs,
        check_vma=False,
    )
```

```python
import functools

import jax
import jax.numpy as jnp
from jax import lax
from jax.experimental import pallas as pl
from jax.experimental.pallas import tpu as pltpu
from jax.sharding import PartitionSpec as P

HEAD_DIM = 64
LANES = 128
VMEM_BYTES = 60 * 1024 * 1024
NORM_EPSILON = 1e-12
HALF_ROOT = 0.7071067811865476
INVERSE_ROOT_TWO_PI = 0.3989422804014327
SCORE_SCALE = HEAD_DIM ** (-0.5)
NT = (((1,), (1,)), ((), ()))
NN = (((1,), (0,)), ((), ()))
TN = (((0,), (0,)), ((), ()))
F32 = jnp.float32
BF16 = jnp.bfloat16


def product(left, right, dims):
    return lax.dot_general(left, right, dims, preferred_element_type=F32)


def head_halves(block):
    lane = lax.broadcasted_iota(jnp.int32, (1, LANES), 1)
    zero = jnp.zeros_like(block)
    return jnp.where(lane < HEAD_DIM, block, zero), jnp.where(lane < HEAD_DIM, zero, block)


def call(kernel, name, meta, grid, inputs, outputs, flops, moved, exps=0, scratch=()):
    return pl.pallas_call(
        kernel,
        out_shape=[jax.ShapeDtypeStruct(shape, dtype) for shape, dtype, spec in outputs],
        grid_spec=pltpu.PrefetchScalarGridSpec(
            num_scalar_prefetch=1,
            grid=grid,
            in_specs=[spec for array, spec in inputs],
            out_specs=[spec for shape, dtype, spec in outputs],
            scratch_shapes=list(scratch),
        ),
        cost_estimate=pl.CostEstimate(flops=0, bytes_accessed=1024, transcendentals=0),
        name=name,
    )(meta, *[array for array, spec in inputs])


def attend_kernel(meta_ref, length_ref, rows_ref, weight_ref, bias_ref, qkv_ref, context_ref, total_ref):
    length = length_ref[meta_ref[1] * pl.num_programs(0) + pl.program_id(0)]
    qkv = (product(rows_ref[...], weight_ref[...], NN) + bias_ref[...]).astype(BF16)
    qkv_ref[...] = qkv
    keys = qkv[:, LANES : 2 * LANES] * SCORE_SCALE
    valid = lax.broadcasted_iota(jnp.int32, (keys.shape[0], 1), 0) < length
    heads = zip(head_halves(qkv[:, :LANES]), head_halves(qkv[:, 2 * LANES :]))
    flipped = None
    for head, (query, value) in enumerate(heads):
        scores = jnp.where(valid, product(keys, query, NT), -1000000000.0)
        peak = jnp.max(scores, axis=0, keepdims=True)
        exponent = jnp.exp(scores - peak)
        total = jnp.sum(exponent, axis=0, keepdims=True)
        probs_low = (exponent * (1.0 / total)).astype(BF16)
        part = product(value, probs_low, TN)
        flipped = part if flipped is None else flipped + part
        total_ref[0, 0, head : head + 1, :] = peak + jnp.log(total)
    context_ref[...] = flipped.T.astype(BF16)


def attend(meta, lengths, rows, weight, bias, pairs):
    row_count, width = rows.shape
    columns = weight.shape[1]
    span, blocks = row_count // pairs, columns // (3 * LANES)
    work = row_count * span * blocks * LANES
    by_block = lambda pair, lanes, meta: (pair, lanes)
    return call(
        attend_kernel,
        "attend",
        meta,
        (pairs, blocks),
        [
            (lengths, pl.BlockSpec(memory_space=pltpu.SMEM)),
            (rows, pl.BlockSpec((span, width), lambda pair, lanes, meta: (pair, 0))),
            (weight, pl.BlockSpec((width, 3 * LANES), lambda pair, lanes, meta: (0, lanes))),
            (bias, pl.BlockSpec((1, 3 * LANES), lambda pair, lanes, meta: (0, lanes))),
        ],
        [
            ((row_count, columns), BF16, pl.BlockSpec((span, 3 * LANES), by_block)),
            ((row_count, blocks * LANES), BF16, pl.BlockSpec((span, LANES), by_block)),
            (
                (pairs, blocks, 2, span),
                F32,
                pl.BlockSpec((1, 1, 2, span), lambda pair, lanes, meta: (pair, lanes, 0, 0)),
            ),
        ],
        flops=16 * work,
        moved=8 * row_count * blocks * LANES,
        exps=work // HEAD_DIM,
    )


def attend_back_kernel(pair, pairs, meta_ref, length_ref, qkv_ref, grad_ref, total_ref, out_ref):
    length = length_ref[meta_ref[1] * pairs + pair]
    keys = qkv_ref[:, LANES : 2 * LANES] * SCORE_SCALE
    values = qkv_ref[:, 2 * LANES :]
    valid = lax.broadcasted_iota(jnp.int32, (keys.shape[0], 1), 0) < length
    heads = zip(head_halves(qkv_ref[:, :LANES]), head_halves(keys), head_halves(grad_ref[...]))
    sums = [None, None, None]
    for head, (query, key, grad) in enumerate(heads):
        scores = jnp.where(valid, product(keys, query, NT), -1000000000.0)
        probs = jnp.exp(scores - total_ref[0, 0, head : head + 1, :])
        grad_probs = product(values, grad, NT)
        weighted = probs * grad_probs
        inner = jnp.sum(weighted, axis=0, keepdims=True)
        grad_scores = (weighted - probs * inner).astype(BF16)
        parts = (
            product(grad_scores, key, TN),
            product(grad_scores, query, NN),
            product(probs.astype(BF16), grad, NN),
        )
        sums = [b if a is None else a + b for a, b in zip(sums, parts)]
    out_ref[:, :LANES] = sums[0].astype(BF16)
    out_ref[:, LANES : 2 * LANES] = (sums[1] * SCORE_SCALE).astype(BF16)
    out_ref[:, 2 * LANES :] = sums[2].astype(BF16)


def attend_back(meta, lengths, qkv, grad, totals, pair, pairs):
    rows, columns = qkv.shape
    span, blocks = rows // pairs, columns // (3 * LANES)
    work = span * span * blocks * LANES
    return call(
        functools.partial(attend_back_kernel, pair, pairs),
        "attend_back",
        meta,
        (blocks,),
        [
            (lengths, pl.BlockSpec(memory_space=pltpu.SMEM)),
            (qkv, pl.BlockSpec((span, 3 * LANES), lambda lanes, meta: (pair, lanes))),
            (grad, pl.BlockSpec((span, LANES), lambda lanes, meta: (pair, lanes))),
            (totals, pl.BlockSpec((1, 1, 2, span), lambda lanes, meta: (pair, lanes, 0, 0))),
        ],
        [((span, columns), BF16, pl.BlockSpec((span, 3 * LANES), lambda lanes, meta: (0, lanes)))],
        flops=28 * work,
        moved=14 * span * blocks * LANES,
        exps=work // HEAD_DIM,
    )[0]


def move_kernel(moves, source_count, target_count, meta_ref, *refs):
    sources = refs[:source_count]
    targets = refs[source_count : source_count + target_count]
    rest = refs[source_count + target_count :]
    buffers, arrived, left = rest[: len(moves)], rest[-2], rest[-1]
    incoming, outgoing = [], []
    for number, (source, row, column, target, to_row, to_column, rows, columns) in enumerate(moves):
        into = sources[source].at[pl.ds(row(meta_ref), rows), pl.ds(column, columns)]
        onto = targets[target].at[pl.ds(to_row(meta_ref), rows), pl.ds(to_column, columns)]
        incoming.append(pltpu.make_async_copy(into, buffers[number], arrived.at[number]))
        outgoing.append(pltpu.make_async_copy(buffers[number], onto, left.at[number]))
    for copy in incoming:
        copy.start()
    for copy_in, copy_out in zip(incoming, outgoing):
        copy_in.wait()
        copy_out.start()
    for copy in outgoing:
        copy.wait()


def move(name, meta, sources, targets, moves):
    return call(
        functools.partial(move_kernel, moves, len(sources), len(targets)),
        name,
        meta,
        (1,),
        [(source, pl.BlockSpec(memory_space=pl.ANY)) for source in sources],
        [(shape, BF16, pl.BlockSpec(memory_space=pl.ANY)) for shape in targets],
        flops=0,
        moved=4 * sum(entry[6] * entry[7] for entry in moves),
        scratch=[pltpu.VMEM(entry[6:], BF16) for entry in moves]
        + [pltpu.SemaphoreType.DMA((len(moves),))] * 2,
    )


def fixed(row):
    return lambda meta_ref: row


def by_place(entry, rows, other=False, offset=0):
    def start(meta_ref):
        place = 1 - meta_ref[entry] if other else meta_ref[entry]
        return pl.multiple_of(place * rows + offset, 16)

    return start


def pack_qkv_kernel(blocks, meta_ref, weight_ref, whole_ref, half_ref, buffer, arrived, left):
    copies = []
    for kind in range(3):
        for block in range(blocks):
            number = 3 * block + kind
            copies.append(
                pltpu.make_async_copy(
                    weight_ref.at[kind, :, pl.ds(block * LANES, LANES)],
                    buffer.at[:, pl.ds(number * LANES, LANES)],
                    arrived.at[number],
                )
            )
    for copy in copies:
        copy.start()
    for copy in copies:
        copy.wait()
    half = half_ref.shape[0]
    mine = pl.ds(by_place(0, half)(meta_ref), half)
    out = [
        pltpu.make_async_copy(buffer.at[mine], half_ref, left.at[0]),
        pltpu.make_async_copy(buffer, whole_ref, left.at[1]),
    ]
    for copy in out:
        copy.start()
    for copy in out:
        copy.wait()


def pack_qkv(meta, weight):
    kinds, rows, columns = weight.shape
    shapes = [(rows, kinds * columns), (rows // 2, kinds * columns)]
    return call(
        functools.partial(pack_qkv_kernel, columns // LANES),
        "pack_qkv",
        meta,
        (1,),
        [(weight, pl.BlockSpec(memory_space=pl.ANY))],
        [(shape, BF16, pl.BlockSpec(memory_space=pl.ANY)) for shape in shapes],
        flops=0,
        moved=5 * weight.size,
        scratch=[
            pltpu.VMEM(shapes[0], BF16),
            pltpu.SemaphoreType.DMA((kinds * columns // LANES,)),
            pltpu.SemaphoreType.DMA((2,)),
        ],
    )


def pack(meta, out_weight, up_weight, down_weight):
    out, up, down = [weight.shape[0] // 2 for weight in (out_weight, up_weight, down_weight)]
    width, units = out_weight.shape[1], up_weight.shape[1]
    fold = units // width
    part = out // fold
    moves = [(1, by_place(0, up), 0, 0, fixed(0), 0, up, units)]
    for i in range(fold):
        moves.append((0, by_place(0, out, offset=i * part), 0, 0, fixed(up), i * width, part, width))
    moves.append((2, by_place(0, down), 0, 1, fixed(0), 0, down, width))
    return move(
        "pack",
        meta,
        [out_weight, up_weight, down_weight],
        [(up + part, units), (down, width)],
        moves,
    )


def unpack(meta, mine, other, out_shape, up_shape):
    out, up = out_shape[0] // 2, up_shape[0] // 2
    width, units = out_shape[1], up_shape[1]
    fold = units // width
    part = out // fold
    moves = []
    for source in (0, 1):
        for i in range(fold):
            onto = by_place(0, out, other=bool(source), offset=i * part)
            moves.append((source, fixed(up), i * width, 0, onto, 0, part, width))
    for source in (0, 1):
        moves.append((source, fixed(0), 0, 1, by_place(0, up, other=bool(source)), 0, up, units))
    return move("unpack", meta, [mine, other], [out_shape, up_shape], moves)


def join(meta, entry, mine, other, name):
    rows, columns = mine[0].shape
    count = len(mine)
    moves = []
    for own in (0, 1):
        for i in range(count):
            onto = by_place(entry, rows * count, other=bool(own), offset=i * rows)
            moves.append((own * count + i, fixed(0), 0, 0, onto, 0, rows, columns))
    return move(name, meta, [*mine, *other], [(2 * count * rows, columns)], moves)[0]


def normalized(rows):
    row_mean = jnp.mean(rows, axis=-1, keepdims=True)
    centered = rows - row_mean
    variance = jnp.mean(centered * centered, axis=-1, keepdims=True)
    scale = lax.rsqrt(variance + NORM_EPSILON)
    return centered * scale, scale


def norm_back(grad, xhat, scale, gain):
    inner = grad * gain
    mean = jnp.mean(inner, axis=-1, keepdims=True)
    along = jnp.mean(inner * xhat, axis=-1, keepdims=True)
    return scale * (inner - mean - xhat * along)


def low(value):
    return value.astype(BF16).astype(F32)


def gelu_pair(value):
    cdf = 0.5 + 0.5 * lax.erf(value * HALF_ROOT)
    slope = cdf + value * (jnp.exp(-0.5 * value * value) * INVERSE_ROOT_TWO_PI)
    return (value * cdf).astype(BF16), slope.astype(BF16)


def by_lane_pair(weight):
    count, rows, columns = weight.shape
    return weight.reshape(count, rows, -1, LANES).transpose(1, 2, 0, 3).reshape(rows, -1)


def swap_tensor(block):
    return lax.ppermute(block, "tensor", [(0, 1), (1, 0)])


def swap_dp(block, devices, stride):
    return lax.ppermute(block, "dp", [(place, place ^ stride) for place in range(devices)])


def boundary(*values):
    return lax.optimization_barrier(values)


def eighths(rows):
    return jnp.sum(rows.astype(F32).reshape(-1, 8, rows.shape[1]), axis=0)


def columns_of(*sums):
    stacked = jnp.concatenate(sums) if len(sums) > 1 else sums[0]
    owner = lax.broadcasted_iota(jnp.int32, (stacked.shape[0], LANES), 0) // 8
    lane = lax.broadcasted_iota(jnp.int32, (stacked.shape[0], LANES), 1)
    return product(stacked.astype(BF16), (owner == lane).astype(BF16), TN)


class Reduction:
    def __init__(self, sides, devices, plan):
        self.devices = devices
        self.plan = list(plan)
        self.left = list(range(devices.bit_length() - 2, -1, -1))
        self.sides = len(sides)
        cut, here = self.halving(self.plan.pop(0))

        def pick(index):
            picked = []
            for parts in sides:
                beside = [
                    self.half(part.astype(BF16).reshape(1, devices, -1, part.shape[1]), cut, index)
                    for part in parts
                ]
                picked.append(jnp.concatenate(beside, axis=-1))
            return jnp.concatenate(picked) if len(picked) > 1 else picked[0]

        self.send, self.terms = pick(1 - here), [pick(here)]

    def halving(self, stage):
        self.stage = stage
        where = self.left.index(stage)
        self.left.remove(stage)
        return 2**where, lax.axis_index("dp") // 2**stage % 2

    def half(self, term, before, index):
        sides, places, rows, columns = term.shape
        cut = term.reshape(sides * before, 2, places // before // 2, rows, columns)
        kept = lax.dynamic_index_in_dim(cut, index, 1, keepdims=False)
        return kept.reshape(sides, places // 2, rows, columns)

    def total(self):
        total = self.terms[0].astype(F32)
        for term in self.terms[1:]:
            total = total + term.astype(F32)
        return total

    def start(self):
        if self.stage == "x":
            self.received = swap_tensor(self.send)
        else:
            self.received = swap_dp(self.send, self.devices, 2**self.stage)

    def absorb(self):
        self.terms.append(self.received)

    def step(self):
        self.absorb()
        total = self.total()
        stage = self.plan.pop(0)
        if stage == "x":
            self.stage = stage
            self.send, self.terms = total[-1:].astype(BF16), [total[:-1]] if self.sides > 1 else []
            self.sides = 1
        else:
            cut, here = self.halving(stage)
            self.send = self.half(total, cut, 1 - here).astype(BF16)
            self.terms = [self.half(total, cut, here)]
        self.start()

    def finish(self):
        while self.plan:
            self.step()
        self.absorb()
        total = self.total()
        return total.reshape(total.shape[-2:])


def body(
    hidden_in,
    pair_lengths,
    candidates,
    qkv_weight,
    qv_bias,
    out_weight,
    out_bias,
    norm1_gain,
    norm1_shift,
    up_weight,
    up_bias,
    down_weight,
    down_bias,
    norm2_gain,
    norm2_shift,
    out_cotangent,
    *,
    devices,
):
    pairs = pair_lengths.shape[0] // 2
    width = hidden_in.shape[1]
    local = qv_bias.shape[1]
    row_count = hidden_in.shape[0] // 2
    span = row_count // pairs
    place, tensor = lax.axis_index("dp"), lax.axis_index("tensor")
    meta = jnp.stack([place % 2, tensor]).astype(jnp.int32)
    bits = list(range(1, devices.bit_length() - 1))

    def own(array, size):
        return lax.dynamic_slice_in_dim(array, tensor * size, size, 0)

    qkv_local_weight, qkv_piece = pack_qkv(meta, qkv_weight)
    qkv_mine = swap_tensor(qkv_piece)
    biases_other = swap_tensor(jnp.concatenate([qv_bias.reshape(-1), up_bias]))
    out_up_piece, down_piece = pack(meta, out_weight, up_weight, down_weight)
    out_up_mine = swap_tensor(out_up_piece)
    rows = own(hidden_in, row_count)

    def project(weight, bias):
        bias = jnp.stack([bias[0], jnp.zeros_like(bias[0]), bias[1]]).reshape(3, 1, local)
        return attend(meta, pair_lengths, rows, weight, by_lane_pair(bias), pairs)

    qkv_local_weight, out_up_piece, down_piece = boundary(qkv_local_weight, out_up_piece, down_piece)
    qkv_local, context_local, totals_local = project(qkv_local_weight, qv_bias)
    context_local, qkv_mine, biases_other = boundary(context_local, qkv_mine, biases_other)
    qkv_other = swap_dp(qkv_mine, devices, 1)
    qkv_remote_weight = join(meta, 0, [qkv_mine], [qkv_other], "join_qkv")
    remote_bias = biases_other[: 2 * local].reshape(2, local)
    qkv_remote, context_remote, totals_remote = project(qkv_remote_weight, remote_bias)
    context_local, context_remote, out_up_mine = boundary(context_local, context_remote, out_up_mine)
    down_mine = swap_tensor(down_piece)
    out_up_other = swap_dp(out_up_mine, devices, 1)
    part_local = product(context_local, out_weight, NN).astype(BF16)
    out_up_mine, out_up_other, part_local = boundary(out_up_mine, out_up_other, part_local)
    out_remote_weight, up_remote_weight = unpack(
        meta, out_up_mine, out_up_other, out_weight.shape, up_weight.shape
    )
    part_remote = low(product(context_remote, out_remote_weight, NN))
    residual = rows.astype(F32) + (part_local.astype(F32) + part_remote) + out_bias
    xhat_one, scale_one = normalized(residual)
    normed_one = xhat_one * norm1_gain + norm1_shift
    normed = normed_one.astype(BF16)

    def expand(weight, bias):
        return boundary(*gelu_pair(product(normed, weight, NN) + bias))

    act_local, slope_local = expand(up_weight, up_bias)
    ff_local = product(act_local, down_weight, NN).astype(BF16)
    act_remote, slope_remote = expand(up_remote_weight, biases_other[2 * local :])
    act_remote, down_mine, ff_local = boundary(act_remote, down_mine, ff_local)
    down_other = swap_dp(down_mine, devices, 1)
    down_remote_weight = join(meta, 0, [down_mine], [down_other], "join_down")
    ff_remote = low(product(act_remote, down_remote_weight, NN))
    xhat, scale = normalized(normed_one + (ff_local.astype(F32) + ff_remote) + down_bias)
    block_mine = (xhat * norm2_gain + norm2_shift).astype(BF16)

    counts = own(candidates, pairs).astype(F32)[:, None, None]
    grad_output = own(out_cotangent, row_count).astype(F32).reshape(pairs, span, width) / counts
    grad_output = grad_output.reshape(row_count, width)
    grad_two = norm_back(grad_output, xhat, scale, norm2_gain)
    grad_two_low = grad_two.astype(BF16)
    sums = [eighths(grad_two), eighths(grad_output * xhat), eighths(grad_output)]
    grad_two_low, block_mine = boundary(grad_two_low, block_mine)
    block_other = swap_tensor(block_mine)

    def weight_grad(left, right):
        return product(left, right, TN).astype(BF16)

    down_sum = Reduction(
        [[weight_grad(grad_two_low, act_local)], [weight_grad(grad_two_low, act_remote)]],
        devices,
        [0] + bits + ["x"],
    )
    grad_two_low, down_sum.send = boundary(grad_two_low, down_sum.send)
    down_sum.start()
    grad_pre = []
    for weight, slope in ((down_weight, slope_local), (down_remote_weight, slope_remote)):
        grad_pre.append((product(grad_two_low, weight, NT) * slope.astype(F32)).astype(BF16))
    pre_local, pre_remote, down_sum.received = boundary(*grad_pre, down_sum.received)
    down_sum.step()
    grad_normed = (
        grad_two + product(pre_local, up_weight, NT) + product(pre_remote, up_remote_weight, NT)
    )
    grad_one = norm_back(grad_normed, xhat_one, scale_one, norm1_gain)
    grad_one_low = grad_one.astype(BF16)
    sums += [eighths(grad_one), eighths(grad_normed * xhat_one), eighths(grad_normed)]
    shared = columns_of(*sums)

    def extras(pre):
        zero = jnp.zeros((8, pre.shape[1]), F32)
        sums_up = eighths(pre)
        first = columns_of(*[zero] * len(sums), sums_up).reshape(devices, 2, -1, LANES)[:, 0]
        second = columns_of(*[zero] * len(sums), zero, sums_up).reshape(devices, 2, -1, LANES)[:, 1]
        return shared + (first + second).reshape(width, LANES)

    wide_sum = Reduction(
        [
            [weight_grad(normed, pre), weight_grad(grad_one_low, context), extras(pre)]
            for pre, context in ((pre_local, context_local), (pre_remote, context_remote))
        ],
        devices,
        [0] + bits + ["x"],
    )
    grad_one_low, wide_sum.send = boundary(grad_one_low, wide_sum.send)
    wide_sum.start()
    back_local = product(grad_one_low, out_weight, NT).astype(BF16)
    back_remote = product(grad_one_low, out_remote_weight, NT).astype(BF16)
    back_remote, back_local, wide_sum.received = boundary(back_remote, back_local, wide_sum.received)
    wide_sum.step()
    grads = {}

    def attention_back(side, pair):
        given = {"local": (qkv_local, back_local, totals_local), "remote": (qkv_remote, back_remote, totals_remote)}
        grads[side, pair] = attend_back(meta, pair_lengths, *given[side], pair, pairs)

    def qkv_grad(side):
        total, sums_qv = 0.0, 0.0
        for pair in range(pairs):
            total += product(rows[pair * span : (pair + 1) * span], grads[side, pair], TN)
            sums_qv += eighths(grads[side, pair])
        column = columns_of(sums_qv).reshape(-1, 3, LANES, LANES)
        column = [column[:, kind].reshape(devices, -1, LANES) for kind in (0, 2)]
        return [total, jnp.concatenate(column, axis=1).reshape(width, LANES)]

    for pair in range(pairs):
        attention_back("remote", pair)
    far_sum = Reduction([qkv_grad("remote")], devices, [0, "x"])
    (far_sum.send,) = boundary(far_sum.send)
    far_sum.start()
    parts = [product(grads["remote", pair], qkv_remote_weight, NT) for pair in range(pairs)]
    parts, back_local, far_sum.received, down_sum.received, block_other = boundary(
        parts, back_local, far_sum.received, down_sum.received, block_other
    )
    far_sum.step()
    down_sum.step()
    grad_in, other_in = [], []
    for pair in range(pairs):
        attention_back("local", pair)
        if pair == 1:
            grads["local", 1], far_sum.received, wide_sum.received = boundary(
                grads["local", 1], far_sum.received, wide_sum.received
            )
            wide_sum.step()
        part = parts[pair] + product(grads["local", pair], qkv_local_weight, NT)
        grad_in.append((grad_one[pair * span : (pair + 1) * span] + part).astype(BF16))
        other_in.append(swap_tensor(grad_in[-1]))
        if pair == 0:
            grad_in[0], back_local, down_sum.received = boundary(grad_in[0], back_local, down_sum.received)
            down_sum.step()
    near_sum = Reduction([qkv_grad("local")], devices, [0] + bits)
    near_sum.send, grad_in[-1] = boundary(near_sum.send, grad_in[-1])
    near_sum.start()
    block_out = join(meta, 1, [block_mine], [block_other], "join_block")
    near_sum.received, block_out = boundary(near_sum.received, block_out)
    near_sum.terms.append(far_sum.received)
    near_sum.step()
    down_sum.step()
    near_sum.received, wide_sum.received, down_sum.received = boundary(
        near_sum.received, wide_sum.received, down_sum.received
    )
    near_sum.step()
    wide_sum.step()
    share_down = down_sum.finish().T
    near_sum.received, share_down = boundary(near_sum.received, share_down)
    while near_sum.plan:
        near_sum.step()
    near_sum.send, wide_sum.received = boundary(near_sum.send, wide_sum.received)
    wide_sum.step()
    near_sum.received, other_in = boundary(near_sum.received, other_in)
    wide = wide_sum.finish()
    units = up_weight.shape[1]
    vectors = wide[:, units + local :].T
    share_qkv = near_sum.finish()
    columns = 3 * local
    share_qv = share_qkv[:, columns].reshape(2, -1)
    share_qkv = share_qkv[:, :columns].reshape(-1, local // LANES, 3, LANES)
    return (
        block_out,
        join(meta, 1, grad_in, other_in, "join_in"),
        share_qkv.transpose(2, 0, 1, 3).reshape(3, -1, local),
        share_qv,
        wide[:, units : units + local].T,
        vectors[3],
        vectors[4],
        vectors[5],
        wide[:, :units],
        vectors[6:8].reshape(-1),
        share_down,
        vectors[0],
        vectors[1],
        vectors[2],
    )


def solution(mesh):
    devices = mesh.shape["dp"]
    in_specs = (
        P("dp", None),
        P("dp"),
        P("dp"),
        P(None, None, "tensor"),
        P(None, "tensor"),
        P("tensor", None),
        P(),
        P(),
        P(),
        P(None, "tensor"),
        P("tensor"),
        P("tensor", None),
        P(),
        P(),
        P(),
        P("dp", None),
    )
    out_specs = (
        P("dp", None),
        P("dp", None),
        P(None, "dp", "tensor"),
        P(None, ("tensor", "dp")),
        P("tensor", "dp"),
        P("dp"),
        P("dp"),
        P("dp"),
        P("dp", "tensor"),
        P(("tensor", "dp")),
        P("tensor", "dp"),
        P("dp"),
        P("dp"),
        P("dp"),
    )
    return jax.shard_map(
        functools.partial(body, devices=devices),
        mesh=mesh,
        in_specs=in_specs,
        out_specs=out_specs,
        check_vma=False,
    )
```

```python
import functools

import jax
import jax.numpy as jnp
from jax import lax
from jax.experimental import pallas as pl
from jax.experimental.pallas import tpu as pltpu
from jax.sharding import PartitionSpec as P

HEAD_DIM = 64
LANES = 128
VMEM_BYTES = 60 * 1024 * 1024
NORM_EPSILON = 1e-12
HALF_ROOT = 0.7071067811865476
INVERSE_ROOT_TWO_PI = 0.3989422804014327
SCORE_SCALE = HEAD_DIM ** (-0.5)
NT = (((1,), (1,)), ((), ()))
NN = (((1,), (0,)), ((), ()))
TN = (((0,), (0,)), ((), ()))
F32 = jnp.float32
BF16 = jnp.bfloat16


def product(left, right, dims):
    return lax.dot_general(left, right, dims, preferred_element_type=F32)


def head_halves(block):
    lane = lax.broadcasted_iota(jnp.int32, (1, LANES), 1)
    zero = jnp.zeros_like(block)
    return jnp.where(lane < HEAD_DIM, block, zero), jnp.where(lane < HEAD_DIM, zero, block)


def call(kernel, name, meta, grid, inputs, outputs, flops, moved, exps=0, scratch=()):
    return pl.pallas_call(
        kernel,
        out_shape=[jax.ShapeDtypeStruct(shape, dtype) for shape, dtype, spec in outputs],
        grid_spec=pltpu.PrefetchScalarGridSpec(
            num_scalar_prefetch=1,
            grid=grid,
            in_specs=[spec for array, spec in inputs],
            out_specs=[spec for shape, dtype, spec in outputs],
            scratch_shapes=list(scratch),
        ),
        cost_estimate=pl.CostEstimate(flops=0, bytes_accessed=1024, transcendentals=0),
        name=name,
    )(meta, *[array for array, spec in inputs])


def attend_kernel(meta_ref, length_ref, rows_ref, weight_ref, bias_ref, qkv_ref, context_ref, total_ref):
    length = length_ref[meta_ref[1] * pl.num_programs(0) + pl.program_id(0)]
    qkv = (product(rows_ref[...], weight_ref[...], NN) + bias_ref[...]).astype(BF16)
    qkv_ref[...] = qkv
    keys = qkv[:, LANES : 2 * LANES] * SCORE_SCALE
    valid = lax.broadcasted_iota(jnp.int32, (keys.shape[0], 1), 0) < length
    heads = zip(head_halves(qkv[:, :LANES]), head_halves(qkv[:, 2 * LANES :]))
    flipped = None
    for head, (query, value) in enumerate(heads):
        scores = jnp.where(valid, product(keys, query, NT), -1000000000.0)
        peak = jnp.max(scores, axis=0, keepdims=True)
        exponent = jnp.exp(scores - peak)
        total = jnp.sum(exponent, axis=0, keepdims=True)
        probs_low = (exponent * (1.0 / total)).astype(BF16)
        part = product(value, probs_low, TN)
        flipped = part if flipped is None else flipped + part
        total_ref[0, 0, head : head + 1, :] = peak + jnp.log(total)
    context_ref[...] = flipped.T.astype(BF16)


def attend(meta, lengths, rows, weight, bias, pairs):
    row_count, width = rows.shape
    columns = weight.shape[1]
    span, blocks = row_count // pairs, columns // (3 * LANES)
    work = row_count * span * blocks * LANES
    by_block = lambda pair, lanes, meta: (pair, lanes)
    return call(
        attend_kernel,
        "attend",
        meta,
        (pairs, blocks),
        [
            (lengths, pl.BlockSpec(memory_space=pltpu.SMEM)),
            (rows, pl.BlockSpec((span, width), lambda pair, lanes, meta: (pair, 0))),
            (weight, pl.BlockSpec((width, 3 * LANES), lambda pair, lanes, meta: (0, lanes))),
            (bias, pl.BlockSpec((1, 3 * LANES), lambda pair, lanes, meta: (0, lanes))),
        ],
        [
            ((row_count, columns), BF16, pl.BlockSpec((span, 3 * LANES), by_block)),
            ((row_count, blocks * LANES), BF16, pl.BlockSpec((span, LANES), by_block)),
            (
                (pairs, blocks, 2, span),
                F32,
                pl.BlockSpec((1, 1, 2, span), lambda pair, lanes, meta: (pair, lanes, 0, 0)),
            ),
        ],
        flops=16 * work,
        moved=8 * row_count * blocks * LANES,
        exps=work // HEAD_DIM,
    )


def attend_back_kernel(
    meta_ref,
    length_ref,
    qkv_ref,
    low_ref,
    out_ref,
    total_ref,
    rows_ref,
    weight_ref,
    base_ref,
    rows_grad_ref,
    weight_grad_ref,
    sums_ref,
    rows_sum,
    weight_sum,
):
    step, lanes = pl.program_id(0), pl.program_id(1)
    length = length_ref[meta_ref[1] * pl.num_programs(0) + step]
    keys = qkv_ref[:, LANES : 2 * LANES] * SCORE_SCALE
    values = qkv_ref[:, 2 * LANES :]
    valid = lax.broadcasted_iota(jnp.int32, (keys.shape[0], 1), 0) < length
    context_grad = product(low_ref[...], out_ref[...], NT).astype(BF16)
    heads = zip(head_halves(qkv_ref[:, :LANES]), head_halves(keys), head_halves(context_grad))
    sums = [None, None, None]
    for head, (query, key, grad) in enumerate(heads):
        scores = jnp.where(valid, product(keys, query, NT), -1000000000.0)
        probs = jnp.exp(scores - total_ref[0, 0, head : head + 1, :])
        grad_probs = product(values, grad, NT)
        weighted = probs * grad_probs
        inner = jnp.sum(weighted, axis=0, keepdims=True)
        grad_scores = (weighted - probs * inner).astype(BF16)
        parts = (
            product(grad_scores, key, TN),
            product(grad_scores, query, NN),
            product(probs.astype(BF16), grad, NN),
        )
        sums = [b if a is None else a + b for a, b in zip(sums, parts)]
    grads = [sums[0].astype(BF16), (sums[1] * SCORE_SCALE).astype(BF16), sums[2].astype(BF16)]
    grads = jnp.concatenate(grads, axis=1)
    rows_part = product(grads, weight_ref[...], NT)
    weight_part = product(rows_ref[...], grads, TN)
    columns = pl.ds(pl.multiple_of(lanes * 3 * LANES, LANES), 3 * LANES)
    column_sums = jnp.sum(grads.astype(F32).reshape(-1, 8, 3 * LANES), axis=0)

    @pl.when(lanes == 0)
    def _():
        rows_sum[...] = base_ref[...] + rows_part

    @pl.when(lanes > 0)
    def _():
        rows_sum[...] += rows_part

    @pl.when(lanes == pl.num_programs(1) - 1)
    def _():
        rows_grad_ref[...] = rows_sum[...].astype(rows_grad_ref.dtype)

    @pl.when(step == 0)
    def _():
        weight_sum[:, columns] = weight_part
        sums_ref[:, columns] = column_sums

    @pl.when(step > 0)
    def _():
        weight_sum[:, columns] += weight_part
        sums_ref[:, columns] += column_sums

    @pl.when(step == pl.num_programs(0) - 1)
    def _():
        weight_grad_ref[:, columns] = weight_sum[:, columns].astype(weight_grad_ref.dtype)


def attend_back(meta, lengths, qkv, low_grad, out, totals, rows, weight, base, rows_type):
    pairs = totals.shape[0]
    width, columns = weight.shape
    span, blocks = rows.shape[0] // pairs, columns // (3 * LANES)
    by_pair = lambda pair, lanes, meta: (pair, 0)
    whole = lambda pair, lanes, meta: (0, 0)
    inputs = [
        (lengths, pl.BlockSpec(memory_space=pltpu.SMEM)),
        (qkv, pl.BlockSpec((span, 3 * LANES), lambda pair, lanes, meta: (pair, lanes))),
        (low_grad, pl.BlockSpec((span, width), by_pair)),
        (out, pl.BlockSpec((LANES, width), lambda pair, lanes, meta: (lanes, 0))),
        (totals, pl.BlockSpec((1, 1, 2, span), lambda pair, lanes, meta: (pair, lanes, 0, 0))),
        (rows, pl.BlockSpec((span, width), by_pair)),
        (weight, pl.BlockSpec((width, 3 * LANES), lambda pair, lanes, meta: (0, lanes))),
        (base, pl.BlockSpec((span, width), by_pair)),
    ]
    return call(
        attend_back_kernel,
        "attend_back",
        meta,
        (pairs, blocks),
        inputs,
        [
            (rows.shape, rows_type, pl.BlockSpec((span, width), by_pair)),
            ((width, columns), BF16, pl.BlockSpec((width, columns), whole)),
            ((8, columns), F32, pl.BlockSpec((8, columns), whole)),
        ],
        flops=0,
        moved=1024,
        scratch=[pltpu.VMEM((span, width), F32), pltpu.VMEM((width, columns), F32)],
    )


def move_kernel(moves, source_count, target_count, meta_ref, *refs):
    sources = refs[:source_count]
    targets = refs[source_count : source_count + target_count]
    rest = refs[source_count + target_count :]
    buffers, arrived, left = rest[: len(moves)], rest[-2], rest[-1]
    incoming, outgoing = [], []
    for number, (source, row, column, target, to_row, to_column, rows, columns) in enumerate(moves):
        into = sources[source].at[pl.ds(row(meta_ref), rows), pl.ds(column, columns)]
        onto = targets[target].at[pl.ds(to_row(meta_ref), rows), pl.ds(to_column, columns)]
        incoming.append(pltpu.make_async_copy(into, buffers[number], arrived.at[number]))
        outgoing.append(pltpu.make_async_copy(buffers[number], onto, left.at[number]))
    for copy in incoming:
        copy.start()
    for copy_in, copy_out in zip(incoming, outgoing):
        copy_in.wait()
        copy_out.start()
    for copy in outgoing:
        copy.wait()


def move(name, meta, sources, targets, moves):
    return call(
        functools.partial(move_kernel, moves, len(sources), len(targets)),
        name,
        meta,
        (1,),
        [(source, pl.BlockSpec(memory_space=pl.ANY)) for source in sources],
        [(shape, BF16, pl.BlockSpec(memory_space=pl.ANY)) for shape in targets],
        flops=0,
        moved=4 * sum(entry[6] * entry[7] for entry in moves),
        scratch=[pltpu.VMEM(entry[6:], BF16) for entry in moves]
        + [pltpu.SemaphoreType.DMA((len(moves),))] * 2,
    )


def fixed(row):
    return lambda meta_ref: row


def by_place(entry, rows, other=False, offset=0):
    def start(meta_ref):
        place = 1 - meta_ref[entry] if other else meta_ref[entry]
        return pl.multiple_of(place * rows + offset, 16)

    return start


def pack_qkv_kernel(blocks, meta_ref, weight_ref, whole_ref, quarter_ref, buffer, arrived, left):
    copies = []
    for kind in range(3):
        for block in range(blocks):
            number = 3 * block + kind
            copies.append(
                pltpu.make_async_copy(
                    weight_ref.at[kind, :, pl.ds(block * LANES, LANES)],
                    buffer.at[:, pl.ds(number * LANES, LANES)],
                    arrived.at[number],
                )
            )
    for copy in copies:
        copy.start()
    for copy in copies:
        copy.wait()
    quarter = quarter_ref.shape[0]
    mine = pl.ds(pl.multiple_of((2 * meta_ref[0] + meta_ref[2]) * quarter, 16), quarter)
    out = [
        pltpu.make_async_copy(buffer.at[mine], quarter_ref, left.at[0]),
        pltpu.make_async_copy(buffer, whole_ref, left.at[1]),
    ]
    for copy in out:
        copy.start()
    for copy in out:
        copy.wait()


def pack_qkv(meta, weight):
    kinds, rows, columns = weight.shape
    shapes = [(rows, kinds * columns), (rows // 4, kinds * columns)]
    return call(
        functools.partial(pack_qkv_kernel, columns // LANES),
        "pack_qkv",
        meta,
        (1,),
        [(weight, pl.BlockSpec(memory_space=pl.ANY))],
        [(shape, BF16, pl.BlockSpec(memory_space=pl.ANY)) for shape in shapes],
        flops=0,
        moved=5 * weight.size,
        scratch=[
            pltpu.VMEM(shapes[0], BF16),
            pltpu.SemaphoreType.DMA((kinds * columns // LANES,)),
            pltpu.SemaphoreType.DMA((2,)),
        ],
    )


def pack(meta, out_weight, up_weight, down_weight):
    out, up, down = [weight.shape[0] // 2 for weight in (out_weight, up_weight, down_weight)]
    width, units = out_weight.shape[1], up_weight.shape[1]
    fold = units // width
    part = out // fold
    moves = [(1, by_place(0, up), 0, 0, fixed(0), 0, up, units)]
    for i in range(fold):
        moves.append((0, by_place(0, out, offset=i * part), 0, 0, fixed(up), i * width, part, width))
    moves.append((2, by_place(0, down), 0, 1, fixed(0), 0, down, width))
    return move(
        "pack",
        meta,
        [out_weight, up_weight, down_weight],
        [(up + part, units), (down, width)],
        moves,
    )


def unpack(meta, mine, other, out_shape, up_shape):
    out, up = out_shape[0] // 2, up_shape[0] // 2
    width, units = out_shape[1], up_shape[1]
    fold = units // width
    part = out // fold
    moves = []
    for source in (0, 1):
        for i in range(fold):
            onto = by_place(0, out, other=bool(source), offset=i * part)
            moves.append((source, fixed(up), i * width, 0, onto, 0, part, width))
    for source in (0, 1):
        moves.append((source, fixed(0), 0, 1, by_place(0, up, other=bool(source)), 0, up, units))
    return move("unpack", meta, [mine, other], [out_shape, up_shape], moves)


def join(meta, entry, mine, other, name):
    rows, columns = mine[0].shape
    count = len(mine)
    moves = []
    for own in (0, 1):
        for i in range(count):
            onto = by_place(entry, rows * count, other=bool(own), offset=i * rows)
            moves.append((own * count + i, fixed(0), 0, 0, onto, 0, rows, columns))
    return move(name, meta, [*mine, *other], [(2 * count * rows, columns)], moves)[0]


def join_quarters(meta, mine, other):
    half, columns = mine.shape
    quarter = half // 2
    moves = []
    for source in (0, 1):
        for part in (0, 1):

            def onto(meta_ref, source=source, part=part):
                core = 1 - meta_ref[0] if source else meta_ref[0]
                chip = 1 - meta_ref[2] if part else meta_ref[2]
                return pl.multiple_of((2 * core + chip) * quarter, 16)

            moves.append((source, fixed(part * quarter), 0, 0, onto, 0, quarter, columns))
    return move("join_qkv", meta, [mine, other], [(2 * half, columns)], moves)[0]


def normalized(rows):
    row_mean = jnp.mean(rows, axis=-1, keepdims=True)
    centered = rows - row_mean
    variance = jnp.mean(centered * centered, axis=-1, keepdims=True)
    scale = lax.rsqrt(variance + NORM_EPSILON)
    return centered * scale, scale


def norm_back(grad, xhat, scale, gain):
    inner = grad * gain
    mean = jnp.mean(inner, axis=-1, keepdims=True)
    along = jnp.mean(inner * xhat, axis=-1, keepdims=True)
    return scale * (inner - mean - xhat * along)


def low(value):
    return value.astype(BF16).astype(F32)


def gelu_pair(value):
    cdf = 0.5 + 0.5 * lax.erf(value * HALF_ROOT)
    slope = cdf + value * (jnp.exp(-0.5 * value * value) * INVERSE_ROOT_TWO_PI)
    return (value * cdf).astype(BF16), slope.astype(BF16)


def by_lane_pair(weight):
    count, rows, columns = weight.shape
    return weight.reshape(count, rows, -1, LANES).transpose(1, 2, 0, 3).reshape(rows, -1)


def swap_tensor(block):
    return lax.ppermute(block, "tensor", [(0, 1), (1, 0)])


def swap_dp(block, devices, stride):
    return lax.ppermute(block, "dp", [(place, place ^ stride) for place in range(devices)])


def boundary(*values):
    return lax.optimization_barrier(values)


def eighths(rows):
    return jnp.sum(rows.astype(F32).reshape(-1, 8, rows.shape[1]), axis=0)


def columns_of(*sums):
    stacked = jnp.concatenate(sums) if len(sums) > 1 else sums[0]
    owner = lax.broadcasted_iota(jnp.int32, (stacked.shape[0], LANES), 0) // 8
    lane = lax.broadcasted_iota(jnp.int32, (stacked.shape[0], LANES), 1)
    return product(stacked.astype(BF16), (owner == lane).astype(BF16), TN)


def halve_kernel(sides, meta_ref, *refs):
    send_ref, keep_ref = refs[-2:]
    core = meta_ref[0]
    number = 0
    for side, parts in enumerate(sides):
        column = 0
        for width in parts:
            first, second = refs[number][:, 0], refs[number][:, 1]
            columns = slice(column, column + width)
            send_ref[side, :, :, columns] = jnp.where(core == 0, second, first)
            keep_ref[side, :, :, columns] = jnp.where(core == 0, first, second)
            number, column = number + 1, column + width


def halve(meta, sides, devices):
    parts = [part.astype(BF16) for side in sides for part in side]
    rows = parts[0].shape[0] // devices
    widths = [[part.shape[1] for part in side] for side in sides]
    shape = (len(sides), devices // 2, rows, sum(widths[0]))
    step = devices // 4
    out_spec = pl.BlockSpec((len(sides), step) + shape[2:], lambda place, meta: (0, place, 0, 0))
    return call(
        functools.partial(halve_kernel, widths),
        "halve",
        meta,
        (2,),
        [
            (
                part.reshape(devices // 2, 2, rows, part.shape[1]),
                pl.BlockSpec((step, 2, rows, part.shape[1]), lambda place, meta: (place, 0, 0, 0)),
            )
            for part in parts
        ],
        [(shape, BF16, out_spec)] * 2,
        flops=0,
        moved=1024,
    )


class Reduction:
    def __init__(self, sides, devices, plan, meta=None):
        self.devices = devices
        self.plan = list(plan)
        self.left = list(range(devices.bit_length() - 2, -1, -1))
        self.sides = len(sides)
        if meta is not None:
            self.stage = self.plan.pop(0)
            self.left.remove(self.stage)
            self.send, kept = halve(meta, sides, devices)
            self.terms = [kept]
            return
        cut, here = self.halving(self.plan.pop(0))

        def pick(index):
            picked = []
            for parts in sides:
                beside = [
                    self.half(part.astype(BF16).reshape(1, devices, -1, part.shape[1]), cut, index)
                    for part in parts
                ]
                picked.append(jnp.concatenate(beside, axis=-1))
            return jnp.concatenate(picked) if len(picked) > 1 else picked[0]

        self.send, self.terms = pick(1 - here), [pick(here)]

    def halving(self, stage):
        self.stage = stage
        where = self.left.index(stage)
        self.left.remove(stage)
        return 2**where, lax.axis_index("dp") // 2**stage % 2

    def half(self, term, before, index):
        sides, places, rows, columns = term.shape
        cut = term.reshape(sides * before, 2, places // before // 2, rows, columns)
        kept = lax.dynamic_index_in_dim(cut, index, 1, keepdims=False)
        return kept.reshape(sides, places // 2, rows, columns)

    def total(self):
        total = self.terms[0].astype(F32)
        for term in self.terms[1:]:
            total = total + term.astype(F32)
        return total

    def start(self):
        if self.stage == "x":
            self.received = swap_tensor(self.send)
        else:
            self.received = swap_dp(self.send, self.devices, 2**self.stage)

    def absorb(self):
        self.terms.append(self.received)

    def step(self):
        self.advance()
        self.start()

    def advance(self):
        self.absorb()
        total = self.total()
        stage = self.plan.pop(0)
        if stage == "x":
            self.stage = stage
            self.send, self.terms = total[-1:].astype(BF16), [total[:-1]] if self.sides > 1 else []
            self.sides = 1
        else:
            cut, here = self.halving(stage)
            self.send = self.half(total, cut, 1 - here).astype(BF16)
            self.terms = [self.half(total, cut, here)]

    def finish(self):
        while self.plan:
            self.step()
        self.absorb()
        total = self.total()
        return total.reshape(total.shape[-2:])


def body(
    hidden_in,
    pair_lengths,
    candidates,
    qkv_weight,
    qv_bias,
    out_weight,
    out_bias,
    norm1_gain,
    norm1_shift,
    up_weight,
    up_bias,
    down_weight,
    down_bias,
    norm2_gain,
    norm2_shift,
    out_cotangent,
    *,
    devices,
):
    pairs = pair_lengths.shape[0] // 2
    width = hidden_in.shape[1]
    local = qv_bias.shape[1]
    row_count = hidden_in.shape[0] // 2
    span = row_count // pairs
    place, tensor = lax.axis_index("dp"), lax.axis_index("tensor")
    meta = jnp.stack([place % 2, tensor, place // 2 % 2]).astype(jnp.int32)
    bits = list(range(1, devices.bit_length() - 1))

    def own(array, size):
        return lax.dynamic_slice_in_dim(array, tensor * size, size, 0)

    qkv_local_weight, qkv_piece = pack_qkv(meta, qkv_weight)
    qkv_mine = swap_tensor(qkv_piece)
    biases_other = swap_tensor(jnp.concatenate([qv_bias.reshape(-1), up_bias]))
    out_up_piece, down_piece = pack(meta, out_weight, up_weight, down_weight)
    out_up_mine = swap_tensor(out_up_piece)
    rows = own(hidden_in, row_count)

    def project(weight, bias):
        bias = jnp.stack([bias[0], jnp.zeros_like(bias[0]), bias[1]]).reshape(3, 1, local)
        return attend(meta, pair_lengths, rows, weight, by_lane_pair(bias), pairs)

    qkv_local_weight, out_up_piece, down_piece, qkv_mine = boundary(
        qkv_local_weight, out_up_piece, down_piece, qkv_mine
    )
    qkv_next = swap_dp(qkv_mine, devices, 2)
    qkv_local, context_local, totals_local = project(qkv_local_weight, qv_bias)
    context_local, qkv_next, biases_other = boundary(context_local, qkv_next, biases_other)
    qkv_half = jnp.concatenate([qkv_mine, qkv_next])
    qkv_remote_weight = join_quarters(meta, qkv_half, swap_dp(qkv_half, devices, 1))
    remote_bias = biases_other[: 2 * local].reshape(2, local)
    qkv_remote, context_remote, totals_remote = project(qkv_remote_weight, remote_bias)
    context_local, context_remote, out_up_mine = boundary(context_local, context_remote, out_up_mine)
    down_mine = swap_tensor(down_piece)
    out_up_other = swap_dp(out_up_mine, devices, 1)
    part_local = product(context_local, out_weight, NN).astype(BF16)
    out_up_mine, out_up_other, part_local = boundary(out_up_mine, out_up_other, part_local)
    out_remote_weight, up_remote_weight = unpack(
        meta, out_up_mine, out_up_other, out_weight.shape, up_weight.shape
    )
    part_remote = low(product(context_remote, out_remote_weight, NN))
    residual = rows.astype(F32) + (part_local.astype(F32) + part_remote) + out_bias
    xhat_one, scale_one = normalized(residual)
    normed_one = xhat_one * norm1_gain + norm1_shift
    normed = normed_one.astype(BF16)

    def expand(weight, bias):
        return boundary(*gelu_pair(product(normed, weight, NN) + bias))

    act_local, slope_local = expand(up_weight, up_bias)
    ff_local = product(act_local, down_weight, NN).astype(BF16)
    act_remote, slope_remote = expand(up_remote_weight, biases_other[2 * local :])
    act_remote, down_mine, ff_local = boundary(act_remote, down_mine, ff_local)
    down_other = swap_dp(down_mine, devices, 1)
    down_remote_weight = join(meta, 0, [down_mine], [down_other], "join_down")
    ff_remote = low(product(act_remote, down_remote_weight, NN))
    xhat, scale = normalized(normed_one + (ff_local.astype(F32) + ff_remote) + down_bias)
    block_mine = (xhat * norm2_gain + norm2_shift).astype(BF16)

    counts = own(candidates, pairs).astype(F32)[:, None, None]
    grad_output = own(out_cotangent, row_count).astype(F32).reshape(pairs, span, width) / counts
    grad_output = grad_output.reshape(row_count, width)
    grad_two = norm_back(grad_output, xhat, scale, norm2_gain)
    grad_two_low = grad_two.astype(BF16)
    sums = [eighths(grad_two), eighths(grad_output * xhat), eighths(grad_output)]
    grad_two_low, block_mine = boundary(grad_two_low, block_mine)
    block_other = swap_tensor(block_mine)

    def weight_grad(left, right):
        return product(left, right, TN).astype(BF16)

    down_sum = Reduction(
        [[weight_grad(grad_two_low, act_local)], [weight_grad(grad_two_low, act_remote)]],
        devices,
        [0] + bits + ["x"],
    )
    grad_two_low, down_sum.send = boundary(grad_two_low, down_sum.send)
    down_sum.start()
    grad_pre = []
    for weight, slope in ((down_weight, slope_local), (down_remote_weight, slope_remote)):
        grad_pre.append((product(grad_two_low, weight, NT) * slope.astype(F32)).astype(BF16))
    pre_local, pre_remote, down_sum.received = boundary(*grad_pre, down_sum.received)
    down_sum.step()
    grad_normed = (
        grad_two + product(pre_local, up_weight, NT) + product(pre_remote, up_remote_weight, NT)
    )
    grad_one = norm_back(grad_normed, xhat_one, scale_one, norm1_gain)
    grad_one_low = grad_one.astype(BF16)
    sums += [eighths(grad_one), eighths(grad_normed * xhat_one), eighths(grad_normed)]
    shared = columns_of(*sums)

    def extras(pre):
        zero = jnp.zeros((8, pre.shape[1]), F32)
        sums_up = eighths(pre)
        first = columns_of(*[zero] * len(sums), sums_up).reshape(devices, 2, -1, LANES)[:, 0]
        second = columns_of(*[zero] * len(sums), zero, sums_up).reshape(devices, 2, -1, LANES)[:, 1]
        return shared + (first + second).reshape(width, LANES)

    wide_sum = Reduction(
        [
            [weight_grad(normed, pre), weight_grad(grad_one_low, context), extras(pre)]
            for pre, context in ((pre_local, context_local), (pre_remote, context_remote))
        ],
        devices,
        [0] + bits[1:2] + bits[:1] + bits[2:] + ["x"],
    )
    grad_one_low, wide_sum.send = boundary(grad_one_low, wide_sum.send)
    wide_sum.start()
    grad_one_low, wide_sum.received = boundary(grad_one_low, wide_sum.received)
    wide_sum.advance()
    grad_one_low, wide_sum.send, wide_sum.terms, down_sum.terms = boundary(
        grad_one_low, wide_sum.send, wide_sum.terms, down_sum.terms
    )
    wide_sum.start()

    def attention_back(side, base, rows_type):
        qkv, out, totals, weight = {
            "local": (qkv_local, out_weight, totals_local, qkv_local_weight),
            "remote": (qkv_remote, out_remote_weight, totals_remote, qkv_remote_weight),
        }[side]
        return attend_back(
            meta, pair_lengths, qkv, grad_one_low, out, totals, rows, weight, base, rows_type
        )

    def qv_columns(sums_qv):
        column = columns_of(sums_qv).reshape(-1, 3, LANES, LANES)
        column = [column[:, kind].reshape(devices, -1, LANES) for kind in (0, 2)]
        return jnp.concatenate(column, axis=1).reshape(width, LANES)

    rows_part, far_grad, far_sums = attention_back("remote", grad_one, F32)
    far_sum = Reduction([[far_grad, qv_columns(far_sums)]], devices, [0, "x"], meta)
    (far_sum.send,) = boundary(far_sum.send)
    far_sum.start()
    rows_part, far_sum.received, down_sum.received, wide_sum.received, block_other = boundary(
        rows_part, far_sum.received, down_sum.received, wide_sum.received, block_other
    )
    far_sum.step()
    down_sum.step()
    wide_sum.step()
    rows_part, far_sum.send, down_sum.send, wide_sum.send, down_sum.terms, wide_sum.terms = boundary(
        rows_part, far_sum.send, down_sum.send, wide_sum.send, down_sum.terms, wide_sum.terms
    )
    grad_in, near_grad, near_sums = attention_back("local", rows_part, BF16)
    near_grad, down_sum.received, wide_sum.received = boundary(
        near_grad, down_sum.received, wide_sum.received
    )
    down_sum.step()
    wide_sum.step()
    other_in = swap_tensor(grad_in)
    near_sum = Reduction([[near_grad, qv_columns(near_sums)]], devices, [0] + bits, meta)
    near_sum.send, block_mine = boundary(near_sum.send, block_mine)
    near_sum.start()
    block_out = join(meta, 1, [block_mine], [block_other], "join_block")
    near_sum.received, far_sum.received, block_out = boundary(near_sum.received, far_sum.received, block_out)
    near_sum.terms.append(far_sum.received)
    near_sum.step()
    near_sum.received, down_sum.received = boundary(near_sum.received, down_sum.received)
    near_sum.step()
    down_sum.step()
    near_sum.received, wide_sum.received = boundary(near_sum.received, wide_sum.received)
    while near_sum.plan:
        near_sum.step()
    wide_sum.step()
    near_sum.send, grad_in, down_sum.received = boundary(near_sum.send, grad_in, down_sum.received)
    share_down = down_sum.finish().T
    wide = wide_sum.finish()
    units = up_weight.shape[1]
    vectors = wide[:, units + local :].T
    share_qkv = near_sum.finish()
    columns = 3 * local
    share_qv = share_qkv[:, columns].reshape(2, -1)
    share_qkv = share_qkv[:, :columns].reshape(-1, local // LANES, 3, LANES)
    return (
        block_out,
        join(meta, 1, [grad_in], [other_in], "join_in"),
        share_qkv.transpose(2, 0, 1, 3).reshape(3, -1, local),
        share_qv,
        wide[:, units : units + local].T,
        vectors[3],
        vectors[4],
        vectors[5],
        wide[:, :units],
        vectors[6:8].reshape(-1),
        share_down,
        vectors[0],
        vectors[1],
        vectors[2],
    )


def solution(mesh):
    devices = mesh.shape["dp"]
    in_specs = (
        P("dp", None),
        P("dp"),
        P("dp"),
        P(None, None, "tensor"),
        P(None, "tensor"),
        P("tensor", None),
        P(),
        P(),
        P(),
        P(None, "tensor"),
        P("tensor"),
        P("tensor", None),
        P(),
        P(),
        P(),
        P("dp", None),
    )
    out_specs = (
        P("dp", None),
        P("dp", None),
        P(None, "dp", "tensor"),
        P(None, ("tensor", "dp")),
        P("tensor", "dp"),
        P("dp"),
        P("dp"),
        P("dp"),
        P("dp", "tensor"),
        P(("tensor", "dp")),
        P("tensor", "dp"),
        P("dp"),
        P("dp"),
        P("dp"),
    )
    return jax.shard_map(
        functools.partial(body, devices=devices),
        mesh=mesh,
        in_specs=in_specs,
        out_specs=out_specs,
        check_vma=False,
    )
```

```python
import functools

import jax
import jax.numpy as jnp
from jax import lax
from jax.experimental import pallas as pl
from jax.experimental.pallas import tpu as pltpu
from jax.sharding import PartitionSpec as P

HEAD_DIM = 64
LANES = 128
VMEM_BYTES = 60 * 1024 * 1024
NORM_EPSILON = 1e-12
HALF_ROOT = 0.7071067811865476
INVERSE_ROOT_TWO_PI = 0.3989422804014327
SCORE_SCALE = HEAD_DIM ** (-0.5)
NT = (((1,), (1,)), ((), ()))
NN = (((1,), (0,)), ((), ()))
TN = (((0,), (0,)), ((), ()))
F32 = jnp.float32
BF16 = jnp.bfloat16


def product(left, right, dims):
    return lax.dot_general(left, right, dims, preferred_element_type=F32)


def head_halves(block):
    lane = lax.broadcasted_iota(jnp.int32, (1, LANES), 1)
    zero = jnp.zeros_like(block)
    return jnp.where(lane < HEAD_DIM, block, zero), jnp.where(lane < HEAD_DIM, zero, block)


def call(kernel, name, meta, grid, inputs, outputs, flops, moved, exps=0, scratch=()):
    return pl.pallas_call(
        kernel,
        out_shape=[jax.ShapeDtypeStruct(shape, dtype) for shape, dtype, spec in outputs],
        grid_spec=pltpu.PrefetchScalarGridSpec(
            num_scalar_prefetch=1,
            grid=grid,
            in_specs=[spec for array, spec in inputs],
            out_specs=[spec for shape, dtype, spec in outputs],
            scratch_shapes=list(scratch),
        ),
        cost_estimate=pl.CostEstimate(flops=0, bytes_accessed=1024, transcendentals=0),
        name=name,
    )(meta, *[array for array, spec in inputs])


def attend_kernel(meta_ref, length_ref, rows_ref, weight_ref, bias_ref, qkv_ref, context_ref, total_ref):
    length = length_ref[meta_ref[1] * pl.num_programs(0) + pl.program_id(0)]
    qkv = (product(rows_ref[...], weight_ref[...], NN) + bias_ref[...]).astype(BF16)
    qkv_ref[...] = qkv
    keys = qkv[:, LANES : 2 * LANES] * SCORE_SCALE
    valid = lax.broadcasted_iota(jnp.int32, (keys.shape[0], 1), 0) < length
    heads = zip(head_halves(qkv[:, :LANES]), head_halves(qkv[:, 2 * LANES :]))
    flipped = None
    for head, (query, value) in enumerate(heads):
        scores = jnp.where(valid, product(keys, query, NT), -1000000000.0)
        peak = jnp.max(scores, axis=0, keepdims=True)
        exponent = jnp.exp(scores - peak)
        total = jnp.sum(exponent, axis=0, keepdims=True)
        probs_low = (exponent * (1.0 / total)).astype(BF16)
        part = product(value, probs_low, TN)
        flipped = part if flipped is None else flipped + part
        total_ref[0, 0, head : head + 1, :] = peak + jnp.log(total)
    context_ref[...] = flipped.T.astype(BF16)


def attend(meta, lengths, rows, weight, bias, pairs):
    row_count, width = rows.shape
    columns = weight.shape[1]
    span, blocks = row_count // pairs, columns // (3 * LANES)
    work = row_count * span * blocks * LANES
    by_block = lambda pair, lanes, meta: (pair, lanes)
    return call(
        attend_kernel,
        "attend",
        meta,
        (pairs, blocks),
        [
            (lengths, pl.BlockSpec(memory_space=pltpu.SMEM)),
            (rows, pl.BlockSpec((span, width), lambda pair, lanes, meta: (pair, 0))),
            (weight, pl.BlockSpec((width, 3 * LANES), lambda pair, lanes, meta: (0, lanes))),
            (bias, pl.BlockSpec((1, 3 * LANES), lambda pair, lanes, meta: (0, lanes))),
        ],
        [
            ((row_count, columns), BF16, pl.BlockSpec((span, 3 * LANES), by_block)),
            ((row_count, blocks * LANES), BF16, pl.BlockSpec((span, LANES), by_block)),
            (
                (pairs, blocks, 2, span),
                F32,
                pl.BlockSpec((1, 1, 2, span), lambda pair, lanes, meta: (pair, lanes, 0, 0)),
            ),
        ],
        flops=16 * work,
        moved=8 * row_count * blocks * LANES,
        exps=work // HEAD_DIM,
    )


def attend_back_kernel(
    meta_ref,
    length_ref,
    qkv_ref,
    low_ref,
    out_ref,
    total_ref,
    rows_ref,
    weight_ref,
    base_ref,
    rows_grad_ref,
    weight_grad_ref,
    sums_ref,
    rows_sum,
    weight_sum,
):
    step, lanes = pl.program_id(0), pl.program_id(1)
    length = length_ref[meta_ref[1] * pl.num_programs(0) + step]
    keys = qkv_ref[:, LANES : 2 * LANES] * SCORE_SCALE
    values = qkv_ref[:, 2 * LANES :]
    valid = lax.broadcasted_iota(jnp.int32, (keys.shape[0], 1), 0) < length
    context_grad = product(low_ref[...], out_ref[...], NT).astype(BF16)
    heads = zip(head_halves(qkv_ref[:, :LANES]), head_halves(keys), head_halves(context_grad))
    sums = [None, None, None]
    for head, (query, key, grad) in enumerate(heads):
        scores = jnp.where(valid, product(keys, query, NT), -1000000000.0)
        probs = jnp.exp(scores - total_ref[0, 0, head : head + 1, :])
        grad_probs = product(values, grad, NT)
        weighted = probs * grad_probs
        inner = jnp.sum(weighted, axis=0, keepdims=True)
        grad_scores = (weighted - probs * inner).astype(BF16)
        parts = (
            product(grad_scores, key, TN),
            product(grad_scores, query, NN),
            product(probs.astype(BF16), grad, NN),
        )
        sums = [b if a is None else a + b for a, b in zip(sums, parts)]
    grads = [sums[0].astype(BF16), (sums[1] * SCORE_SCALE).astype(BF16), sums[2].astype(BF16)]
    grads = jnp.concatenate(grads, axis=1)
    rows_part = product(grads, weight_ref[...], NT)
    weight_part = product(rows_ref[...], grads, TN)
    columns = pl.ds(pl.multiple_of(lanes * 3 * LANES, LANES), 3 * LANES)
    column_sums = jnp.sum(grads.astype(F32).reshape(-1, 8, 3 * LANES), axis=0)

    @pl.when(lanes == 0)
    def _():
        rows_sum[...] = base_ref[...] + rows_part

    @pl.when(lanes > 0)
    def _():
        rows_sum[...] += rows_part

    @pl.when(lanes == pl.num_programs(1) - 1)
    def _():
        rows_grad_ref[...] = rows_sum[...].astype(rows_grad_ref.dtype)

    @pl.when(step == 0)
    def _():
        weight_sum[:, columns] = weight_part
        sums_ref[:, columns] = column_sums

    @pl.when(step > 0)
    def _():
        weight_sum[:, columns] += weight_part
        sums_ref[:, columns] += column_sums

    @pl.when(step == pl.num_programs(0) - 1)
    def _():
        weight_grad_ref[:, columns] = weight_sum[:, columns].astype(weight_grad_ref.dtype)


def attend_back(meta, lengths, qkv, low_grad, out, totals, rows, weight, base, rows_type):
    pairs = totals.shape[0]
    width, columns = weight.shape
    span, blocks = rows.shape[0] // pairs, columns // (3 * LANES)
    by_pair = lambda pair, lanes, meta: (pair, 0)
    whole = lambda pair, lanes, meta: (0, 0)
    inputs = [
        (lengths, pl.BlockSpec(memory_space=pltpu.SMEM)),
        (qkv, pl.BlockSpec((span, 3 * LANES), lambda pair, lanes, meta: (pair, lanes))),
        (low_grad, pl.BlockSpec((span, width), by_pair)),
        (out, pl.BlockSpec((LANES, width), lambda pair, lanes, meta: (lanes, 0))),
        (totals, pl.BlockSpec((1, 1, 2, span), lambda pair, lanes, meta: (pair, lanes, 0, 0))),
        (rows, pl.BlockSpec((span, width), by_pair)),
        (weight, pl.BlockSpec((width, 3 * LANES), lambda pair, lanes, meta: (0, lanes))),
        (base, pl.BlockSpec((span, width), by_pair)),
    ]
    return call(
        attend_back_kernel,
        "attend_back",
        meta,
        (pairs, blocks),
        inputs,
        [
            (rows.shape, rows_type, pl.BlockSpec((span, width), by_pair)),
            ((width, columns), BF16, pl.BlockSpec((width, columns), whole)),
            ((8, columns), F32, pl.BlockSpec((8, columns), whole)),
        ],
        flops=0,
        moved=1024,
        scratch=[pltpu.VMEM((span, width), F32), pltpu.VMEM((width, columns), F32)],
    )


def move_kernel(moves, source_count, target_count, meta_ref, *refs):
    sources = refs[:source_count]
    targets = refs[source_count : source_count + target_count]
    rest = refs[source_count + target_count :]
    buffers, arrived, left = rest[: len(moves)], rest[-2], rest[-1]
    incoming, outgoing = [], []
    for number, (source, row, column, target, to_row, to_column, rows, columns) in enumerate(moves):
        into = sources[source].at[pl.ds(row(meta_ref), rows), pl.ds(column, columns)]
        onto = targets[target].at[pl.ds(to_row(meta_ref), rows), pl.ds(to_column, columns)]
        incoming.append(pltpu.make_async_copy(into, buffers[number], arrived.at[number]))
        outgoing.append(pltpu.make_async_copy(buffers[number], onto, left.at[number]))
    for copy in incoming:
        copy.start()
    for copy_in, copy_out in zip(incoming, outgoing):
        copy_in.wait()
        copy_out.start()
    for copy in outgoing:
        copy.wait()


def move(name, meta, sources, targets, moves):
    return call(
        functools.partial(move_kernel, moves, len(sources), len(targets)),
        name,
        meta,
        (1,),
        [(source, pl.BlockSpec(memory_space=pl.ANY)) for source in sources],
        [(shape, BF16, pl.BlockSpec(memory_space=pl.ANY)) for shape in targets],
        flops=0,
        moved=4 * sum(entry[6] * entry[7] for entry in moves),
        scratch=[pltpu.VMEM(entry[6:], BF16) for entry in moves]
        + [pltpu.SemaphoreType.DMA((len(moves),))] * 2,
    )


def fixed(row):
    return lambda meta_ref: row


def by_place(entry, rows, other=False, offset=0):
    def start(meta_ref):
        place = 1 - meta_ref[entry] if other else meta_ref[entry]
        return pl.multiple_of(place * rows + offset, 16)

    return start


def pack_qkv_kernel(blocks, meta_ref, weight_ref, whole_ref, quarter_ref, buffer, arrived, left):
    copies = []
    for kind in range(3):
        for block in range(blocks):
            number = 3 * block + kind
            copies.append(
                pltpu.make_async_copy(
                    weight_ref.at[kind, :, pl.ds(block * LANES, LANES)],
                    buffer.at[:, pl.ds(number * LANES, LANES)],
                    arrived.at[number],
                )
            )
    for copy in copies:
        copy.start()
    for copy in copies:
        copy.wait()
    quarter = quarter_ref.shape[0]
    mine = pl.ds(pl.multiple_of((2 * meta_ref[0] + meta_ref[2]) * quarter, 16), quarter)
    out = [
        pltpu.make_async_copy(buffer.at[mine], quarter_ref, left.at[0]),
        pltpu.make_async_copy(buffer, whole_ref, left.at[1]),
    ]
    for copy in out:
        copy.start()
    for copy in out:
        copy.wait()


def pack_qkv(meta, weight):
    kinds, rows, columns = weight.shape
    shapes = [(rows, kinds * columns), (rows // 4, kinds * columns)]
    return call(
        functools.partial(pack_qkv_kernel, columns // LANES),
        "pack_qkv",
        meta,
        (1,),
        [(weight, pl.BlockSpec(memory_space=pl.ANY))],
        [(shape, BF16, pl.BlockSpec(memory_space=pl.ANY)) for shape in shapes],
        flops=0,
        moved=5 * weight.size,
        scratch=[
            pltpu.VMEM(shapes[0], BF16),
            pltpu.SemaphoreType.DMA((kinds * columns // LANES,)),
            pltpu.SemaphoreType.DMA((2,)),
        ],
    )


def pack(meta, out_weight, up_weight, down_weight):
    out, up, down = [weight.shape[0] // 2 for weight in (out_weight, up_weight, down_weight)]
    width, units = out_weight.shape[1], up_weight.shape[1]
    fold = units // width
    part = out // fold
    moves = [(1, by_place(0, up), 0, 0, fixed(0), 0, up, units)]
    for i in range(fold):
        moves.append((0, by_place(0, out, offset=i * part), 0, 0, fixed(up), i * width, part, width))
    moves.append((2, by_place(0, down), 0, 1, fixed(0), 0, down, width))
    return move(
        "pack",
        meta,
        [out_weight, up_weight, down_weight],
        [(up + part, units), (down, width)],
        moves,
    )


def unpack(meta, mine, other, out_shape, up_shape):
    out, up = out_shape[0] // 2, up_shape[0] // 2
    width, units = out_shape[1], up_shape[1]
    fold = units // width
    part = out // fold
    moves = []
    for source in (0, 1):
        for i in range(fold):
            onto = by_place(0, out, other=bool(source), offset=i * part)
            moves.append((source, fixed(up), i * width, 0, onto, 0, part, width))
    for source in (0, 1):
        moves.append((source, fixed(0), 0, 1, by_place(0, up, other=bool(source)), 0, up, units))
    return move("unpack", meta, [mine, other], [out_shape, up_shape], moves)


def join(meta, entry, mine, other, name):
    rows, columns = mine[0].shape
    count = len(mine)
    moves = []
    for own in (0, 1):
        for i in range(count):
            onto = by_place(entry, rows * count, other=bool(own), offset=i * rows)
            moves.append((own * count + i, fixed(0), 0, 0, onto, 0, rows, columns))
    return move(name, meta, [*mine, *other], [(2 * count * rows, columns)], moves)[0]


def join_quarters(meta, mine, other):
    half, columns = mine.shape
    quarter = half // 2
    moves = []
    for source in (0, 1):
        for part in (0, 1):

            def onto(meta_ref, source=source, part=part):
                core = 1 - meta_ref[0] if source else meta_ref[0]
                chip = 1 - meta_ref[2] if part else meta_ref[2]
                return pl.multiple_of((2 * core + chip) * quarter, 16)

            moves.append((source, fixed(part * quarter), 0, 0, onto, 0, quarter, columns))
    return move("join_qkv", meta, [mine, other], [(2 * half, columns)], moves)[0]


def normalized(rows):
    row_mean = jnp.mean(rows, axis=-1, keepdims=True)
    centered = rows - row_mean
    variance = jnp.mean(centered * centered, axis=-1, keepdims=True)
    scale = lax.rsqrt(variance + NORM_EPSILON)
    return centered * scale, scale


def norm_back(grad, xhat, scale, gain):
    inner = grad * gain
    mean = jnp.mean(inner, axis=-1, keepdims=True)
    along = jnp.mean(inner * xhat, axis=-1, keepdims=True)
    return scale * (inner - mean - xhat * along)


def low(value):
    return value.astype(BF16).astype(F32)


def gelu_pair(value):
    cdf = 0.5 + 0.5 * lax.erf(value * HALF_ROOT)
    slope = cdf + value * (jnp.exp(-0.5 * value * value) * INVERSE_ROOT_TWO_PI)
    return (value * cdf).astype(BF16), slope.astype(BF16)


def by_lane_pair(weight):
    count, rows, columns = weight.shape
    return weight.reshape(count, rows, -1, LANES).transpose(1, 2, 0, 3).reshape(rows, -1)


def swap_tensor(block):
    return lax.ppermute(block, "tensor", [(0, 1), (1, 0)])


def swap_dp(block, devices, stride):
    return lax.ppermute(block, "dp", [(place, place ^ stride) for place in range(devices)])


def boundary(*values):
    return lax.optimization_barrier(values)


def eighths(rows):
    return jnp.sum(rows.astype(F32).reshape(-1, 8, rows.shape[1]), axis=0)


def columns_of(*sums):
    stacked = jnp.concatenate(sums) if len(sums) > 1 else sums[0]
    owner = lax.broadcasted_iota(jnp.int32, (stacked.shape[0], LANES), 0) // 8
    lane = lax.broadcasted_iota(jnp.int32, (stacked.shape[0], LANES), 1)
    return product(stacked.astype(BF16), (owner == lane).astype(BF16), TN)


def halve_kernel(sides, meta_ref, *refs):
    send_ref, keep_ref = refs[-2:]
    core = meta_ref[0]
    number = 0
    for side, parts in enumerate(sides):
        column = 0
        for width in parts:
            first, second = refs[number][:, 0], refs[number][:, 1]
            columns = slice(column, column + width)
            send_ref[side, :, :, columns] = jnp.where(core == 0, second, first)
            keep_ref[side, :, :, columns] = jnp.where(core == 0, first, second)
            number, column = number + 1, column + width


def halve(meta, sides, devices):
    parts = [part.astype(BF16) for side in sides for part in side]
    rows = parts[0].shape[0] // devices
    widths = [[part.shape[1] for part in side] for side in sides]
    shape = (len(sides), devices // 2, rows, sum(widths[0]))
    step = devices // 4
    out_spec = pl.BlockSpec((len(sides), step) + shape[2:], lambda place, meta: (0, place, 0, 0))
    return call(
        functools.partial(halve_kernel, widths),
        "halve",
        meta,
        (2,),
        [
            (
                part.reshape(devices // 2, 2, rows, part.shape[1]),
                pl.BlockSpec((step, 2, rows, part.shape[1]), lambda place, meta: (place, 0, 0, 0)),
            )
            for part in parts
        ],
        [(shape, BF16, out_spec)] * 2,
        flops=0,
        moved=1024,
    )


def total_of(terms):
    total = terms[0].astype(F32)
    for term in terms[1:]:
        total = total + term.astype(F32)
    return total


def spread_kernel(meta_ref, *refs):
    out_ref = refs[-1]
    total = sum(ref[...].astype(F32) for ref in refs[:-1])
    for block in range(total.shape[1] // (3 * LANES)):
        for kind in range(3):
            start = (3 * block + kind) * LANES
            out_ref[kind, :, block * LANES : (block + 1) * LANES] = total[:, start : start + LANES]


def spread(meta, terms, columns):
    rows = terms[0].shape[0]
    spec = pl.BlockSpec((rows, 3 * columns), lambda i, meta: (0, 0))
    shape = (3, rows, columns)
    return call(
        spread_kernel,
        "spread",
        meta,
        (1,),
        [(term, spec) for term in terms],
        [(shape, F32, pl.BlockSpec(shape, lambda i, meta: (0, 0, 0)))],
        flops=0,
        moved=1024,
    )[0]


class Reduction:
    def __init__(self, sides, devices, plan, meta=None):
        self.devices = devices
        self.plan = list(plan)
        self.left = list(range(devices.bit_length() - 2, -1, -1))
        self.sides = len(sides)
        if meta is not None:
            self.stage = self.plan.pop(0)
            self.left.remove(self.stage)
            self.send, kept = halve(meta, sides, devices)
            self.terms = [kept]
            return
        cut, here = self.halving(self.plan.pop(0))

        def pick(index):
            picked = []
            for parts in sides:
                beside = [
                    self.half(part.astype(BF16).reshape(1, devices, -1, part.shape[1]), cut, index)
                    for part in parts
                ]
                picked.append(jnp.concatenate(beside, axis=-1))
            return jnp.concatenate(picked) if len(picked) > 1 else picked[0]

        self.send, self.terms = pick(1 - here), [pick(here)]

    def halving(self, stage):
        self.stage = stage
        where = self.left.index(stage)
        self.left.remove(stage)
        return 2**where, lax.axis_index("dp") // 2**stage % 2

    def half(self, term, before, index):
        sides, places, rows, columns = term.shape
        cut = term.reshape(sides * before, 2, places // before // 2, rows, columns)
        kept = lax.dynamic_index_in_dim(cut, index, 1, keepdims=False)
        return kept.reshape(sides, places // 2, rows, columns)

    def start(self):
        if self.stage == "x":
            self.received = swap_tensor(self.send)
        else:
            self.received = swap_dp(self.send, self.devices, 2**self.stage)

    def step(self):
        self.advance()
        self.start()

    def advance(self):
        self.terms.append(self.received)
        terms, stage = self.terms, self.plan.pop(0)
        if terms[0].shape[1] == self.devices // 2:
            terms = [total_of(terms)]
        if stage == "x":
            self.stage = stage
            self.send = total_of([term[-1:] for term in terms]).astype(BF16)
            self.terms = [total_of([term[:-1] for term in terms])] if self.sides > 1 else []
            self.sides = 1
        else:
            cut, here = self.halving(stage)
            self.send = total_of([self.half(term, cut, 1 - here) for term in terms]).astype(BF16)
            self.terms = [total_of([self.half(term, cut, here) for term in terms])]

    def finish(self):
        while self.plan:
            self.step()
        self.terms.append(self.received)
        return total_of([term.reshape(term.shape[-2:]) for term in self.terms])


def body(
    hidden_in,
    pair_lengths,
    candidates,
    qkv_weight,
    qv_bias,
    out_weight,
    out_bias,
    norm1_gain,
    norm1_shift,
    up_weight,
    up_bias,
    down_weight,
    down_bias,
    norm2_gain,
    norm2_shift,
    out_cotangent,
    *,
    devices,
):
    pairs = pair_lengths.shape[0] // 2
    width = hidden_in.shape[1]
    local = qv_bias.shape[1]
    row_count = hidden_in.shape[0] // 2
    span = row_count // pairs
    place, tensor = lax.axis_index("dp"), lax.axis_index("tensor")
    meta = jnp.stack([place % 2, tensor, place // 2 % 2]).astype(jnp.int32)
    bits = list(range(1, devices.bit_length() - 1))

    def own(array, size):
        return lax.dynamic_slice_in_dim(array, tensor * size, size, 0)

    qkv_local_weight, qkv_piece = pack_qkv(meta, qkv_weight)
    qkv_mine = swap_tensor(qkv_piece)
    biases_other = swap_tensor(jnp.concatenate([qv_bias.reshape(-1), up_bias]))
    out_up_piece, down_piece = pack(meta, out_weight, up_weight, down_weight)
    out_up_mine = swap_tensor(out_up_piece)
    rows = own(hidden_in, row_count)

    def qkv_bias(bias):
        return by_lane_pair(jnp.stack([bias[0], jnp.zeros_like(bias[0]), bias[1]]).reshape(3, 1, local))

    bias_local = qkv_bias(qv_bias)
    rows, bias_local, qkv_local_weight, out_up_piece, down_piece, qkv_mine, biases_other = boundary(
        rows, bias_local, qkv_local_weight, out_up_piece, down_piece, qkv_mine, biases_other
    )
    qkv_next = swap_dp(qkv_mine, devices, 2)
    qkv_local, context_local, totals_local = attend(
        meta, pair_lengths, rows, qkv_local_weight, bias_local, pairs
    )
    context_local, qkv_next = boundary(context_local, qkv_next)
    qkv_half = jnp.concatenate([qkv_mine, qkv_next])
    qkv_remote_weight = join_quarters(meta, qkv_half, swap_dp(qkv_half, devices, 1))
    remote_bias = biases_other[: 2 * local].reshape(2, local)
    qkv_remote, context_remote, totals_remote = attend(
        meta, pair_lengths, rows, qkv_remote_weight, qkv_bias(remote_bias), pairs
    )
    context_local, context_remote, out_up_mine = boundary(context_local, context_remote, out_up_mine)
    down_mine = swap_tensor(down_piece)
    out_up_other = swap_dp(out_up_mine, devices, 1)
    part_local = product(context_local, out_weight, NN).astype(BF16)
    out_up_mine, out_up_other, part_local = boundary(out_up_mine, out_up_other, part_local)
    out_remote_weight, up_remote_weight = unpack(
        meta, out_up_mine, out_up_other, out_weight.shape, up_weight.shape
    )
    part_remote = low(product(context_remote, out_remote_weight, NN))
    residual = rows.astype(F32) + (part_local.astype(F32) + part_remote) + out_bias
    xhat_one, scale_one = normalized(residual)
    normed_one = xhat_one * norm1_gain + norm1_shift
    normed = normed_one.astype(BF16)

    def expand(weight, bias):
        return boundary(*gelu_pair(product(normed, weight, NN) + bias))

    act_local, slope_local = expand(up_weight, up_bias)
    ff_local = product(act_local, down_weight, NN).astype(BF16)
    act_remote, slope_remote = expand(up_remote_weight, biases_other[2 * local :])
    act_remote, down_mine, ff_local = boundary(act_remote, down_mine, ff_local)
    down_other = swap_dp(down_mine, devices, 1)
    down_remote_weight = join(meta, 0, [down_mine], [down_other], "join_down")
    ff_remote = low(product(act_remote, down_remote_weight, NN))
    xhat, scale = normalized(normed_one + (ff_local.astype(F32) + ff_remote) + down_bias)
    block_mine = (xhat * norm2_gain + norm2_shift).astype(BF16)

    counts = own(candidates, pairs).astype(F32)[:, None, None]
    grad_output = own(out_cotangent, row_count).astype(F32).reshape(pairs, span, width) / counts
    grad_output = grad_output.reshape(row_count, width)
    grad_two = norm_back(grad_output, xhat, scale, norm2_gain)
    grad_two_low = grad_two.astype(BF16)
    sums = [eighths(grad_two), eighths(grad_output * xhat), eighths(grad_output)]
    grad_two_low, block_mine = boundary(grad_two_low, block_mine)
    block_other = swap_tensor(block_mine)

    def weight_grad(left, right):
        return product(left, right, TN).astype(BF16)

    down_sum = Reduction(
        [[weight_grad(grad_two_low, act_local)], [weight_grad(grad_two_low, act_remote)]],
        devices,
        [0] + bits[:1] + ["x"] + bits[1:],
    )
    grad_two_low, down_sum.send = boundary(grad_two_low, down_sum.send)
    down_sum.start()
    grad_pre = []
    for weight, slope in ((down_weight, slope_local), (down_remote_weight, slope_remote)):
        grad_pre.append((product(grad_two_low, weight, NT) * slope.astype(F32)).astype(BF16))
    pre_local, pre_remote, down_sum.received = boundary(*grad_pre, down_sum.received)
    down_sum.step()
    grad_normed = (
        grad_two + product(pre_local, up_weight, NT) + product(pre_remote, up_remote_weight, NT)
    )
    grad_one = norm_back(grad_normed, xhat_one, scale_one, norm1_gain)
    grad_one_low = grad_one.astype(BF16)
    sums += [eighths(grad_one), eighths(grad_normed * xhat_one), eighths(grad_normed)]
    shared = columns_of(*sums)

    def extras(pre):
        zero = jnp.zeros((8, pre.shape[1]), F32)
        sums_up = eighths(pre)
        first = columns_of(*[zero] * len(sums), sums_up).reshape(devices, 2, -1, LANES)[:, 0]
        second = columns_of(*[zero] * len(sums), zero, sums_up).reshape(devices, 2, -1, LANES)[:, 1]
        return shared + (first + second).reshape(width, LANES)

    wide_sum = Reduction(
        [
            [weight_grad(normed, pre), weight_grad(grad_one_low, context), extras(pre)]
            for pre, context in ((pre_local, context_local), (pre_remote, context_remote))
        ],
        devices,
        [0] + bits[1:] + bits[:1] + ["x"],
    )
    grad_one_low, wide_sum.send = boundary(grad_one_low, wide_sum.send)
    wide_sum.start()
    grad_one_low, wide_sum.received = boundary(grad_one_low, wide_sum.received)
    wide_sum.advance()
    grad_one_low, wide_sum.send, wide_sum.terms, down_sum.terms = boundary(
        grad_one_low, wide_sum.send, wide_sum.terms, down_sum.terms
    )
    wide_sum.start()

    def attention_back(side, base, rows_type):
        qkv, out, totals, weight = {
            "local": (qkv_local, out_weight, totals_local, qkv_local_weight),
            "remote": (qkv_remote, out_remote_weight, totals_remote, qkv_remote_weight),
        }[side]
        return attend_back(
            meta, pair_lengths, qkv, grad_one_low, out, totals, rows, weight, base, rows_type
        )

    def qv_columns(sums_qv):
        column = columns_of(sums_qv).reshape(-1, 3, LANES, LANES)
        column = [column[:, kind].reshape(devices, -1, LANES) for kind in (0, 2)]
        return jnp.concatenate(column, axis=1).reshape(width, LANES)

    rows_part, far_grad, far_sums = attention_back("remote", grad_one, F32)
    far_sum = Reduction([[far_grad, qv_columns(far_sums)]], devices, [0, "x"], meta)
    (far_sum.send,) = boundary(far_sum.send)
    far_sum.start()
    rows_part, down_sum.received, wide_sum.received, block_other = boundary(
        rows_part, down_sum.received, wide_sum.received, block_other
    )
    down_sum.advance()
    wide_sum.advance()
    rows_part, far_sum.received, down_sum.send, wide_sum.send = boundary(
        rows_part, far_sum.received, down_sum.send, wide_sum.send
    )
    wide_sum.start()
    far_sum.advance()
    rows_part, far_sum.send = boundary(rows_part, far_sum.send)
    far_sum.start()
    down_sum.start()
    grad_in, near_grad, near_sums = attention_back("local", rows_part, BF16)
    near_grad, down_sum.received, wide_sum.received = boundary(
        near_grad, down_sum.received, wide_sum.received
    )
    down_sum.step()
    wide_sum.step()
    other_in = swap_tensor(grad_in)
    near_sum = Reduction([[near_grad, qv_columns(near_sums)]], devices, [0] + bits, meta)
    near_sum.send, block_mine = boundary(near_sum.send, block_mine)
    near_sum.start()
    block_out = join(meta, 1, [block_mine], [block_other], "join_block")
    near_sum.received, far_sum.received, block_out = boundary(near_sum.received, far_sum.received, block_out)
    near_sum.terms.append(far_sum.received)
    near_sum.step()
    near_sum.received, down_sum.received = boundary(near_sum.received, down_sum.received)
    near_sum.step()
    down_sum.step()
    near_sum.received, wide_sum.received = boundary(near_sum.received, wide_sum.received)
    while near_sum.plan:
        near_sum.step()
    wide_sum.step()
    near_sum.send, grad_in, down_sum.received = boundary(near_sum.send, grad_in, down_sum.received)
    share_down = down_sum.finish().T
    wide = wide_sum.finish()
    units = up_weight.shape[1]
    vectors = wide[:, units + local :].T
    near_sum.received, share_down = boundary(near_sum.received, share_down)
    near_terms = [term.reshape(term.shape[-2:]) for term in near_sum.terms + [near_sum.received]]
    share_qkv = spread(meta, near_terms, local)
    share_qv = total_of([term[:, 3 * local] for term in near_terms]).reshape(2, -1)
    return (
        block_out,
        join(meta, 1, [grad_in], [other_in], "join_in"),
        share_qkv,
        share_qv,
        wide[:, units : units + local].T,
        vectors[3],
        vectors[4],
        vectors[5],
        wide[:, :units],
        vectors[6:8].reshape(-1),
        share_down,
        vectors[0],
        vectors[1],
        vectors[2],
    )


def solution(mesh):
    devices = mesh.shape["dp"]
    in_specs = (
        P("dp", None),
        P("dp"),
        P("dp"),
        P(None, None, "tensor"),
        P(None, "tensor"),
        P("tensor", None),
        P(),
        P(),
        P(),
        P(None, "tensor"),
        P("tensor"),
        P("tensor", None),
        P(),
        P(),
        P(),
        P("dp", None),
    )
    out_specs = (
        P("dp", None),
        P("dp", None),
        P(None, "dp", "tensor"),
        P(None, ("tensor", "dp")),
        P("tensor", "dp"),
        P("dp"),
        P("dp"),
        P("dp"),
        P("dp", "tensor"),
        P(("tensor", "dp")),
        P("tensor", "dp"),
        P("dp"),
        P("dp"),
        P("dp"),
    )
    return jax.shard_map(
        functools.partial(body, devices=devices),
        mesh=mesh,
        in_specs=in_specs,
        out_specs=out_specs,
        check_vma=False,
    )
```

```python
import functools

import jax
import jax.numpy as jnp
from jax import lax
from jax.experimental import pallas as pl
from jax.experimental.pallas import tpu as pltpu
from jax.sharding import PartitionSpec as P

HEAD_DIM = 64
LANES = 128
VMEM_BYTES = 60 * 1024 * 1024
NORM_EPSILON = 1e-12
HALF_ROOT = 0.7071067811865476
INVERSE_ROOT_TWO_PI = 0.3989422804014327
SCORE_SCALE = HEAD_DIM ** (-0.5)
NT = (((1,), (1,)), ((), ()))
NN = (((1,), (0,)), ((), ()))
TN = (((0,), (0,)), ((), ()))
F32 = jnp.float32
BF16 = jnp.bfloat16


def product(left, right, dims):
    return lax.dot_general(left, right, dims, preferred_element_type=F32)


def head_halves(block):
    lane = lax.broadcasted_iota(jnp.int32, (1, LANES), 1)
    zero = jnp.zeros_like(block)
    return jnp.where(lane < HEAD_DIM, block, zero), jnp.where(lane < HEAD_DIM, zero, block)


def call(kernel, name, meta, grid, inputs, outputs, flops, moved, exps=0, scratch=()):
    return pl.pallas_call(
        kernel,
        out_shape=[jax.ShapeDtypeStruct(shape, dtype) for shape, dtype, spec in outputs],
        grid_spec=pltpu.PrefetchScalarGridSpec(
            num_scalar_prefetch=1,
            grid=grid,
            in_specs=[spec for array, spec in inputs],
            out_specs=[spec for shape, dtype, spec in outputs],
            scratch_shapes=list(scratch),
        ),
        cost_estimate=pl.CostEstimate(flops=0, bytes_accessed=1024, transcendentals=0),
        name=name,
    )(meta, *[array for array, spec in inputs])


def attend_kernel(meta_ref, length_ref, rows_ref, weight_ref, bias_ref, qkv_ref, context_ref, total_ref):
    length = length_ref[meta_ref[1] * pl.num_programs(0) + pl.program_id(0)]
    qkv = (product(rows_ref[...], weight_ref[...], NN) + bias_ref[...]).astype(BF16)
    qkv_ref[...] = qkv
    keys = qkv[:, LANES : 2 * LANES] * SCORE_SCALE
    valid = lax.broadcasted_iota(jnp.int32, (keys.shape[0], 1), 0) < length
    heads = zip(head_halves(qkv[:, :LANES]), head_halves(qkv[:, 2 * LANES :]))
    flipped = None
    for head, (query, value) in enumerate(heads):
        scores = jnp.where(valid, product(keys, query, NT), -1000000000.0)
        peak = jnp.max(scores, axis=0, keepdims=True)
        exponent = jnp.exp(scores - peak)
        total = jnp.sum(exponent, axis=0, keepdims=True)
        probs_low = (exponent * (1.0 / total)).astype(BF16)
        part = product(value, probs_low, TN)
        flipped = part if flipped is None else flipped + part
        total_ref[0, 0, head : head + 1, :] = peak + jnp.log(total)
    context_ref[...] = flipped.T.astype(BF16)


def attend(meta, lengths, rows, weight, bias, pairs):
    row_count, width = rows.shape
    columns = weight.shape[1]
    span, blocks = row_count // pairs, columns // (3 * LANES)
    work = row_count * span * blocks * LANES
    by_block = lambda pair, lanes, meta: (pair, lanes)
    return call(
        attend_kernel,
        "attend",
        meta,
        (pairs, blocks),
        [
            (lengths, pl.BlockSpec(memory_space=pltpu.SMEM)),
            (rows, pl.BlockSpec((span, width), lambda pair, lanes, meta: (pair, 0))),
            (weight, pl.BlockSpec((width, 3 * LANES), lambda pair, lanes, meta: (0, lanes))),
            (bias, pl.BlockSpec((1, 3 * LANES), lambda pair, lanes, meta: (0, lanes))),
        ],
        [
            ((row_count, columns), BF16, pl.BlockSpec((span, 3 * LANES), by_block)),
            ((row_count, blocks * LANES), BF16, pl.BlockSpec((span, LANES), by_block)),
            (
                (pairs, blocks, 2, span),
                F32,
                pl.BlockSpec((1, 1, 2, span), lambda pair, lanes, meta: (pair, lanes, 0, 0)),
            ),
        ],
        flops=16 * work,
        moved=8 * row_count * blocks * LANES,
        exps=work // HEAD_DIM,
    )


def attend_back_kernel(
    meta_ref,
    length_ref,
    qkv_ref,
    low_ref,
    out_ref,
    total_ref,
    rows_ref,
    weight_ref,
    base_ref,
    rows_grad_ref,
    weight_grad_ref,
    sums_ref,
    rows_sum,
    weight_sum,
):
    step, lanes = pl.program_id(0), pl.program_id(1)
    length = length_ref[meta_ref[1] * pl.num_programs(0) + step]
    keys = qkv_ref[:, LANES : 2 * LANES] * SCORE_SCALE
    values = qkv_ref[:, 2 * LANES :]
    valid = lax.broadcasted_iota(jnp.int32, (keys.shape[0], 1), 0) < length
    context_grad = product(low_ref[...], out_ref[...], NT).astype(BF16)
    heads = zip(head_halves(qkv_ref[:, :LANES]), head_halves(keys), head_halves(context_grad))
    sums = [None, None, None]
    for head, (query, key, grad) in enumerate(heads):
        scores = jnp.where(valid, product(keys, query, NT), -1000000000.0)
        probs = jnp.exp(scores - total_ref[0, 0, head : head + 1, :])
        grad_probs = product(values, grad, NT)
        weighted = probs * grad_probs
        inner = jnp.sum(weighted, axis=0, keepdims=True)
        grad_scores = (weighted - probs * inner).astype(BF16)
        parts = (
            product(grad_scores, key, TN),
            product(grad_scores, query, NN),
            product(probs.astype(BF16), grad, NN),
        )
        sums = [b if a is None else a + b for a, b in zip(sums, parts)]
    grads = [sums[0].astype(BF16), (sums[1] * SCORE_SCALE).astype(BF16), sums[2].astype(BF16)]
    grads = jnp.concatenate(grads, axis=1)
    rows_part = product(grads, weight_ref[...], NT)
    weight_part = product(rows_ref[...], grads, TN)
    columns = pl.ds(pl.multiple_of(lanes * 3 * LANES, LANES), 3 * LANES)
    column_sums = jnp.sum(grads.astype(F32).reshape(-1, 8, 3 * LANES), axis=0)

    @pl.when(lanes == 0)
    def _():
        rows_sum[...] = base_ref[...] + rows_part

    @pl.when(lanes > 0)
    def _():
        rows_sum[...] += rows_part

    @pl.when(lanes == pl.num_programs(1) - 1)
    def _():
        rows_grad_ref[...] = rows_sum[...].astype(rows_grad_ref.dtype)

    @pl.when(step == 0)
    def _():
        weight_sum[:, columns] = weight_part
        sums_ref[:, columns] = column_sums

    @pl.when(step > 0)
    def _():
        weight_sum[:, columns] += weight_part
        sums_ref[:, columns] += column_sums

    @pl.when(step == pl.num_programs(0) - 1)
    def _():
        weight_grad_ref[:, columns] = weight_sum[:, columns].astype(weight_grad_ref.dtype)


def attend_back(meta, lengths, qkv, low_grad, out, totals, rows, weight, base, rows_type):
    pairs = totals.shape[0]
    width, columns = weight.shape
    span, blocks = rows.shape[0] // pairs, columns // (3 * LANES)
    by_pair = lambda pair, lanes, meta: (pair, 0)
    whole = lambda pair, lanes, meta: (0, 0)
    inputs = [
        (lengths, pl.BlockSpec(memory_space=pltpu.SMEM)),
        (qkv, pl.BlockSpec((span, 3 * LANES), lambda pair, lanes, meta: (pair, lanes))),
        (low_grad, pl.BlockSpec((span, width), by_pair)),
        (out, pl.BlockSpec((LANES, width), lambda pair, lanes, meta: (lanes, 0))),
        (totals, pl.BlockSpec((1, 1, 2, span), lambda pair, lanes, meta: (pair, lanes, 0, 0))),
        (rows, pl.BlockSpec((span, width), by_pair)),
        (weight, pl.BlockSpec((width, 3 * LANES), lambda pair, lanes, meta: (0, lanes))),
        (base, pl.BlockSpec((span, width), by_pair)),
    ]
    return call(
        attend_back_kernel,
        "attend_back",
        meta,
        (pairs, blocks),
        inputs,
        [
            (rows.shape, rows_type, pl.BlockSpec((span, width), by_pair)),
            ((width, columns), BF16, pl.BlockSpec((width, columns), whole)),
            ((8, columns), F32, pl.BlockSpec((8, columns), whole)),
        ],
        flops=0,
        moved=1024,
        scratch=[pltpu.VMEM((span, width), F32), pltpu.VMEM((width, columns), F32)],
    )


def move_kernel(moves, source_count, target_count, meta_ref, *refs):
    sources = refs[:source_count]
    targets = refs[source_count : source_count + target_count]
    rest = refs[source_count + target_count :]
    buffers, arrived, left = rest[: len(moves)], rest[-2], rest[-1]
    incoming, outgoing = [], []
    for number, (source, row, column, target, to_row, to_column, rows, columns) in enumerate(moves):
        into = sources[source].at[pl.ds(row(meta_ref), rows), pl.ds(column, columns)]
        onto = targets[target].at[pl.ds(to_row(meta_ref), rows), pl.ds(to_column, columns)]
        incoming.append(pltpu.make_async_copy(into, buffers[number], arrived.at[number]))
        outgoing.append(pltpu.make_async_copy(buffers[number], onto, left.at[number]))
    for copy in incoming:
        copy.start()
    for copy_in, copy_out in zip(incoming, outgoing):
        copy_in.wait()
        copy_out.start()
    for copy in outgoing:
        copy.wait()


def pieces(entry):
    source, row, column, target, to_row, to_column, rows, columns = entry
    count = next((n for n in (4, 2) if rows % (16 * n) == 0 and rows * columns >= n * 2**16), 1)
    step = rows // count
    return [
        (
            source,
            functools.partial(lambda meta_ref, base, at: pl.multiple_of(base(meta_ref) + at, 16), base=row, at=i * step)
            if rows % 16 == 0
            else row,
            column,
            target,
            functools.partial(
                lambda meta_ref, base, at: pl.multiple_of(base(meta_ref) + at, 16), base=to_row, at=i * step
            )
            if rows % 16 == 0
            else to_row,
            to_column,
            step,
            columns,
        )
        for i in range(count)
    ]


def move(name, meta, sources, targets, moves):
    moves = [part for entry in moves for part in pieces(entry)]
    return call(
        functools.partial(move_kernel, moves, len(sources), len(targets)),
        name,
        meta,
        (1,),
        [(source, pl.BlockSpec(memory_space=pl.ANY)) for source in sources],
        [(shape, BF16, pl.BlockSpec(memory_space=pl.ANY)) for shape in targets],
        flops=0,
        moved=4 * sum(entry[6] * entry[7] for entry in moves),
        scratch=[pltpu.VMEM(entry[6:], BF16) for entry in moves]
        + [pltpu.SemaphoreType.DMA((len(moves),))] * 2,
    )


def fixed(row):
    return lambda meta_ref: row


def by_place(entry, rows, other=False, offset=0):
    def start(meta_ref):
        place = 1 - meta_ref[entry] if other else meta_ref[entry]
        return pl.multiple_of(place * rows + offset, 16)

    return start


def pack_qkv_kernel(blocks, meta_ref, weight_ref, whole_ref, quarter_ref, buffer, arrived, left):
    copies = []
    for kind in range(3):
        for block in range(blocks):
            number = 3 * block + kind
            copies.append(
                pltpu.make_async_copy(
                    weight_ref.at[kind, :, pl.ds(block * LANES, LANES)],
                    buffer.at[:, pl.ds(number * LANES, LANES)],
                    arrived.at[number],
                )
            )
    for copy in copies:
        copy.start()
    for copy in copies:
        copy.wait()
    quarter = quarter_ref.shape[0]
    mine = pl.ds(pl.multiple_of((2 * meta_ref[0] + meta_ref[2]) * quarter, 16), quarter)
    out = [
        pltpu.make_async_copy(buffer.at[mine], quarter_ref, left.at[0]),
        pltpu.make_async_copy(buffer, whole_ref, left.at[1]),
    ]
    for copy in out:
        copy.start()
    for copy in out:
        copy.wait()


def pack_qkv(meta, weight):
    kinds, rows, columns = weight.shape
    shapes = [(rows, kinds * columns), (rows // 4, kinds * columns)]
    return call(
        functools.partial(pack_qkv_kernel, columns // LANES),
        "pack_qkv",
        meta,
        (1,),
        [(weight, pl.BlockSpec(memory_space=pl.ANY))],
        [(shape, BF16, pl.BlockSpec(memory_space=pl.ANY)) for shape in shapes],
        flops=0,
        moved=5 * weight.size,
        scratch=[
            pltpu.VMEM(shapes[0], BF16),
            pltpu.SemaphoreType.DMA((kinds * columns // LANES,)),
            pltpu.SemaphoreType.DMA((2,)),
        ],
    )


def pack(meta, out_weight, up_weight, down_weight):
    out, up, down = [weight.shape[0] // 2 for weight in (out_weight, up_weight, down_weight)]
    width, units = out_weight.shape[1], up_weight.shape[1]
    fold = units // width
    part = out // fold
    moves = [(1, by_place(0, up), 0, 0, fixed(0), 0, up, units)]
    for i in range(fold):
        moves.append((0, by_place(0, out, offset=i * part), 0, 0, fixed(up), i * width, part, width))
    moves.append((2, by_place(0, down), 0, 1, fixed(0), 0, down, width))
    return move(
        "pack",
        meta,
        [out_weight, up_weight, down_weight],
        [(up + part, units), (down, width)],
        moves,
    )


def unpack(meta, mine, other, out_shape, up_shape):
    out, up = out_shape[0] // 2, up_shape[0] // 2
    width, units = out_shape[1], up_shape[1]
    fold = units // width
    part = out // fold
    moves = []
    for source in (0, 1):
        for i in range(fold):
            onto = by_place(0, out, other=bool(source), offset=i * part)
            moves.append((source, fixed(up), i * width, 0, onto, 0, part, width))
    for source in (0, 1):
        moves.append((source, fixed(0), 0, 1, by_place(0, up, other=bool(source)), 0, up, units))
    return move("unpack", meta, [mine, other], [out_shape, up_shape], moves)


def join(meta, entry, mine, other, name):
    rows, columns = mine[0].shape
    count = len(mine)
    moves = []
    for own in (0, 1):
        for i in range(count):
            onto = by_place(entry, rows * count, other=bool(own), offset=i * rows)
            moves.append((own * count + i, fixed(0), 0, 0, onto, 0, rows, columns))
    return move(name, meta, [*mine, *other], [(2 * count * rows, columns)], moves)[0]


def join_quarters(meta, mine, other):
    half, columns = mine.shape
    quarter = half // 2
    moves = []
    for source in (0, 1):
        for part in (0, 1):

            def onto(meta_ref, source=source, part=part):
                core = 1 - meta_ref[0] if source else meta_ref[0]
                chip = 1 - meta_ref[2] if part else meta_ref[2]
                return pl.multiple_of((2 * core + chip) * quarter, 16)

            moves.append((source, fixed(part * quarter), 0, 0, onto, 0, quarter, columns))
    return move("join_qkv", meta, [mine, other], [(2 * half, columns)], moves)[0]


def normalized(rows):
    row_mean = jnp.mean(rows, axis=-1, keepdims=True)
    centered = rows - row_mean
    variance = jnp.mean(centered * centered, axis=-1, keepdims=True)
    scale = lax.rsqrt(variance + NORM_EPSILON)
    return centered * scale, scale


def norm_back(grad, xhat, scale, gain):
    inner = grad * gain
    mean = jnp.mean(inner, axis=-1, keepdims=True)
    along = jnp.mean(inner * xhat, axis=-1, keepdims=True)
    return scale * (inner - mean - xhat * along)


def low(value):
    return value.astype(BF16).astype(F32)


def gelu_pair(value):
    cdf = 0.5 + 0.5 * lax.erf(value * HALF_ROOT)
    slope = cdf + value * (jnp.exp(-0.5 * value * value) * INVERSE_ROOT_TWO_PI)
    return (value * cdf).astype(BF16), slope.astype(BF16)


def by_lane_pair(weight):
    count, rows, columns = weight.shape
    return weight.reshape(count, rows, -1, LANES).transpose(1, 2, 0, 3).reshape(rows, -1)


def swap_tensor(block):
    return lax.ppermute(block, "tensor", [(0, 1), (1, 0)])


def swap_dp(block, devices, stride):
    return lax.ppermute(block, "dp", [(place, place ^ stride) for place in range(devices)])


def boundary(*values):
    return lax.optimization_barrier(values)


def eighths(rows):
    return jnp.sum(rows.astype(F32).reshape(-1, 8, rows.shape[1]), axis=0)


def columns_of(*sums):
    stacked = jnp.concatenate(sums) if len(sums) > 1 else sums[0]
    owner = lax.broadcasted_iota(jnp.int32, (stacked.shape[0], LANES), 0) // 8
    lane = lax.broadcasted_iota(jnp.int32, (stacked.shape[0], LANES), 1)
    return product(stacked.astype(BF16), (owner == lane).astype(BF16), TN)


def halve_kernel(sides, meta_ref, *refs):
    send_ref, keep_ref = refs[-2:]
    core = meta_ref[0]
    number = 0
    for side, parts in enumerate(sides):
        column = 0
        for width in parts:
            first, second = refs[number][:, 0], refs[number][:, 1]
            columns = slice(column, column + width)
            send_ref[side, :, :, columns] = jnp.where(core == 0, second, first)
            keep_ref[side, :, :, columns] = jnp.where(core == 0, first, second)
            number, column = number + 1, column + width


def halve(meta, sides, devices):
    parts = [part.astype(BF16) for side in sides for part in side]
    rows = parts[0].shape[0] // devices
    widths = [[part.shape[1] for part in side] for side in sides]
    shape = (len(sides), devices // 2, rows, sum(widths[0]))
    step = devices // 4
    out_spec = pl.BlockSpec((len(sides), step) + shape[2:], lambda place, meta: (0, place, 0, 0))
    return call(
        functools.partial(halve_kernel, widths),
        "halve",
        meta,
        (2,),
        [
            (
                part.reshape(devices // 2, 2, rows, part.shape[1]),
                pl.BlockSpec((step, 2, rows, part.shape[1]), lambda place, meta: (place, 0, 0, 0)),
            )
            for part in parts
        ],
        [(shape, BF16, out_spec)] * 2,
        flops=0,
        moved=1024,
    )


def total_of(terms):
    total = terms[0].astype(F32)
    for term in terms[1:]:
        total = total + term.astype(F32)
    return total


def spread_kernel(meta_ref, *refs):
    out_ref = refs[-1]
    total = sum(ref[...].astype(F32) for ref in refs[:-1])
    for block in range(total.shape[1] // (3 * LANES)):
        for kind in range(3):
            start = (3 * block + kind) * LANES
            out_ref[kind, :, block * LANES : (block + 1) * LANES] = total[:, start : start + LANES]


def spread(meta, terms, columns):
    rows = terms[0].shape[0]
    spec = pl.BlockSpec((rows, 3 * columns), lambda i, meta: (0, 0))
    shape = (3, rows, columns)
    return call(
        spread_kernel,
        "spread",
        meta,
        (1,),
        [(term, spec) for term in terms],
        [(shape, F32, pl.BlockSpec(shape, lambda i, meta: (0, 0, 0)))],
        flops=0,
        moved=1024,
    )[0]


class Reduction:
    def __init__(self, sides, devices, plan, meta=None):
        self.devices = devices
        self.plan = list(plan)
        self.left = list(range(devices.bit_length() - 2, -1, -1))
        self.sides = len(sides)
        if meta is not None:
            self.stage = self.plan.pop(0)
            self.left.remove(self.stage)
            self.send, kept = halve(meta, sides, devices)
            self.terms = [kept]
            return
        cut, here = self.halving(self.plan.pop(0))

        def pick(index):
            picked = []
            for parts in sides:
                beside = [
                    self.half(part.astype(BF16).reshape(1, devices, -1, part.shape[1]), cut, index)
                    for part in parts
                ]
                picked.append(jnp.concatenate(beside, axis=-1))
            return jnp.concatenate(picked) if len(picked) > 1 else picked[0]

        self.send, self.terms = pick(1 - here), [pick(here)]

    def halving(self, stage):
        self.stage = stage
        where = self.left.index(stage)
        self.left.remove(stage)
        return 2**where, lax.axis_index("dp") // 2**stage % 2

    def half(self, term, before, index):
        sides, places, rows, columns = term.shape
        cut = term.reshape(sides * before, 2, places // before // 2, rows, columns)
        kept = lax.dynamic_index_in_dim(cut, index, 1, keepdims=False)
        return kept.reshape(sides, places // 2, rows, columns)

    def start(self):
        if self.stage == "x":
            self.received = swap_tensor(self.send)
        else:
            self.received = swap_dp(self.send, self.devices, 2**self.stage)

    def step(self):
        self.advance()
        self.start()

    def advance(self):
        self.terms.append(self.received)
        terms, stage = self.terms, self.plan.pop(0)
        if terms[0].shape[1] == self.devices // 2:
            terms = [total_of(terms)]
        if stage == "x":
            self.stage = stage
            self.send = total_of([term[-1:] for term in terms]).astype(BF16)
            self.terms = [total_of([term[:-1] for term in terms])] if self.sides > 1 else []
            self.sides = 1
        else:
            cut, here = self.halving(stage)
            self.send = total_of([self.half(term, cut, 1 - here) for term in terms]).astype(BF16)
            self.terms = [total_of([self.half(term, cut, here) for term in terms])]

    def finish(self):
        while self.plan:
            self.step()
        self.terms.append(self.received)
        return total_of([term.reshape(term.shape[-2:]) for term in self.terms])


def body(
    hidden_in,
    pair_lengths,
    candidates,
    qkv_weight,
    qv_bias,
    out_weight,
    out_bias,
    norm1_gain,
    norm1_shift,
    up_weight,
    up_bias,
    down_weight,
    down_bias,
    norm2_gain,
    norm2_shift,
    out_cotangent,
    *,
    devices,
):
    pairs = pair_lengths.shape[0] // 2
    width = hidden_in.shape[1]
    local = qv_bias.shape[1]
    row_count = hidden_in.shape[0] // 2
    span = row_count // pairs
    place, tensor = lax.axis_index("dp"), lax.axis_index("tensor")
    meta = jnp.stack([place % 2, tensor, place // 2 % 2]).astype(jnp.int32)
    bits = list(range(1, devices.bit_length() - 1))

    def own(array, size):
        return lax.dynamic_slice_in_dim(array, tensor * size, size, 0)

    qkv_local_weight, qkv_piece = pack_qkv(meta, qkv_weight)
    qkv_mine = swap_tensor(qkv_piece)
    biases_other = swap_tensor(jnp.concatenate([qv_bias.reshape(-1), up_bias]))
    out_up_piece, down_piece = pack(meta, out_weight, up_weight, down_weight)
    out_up_mine = swap_tensor(out_up_piece)
    rows = own(hidden_in, row_count)

    def qkv_bias(bias):
        return by_lane_pair(jnp.stack([bias[0], jnp.zeros_like(bias[0]), bias[1]]).reshape(3, 1, local))

    bias_local = qkv_bias(qv_bias)
    rows, bias_local, qkv_local_weight, out_up_piece, down_piece, qkv_mine, biases_other = boundary(
        rows, bias_local, qkv_local_weight, out_up_piece, down_piece, qkv_mine, biases_other
    )
    qkv_next = swap_dp(qkv_mine, devices, 2)
    qkv_local, context_local, totals_local = attend(
        meta, pair_lengths, rows, qkv_local_weight, bias_local, pairs
    )
    context_local, qkv_next = boundary(context_local, qkv_next)
    qkv_half = jnp.concatenate([qkv_mine, qkv_next])
    qkv_remote_weight = join_quarters(meta, qkv_half, swap_dp(qkv_half, devices, 1))
    remote_bias = biases_other[: 2 * local].reshape(2, local)
    qkv_remote, context_remote, totals_remote = attend(
        meta, pair_lengths, rows, qkv_remote_weight, qkv_bias(remote_bias), pairs
    )
    context_local, context_remote, out_up_mine = boundary(context_local, context_remote, out_up_mine)
    down_mine = swap_tensor(down_piece)
    out_up_other = swap_dp(out_up_mine, devices, 1)
    part_local = product(context_local, out_weight, NN).astype(BF16)
    out_up_mine, out_up_other, part_local = boundary(out_up_mine, out_up_other, part_local)
    out_remote_weight, up_remote_weight = unpack(
        meta, out_up_mine, out_up_other, out_weight.shape, up_weight.shape
    )
    part_remote = low(product(context_remote, out_remote_weight, NN))
    residual = rows.astype(F32) + (part_local.astype(F32) + part_remote) + out_bias
    xhat_one, scale_one = normalized(residual)
    normed_one = xhat_one * norm1_gain + norm1_shift
    normed = normed_one.astype(BF16)

    def expand(weight, bias):
        return boundary(*gelu_pair(product(normed, weight, NN) + bias))

    act_local, slope_local = expand(up_weight, up_bias)
    ff_local = product(act_local, down_weight, NN).astype(BF16)
    act_remote, slope_remote = expand(up_remote_weight, biases_other[2 * local :])
    act_remote, down_mine, ff_local = boundary(act_remote, down_mine, ff_local)
    down_other = swap_dp(down_mine, devices, 1)
    down_remote_weight = join(meta, 0, [down_mine], [down_other], "join_down")
    ff_remote = low(product(act_remote, down_remote_weight, NN))
    xhat, scale = normalized(normed_one + (ff_local.astype(F32) + ff_remote) + down_bias)
    block_mine = (xhat * norm2_gain + norm2_shift).astype(BF16)

    counts = own(candidates, pairs).astype(F32)[:, None, None]
    grad_output = own(out_cotangent, row_count).astype(F32).reshape(pairs, span, width) / counts
    grad_output = grad_output.reshape(row_count, width)
    grad_two = norm_back(grad_output, xhat, scale, norm2_gain)
    grad_two_low = grad_two.astype(BF16)
    sums = [eighths(grad_two), eighths(grad_output * xhat), eighths(grad_output)]
    grad_two_low, block_mine = boundary(grad_two_low, block_mine)
    block_other = swap_tensor(block_mine)

    def weight_grad(left, right):
        return product(left, right, TN).astype(BF16)

    down_sum = Reduction(
        [[weight_grad(grad_two_low, act_local)], [weight_grad(grad_two_low, act_remote)]],
        devices,
        [0] + bits[:1] + ["x"] + bits[1:],
    )
    grad_two_low, down_sum.send = boundary(grad_two_low, down_sum.send)
    down_sum.start()
    grad_pre = []
    for weight, slope in ((down_weight, slope_local), (down_remote_weight, slope_remote)):
        grad_pre.append((product(grad_two_low, weight, NT) * slope.astype(F32)).astype(BF16))
    pre_local, pre_remote, down_sum.received = boundary(*grad_pre, down_sum.received)
    down_sum.step()
    grad_normed = (
        grad_two + product(pre_local, up_weight, NT) + product(pre_remote, up_remote_weight, NT)
    )
    grad_one = norm_back(grad_normed, xhat_one, scale_one, norm1_gain)
    grad_one_low = grad_one.astype(BF16)
    sums += [eighths(grad_one), eighths(grad_normed * xhat_one), eighths(grad_normed)]
    shared = columns_of(*sums)

    def extras(pre):
        zero = jnp.zeros((8, pre.shape[1]), F32)
        sums_up = eighths(pre)
        first = columns_of(*[zero] * len(sums), sums_up).reshape(devices, 2, -1, LANES)[:, 0]
        second = columns_of(*[zero] * len(sums), zero, sums_up).reshape(devices, 2, -1, LANES)[:, 1]
        return shared + (first + second).reshape(width, LANES)

    wide_sum = Reduction(
        [
            [weight_grad(normed, pre), weight_grad(grad_one_low, context), extras(pre)]
            for pre, context in ((pre_local, context_local), (pre_remote, context_remote))
        ],
        devices,
        [0] + bits[1:] + bits[:1] + ["x"],
    )
    grad_one_low, wide_sum.send = boundary(grad_one_low, wide_sum.send)
    wide_sum.start()
    grad_one_low, wide_sum.received = boundary(grad_one_low, wide_sum.received)
    wide_sum.advance()
    grad_one_low, wide_sum.send, wide_sum.terms, down_sum.terms = boundary(
        grad_one_low, wide_sum.send, wide_sum.terms, down_sum.terms
    )
    wide_sum.start()

    def attention_back(side, base, rows_type):
        qkv, out, totals, weight = {
            "local": (qkv_local, out_weight, totals_local, qkv_local_weight),
            "remote": (qkv_remote, out_remote_weight, totals_remote, qkv_remote_weight),
        }[side]
        return attend_back(
            meta, pair_lengths, qkv, grad_one_low, out, totals, rows, weight, base, rows_type
        )

    def qv_columns(sums_qv):
        column = columns_of(sums_qv).reshape(-1, 3, LANES, LANES)
        column = [column[:, kind].reshape(devices, -1, LANES) for kind in (0, 2)]
        return jnp.concatenate(column, axis=1).reshape(width, LANES)

    rows_part, far_grad, far_sums = attention_back("remote", grad_one, F32)
    far_sum = Reduction([[far_grad, qv_columns(far_sums)]], devices, [0, "x"], meta)
    (far_sum.send,) = boundary(far_sum.send)
    far_sum.start()
    rows_part, down_sum.received, wide_sum.received, block_other = boundary(
        rows_part, down_sum.received, wide_sum.received, block_other
    )
    down_sum.advance()
    wide_sum.advance()
    rows_part, far_sum.received, down_sum.send, wide_sum.send = boundary(
        rows_part, far_sum.received, down_sum.send, wide_sum.send
    )
    wide_sum.start()
    far_sum.advance()
    rows_part, far_sum.send = boundary(rows_part, far_sum.send)
    far_sum.start()
    down_sum.start()
    grad_in, near_grad, near_sums = attention_back("local", rows_part, BF16)
    near_grad, down_sum.received, wide_sum.received = boundary(
        near_grad, down_sum.received, wide_sum.received
    )
    down_sum.step()
    wide_sum.step()
    other_in = swap_tensor(grad_in)
    near_sum = Reduction([[near_grad, qv_columns(near_sums)]], devices, [0] + bits, meta)
    near_sum.send, block_mine = boundary(near_sum.send, block_mine)
    near_sum.start()
    block_out = join(meta, 1, [block_mine], [block_other], "join_block")
    near_sum.received, far_sum.received, block_out = boundary(near_sum.received, far_sum.received, block_out)
    near_sum.terms.append(far_sum.received)
    near_sum.step()
    near_sum.send, down_sum.received = boundary(near_sum.send, down_sum.received)
    share_down = down_sum.finish().T
    near_sum.received, share_down = boundary(near_sum.received, share_down)
    near_sum.step()
    near_sum.received, wide_sum.received = boundary(near_sum.received, wide_sum.received)
    while near_sum.plan:
        near_sum.step()
    wide_sum.step()
    near_sum.send, grad_in = boundary(near_sum.send, grad_in)
    wide = wide_sum.finish()
    units = up_weight.shape[1]
    vectors = wide[:, units + local :].T
    near_terms = [term.reshape(term.shape[-2:]) for term in near_sum.terms + [near_sum.received]]
    share_qkv = spread(meta, near_terms, local)
    share_qv = total_of([term[:, 3 * local] for term in near_terms]).reshape(2, -1)
    return (
        block_out,
        join(meta, 1, [grad_in], [other_in], "join_in"),
        share_qkv,
        share_qv,
        wide[:, units : units + local].T,
        vectors[3],
        vectors[4],
        vectors[5],
        wide[:, :units],
        vectors[6:8].reshape(-1),
        share_down,
        vectors[0],
        vectors[1],
        vectors[2],
    )


def solution(mesh):
    devices = mesh.shape["dp"]
    in_specs = (
        P("dp", None),
        P("dp"),
        P("dp"),
        P(None, None, "tensor"),
        P(None, "tensor"),
        P("tensor", None),
        P(),
        P(),
        P(),
        P(None, "tensor"),
        P("tensor"),
        P("tensor", None),
        P(),
        P(),
        P(),
        P("dp", None),
    )
    out_specs = (
        P("dp", None),
        P("dp", None),
        P(None, "dp", "tensor"),
        P(None, ("tensor", "dp")),
        P("tensor", "dp"),
        P("dp"),
        P("dp"),
        P("dp"),
        P("dp", "tensor"),
        P(("tensor", "dp")),
        P("tensor", "dp"),
        P("dp"),
        P("dp"),
        P("dp"),
    )
    return jax.shard_map(
        functools.partial(body, devices=devices),
        mesh=mesh,
        in_specs=in_specs,
        out_specs=out_specs,
        check_vma=False,
    )
```

```python
import functools

import jax
import jax.numpy as jnp
from jax import lax
from jax.experimental import pallas as pl
from jax.experimental.pallas import tpu as pltpu
from jax.sharding import PartitionSpec as P

HEAD_DIM = 64
LANES = 128
VMEM_BYTES = 60 * 1024 * 1024
NORM_EPSILON = 1e-12
HALF_ROOT = 0.7071067811865476
INVERSE_ROOT_TWO_PI = 0.3989422804014327
SCORE_SCALE = HEAD_DIM ** (-0.5)
NT = (((1,), (1,)), ((), ()))
NN = (((1,), (0,)), ((), ()))
TN = (((0,), (0,)), ((), ()))
F32 = jnp.float32
BF16 = jnp.bfloat16


def product(left, right, dims):
    return lax.dot_general(left, right, dims, preferred_element_type=F32)


def head_halves(block):
    lane = lax.broadcasted_iota(jnp.int32, (1, LANES), 1)
    zero = jnp.zeros_like(block)
    return jnp.where(lane < HEAD_DIM, block, zero), jnp.where(lane < HEAD_DIM, zero, block)


def call(kernel, name, meta, grid, inputs, outputs, flops, moved, exps=0, scratch=()):
    return pl.pallas_call(
        kernel,
        out_shape=[jax.ShapeDtypeStruct(shape, dtype) for shape, dtype, spec in outputs],
        grid_spec=pltpu.PrefetchScalarGridSpec(
            num_scalar_prefetch=1,
            grid=grid,
            in_specs=[spec for array, spec in inputs],
            out_specs=[spec for shape, dtype, spec in outputs],
            scratch_shapes=list(scratch),
        ),
        cost_estimate=pl.CostEstimate(flops=0, bytes_accessed=1024, transcendentals=0),
        name=name,
    )(meta, *[array for array, spec in inputs])


def attend_kernel(meta_ref, length_ref, rows_ref, weight_ref, bias_ref, qkv_ref, context_ref, total_ref):
    length = length_ref[meta_ref[1] * pl.num_programs(0) + pl.program_id(0)]
    qkv = (product(rows_ref[...], weight_ref[...], NN) + bias_ref[...]).astype(BF16)
    qkv_ref[...] = qkv
    keys = qkv[:, LANES : 2 * LANES] * SCORE_SCALE
    valid = lax.broadcasted_iota(jnp.int32, (keys.shape[0], 1), 0) < length
    heads = zip(head_halves(qkv[:, :LANES]), head_halves(qkv[:, 2 * LANES :]))
    flipped = None
    for head, (query, value) in enumerate(heads):
        scores = jnp.where(valid, product(keys, query, NT), -1000000000.0)
        peak = jnp.max(scores, axis=0, keepdims=True)
        exponent = jnp.exp(scores - peak)
        total = jnp.sum(exponent, axis=0, keepdims=True)
        probs_low = (exponent * (1.0 / total)).astype(BF16)
        part = product(value, probs_low, TN)
        flipped = part if flipped is None else flipped + part
        total_ref[0, 0, head : head + 1, :] = peak + jnp.log(total)
    context_ref[...] = flipped.T.astype(BF16)


def attend(meta, lengths, rows, weight, bias, pairs):
    row_count, width = rows.shape
    columns = weight.shape[1]
    span, blocks = row_count // pairs, columns // (3 * LANES)
    work = row_count * span * blocks * LANES
    by_block = lambda pair, lanes, meta: (pair, lanes)
    return call(
        attend_kernel,
        "attend",
        meta,
        (pairs, blocks),
        [
            (lengths, pl.BlockSpec(memory_space=pltpu.SMEM)),
            (rows, pl.BlockSpec((span, width), lambda pair, lanes, meta: (pair, 0))),
            (weight, pl.BlockSpec((width, 3 * LANES), lambda pair, lanes, meta: (0, lanes))),
            (bias, pl.BlockSpec((1, 3 * LANES), lambda pair, lanes, meta: (0, lanes))),
        ],
        [
            ((row_count, columns), BF16, pl.BlockSpec((span, 3 * LANES), by_block)),
            ((row_count, blocks * LANES), BF16, pl.BlockSpec((span, LANES), by_block)),
            (
                (pairs, blocks, 2, span),
                F32,
                pl.BlockSpec((1, 1, 2, span), lambda pair, lanes, meta: (pair, lanes, 0, 0)),
            ),
        ],
        flops=16 * work,
        moved=8 * row_count * blocks * LANES,
        exps=work // HEAD_DIM,
    )


def attend_back_kernel(
    meta_ref,
    length_ref,
    qkv_ref,
    low_ref,
    out_ref,
    total_ref,
    rows_ref,
    weight_ref,
    base_ref,
    rows_grad_ref,
    weight_grad_ref,
    sums_ref,
    rows_sum,
    weight_sum,
):
    step, lanes = pl.program_id(0), pl.program_id(1)
    length = length_ref[meta_ref[1] * pl.num_programs(0) + step]
    keys = qkv_ref[:, LANES : 2 * LANES] * SCORE_SCALE
    values = qkv_ref[:, 2 * LANES :]
    valid = lax.broadcasted_iota(jnp.int32, (keys.shape[0], 1), 0) < length
    context_grad = product(low_ref[...], out_ref[...], NT).astype(BF16)
    heads = zip(head_halves(qkv_ref[:, :LANES]), head_halves(keys), head_halves(context_grad))
    sums = [None, None, None]
    for head, (query, key, grad) in enumerate(heads):
        scores = jnp.where(valid, product(keys, query, NT), -1000000000.0)
        probs = jnp.exp(scores - total_ref[0, 0, head : head + 1, :])
        grad_probs = product(values, grad, NT)
        weighted = probs * grad_probs
        inner = jnp.sum(weighted, axis=0, keepdims=True)
        grad_scores = (weighted - probs * inner).astype(BF16)
        parts = (
            product(grad_scores, key, TN),
            product(grad_scores, query, NN),
            product(probs.astype(BF16), grad, NN),
        )
        sums = [b if a is None else a + b for a, b in zip(sums, parts)]
    grads = [sums[0].astype(BF16), (sums[1] * SCORE_SCALE).astype(BF16), sums[2].astype(BF16)]
    grads = jnp.concatenate(grads, axis=1)
    rows_part = product(grads, weight_ref[...], NT)
    weight_part = product(rows_ref[...], grads, TN)
    columns = pl.ds(pl.multiple_of(lanes * 3 * LANES, LANES), 3 * LANES)
    column_sums = jnp.sum(grads.astype(F32).reshape(-1, 8, 3 * LANES), axis=0)

    @pl.when(lanes == 0)
    def _():
        rows_sum[...] = base_ref[...] + rows_part

    @pl.when(lanes > 0)
    def _():
        rows_sum[...] += rows_part

    @pl.when(lanes == pl.num_programs(1) - 1)
    def _():
        rows_grad_ref[...] = rows_sum[...].astype(rows_grad_ref.dtype)

    @pl.when(step == 0)
    def _():
        weight_sum[:, columns] = weight_part
        sums_ref[:, columns] = column_sums

    @pl.when(step > 0)
    def _():
        weight_sum[:, columns] += weight_part
        sums_ref[:, columns] += column_sums

    @pl.when(step == pl.num_programs(0) - 1)
    def _():
        weight_grad_ref[:, columns] = weight_sum[:, columns].astype(weight_grad_ref.dtype)


def attend_back(meta, lengths, qkv, low_grad, out, totals, rows, weight, base, rows_type):
    pairs = totals.shape[0]
    width, columns = weight.shape
    span, blocks = rows.shape[0] // pairs, columns // (3 * LANES)
    by_pair = lambda pair, lanes, meta: (pair, 0)
    whole = lambda pair, lanes, meta: (0, 0)
    inputs = [
        (lengths, pl.BlockSpec(memory_space=pltpu.SMEM)),
        (qkv, pl.BlockSpec((span, 3 * LANES), lambda pair, lanes, meta: (pair, lanes))),
        (low_grad, pl.BlockSpec((span, width), by_pair)),
        (out, pl.BlockSpec((LANES, width), lambda pair, lanes, meta: (lanes, 0))),
        (totals, pl.BlockSpec((1, 1, 2, span), lambda pair, lanes, meta: (pair, lanes, 0, 0))),
        (rows, pl.BlockSpec((span, width), by_pair)),
        (weight, pl.BlockSpec((width, 3 * LANES), lambda pair, lanes, meta: (0, lanes))),
        (base, pl.BlockSpec((span, width), by_pair)),
    ]
    return call(
        attend_back_kernel,
        "attend_back",
        meta,
        (pairs, blocks),
        inputs,
        [
            (rows.shape, rows_type, pl.BlockSpec((span, width), by_pair)),
            ((width, columns), BF16, pl.BlockSpec((width, columns), whole)),
            ((8, columns), F32, pl.BlockSpec((8, columns), whole)),
        ],
        flops=0,
        moved=1024,
        scratch=[pltpu.VMEM((span, width), F32), pltpu.VMEM((width, columns), F32)],
    )


def move_kernel(moves, source_count, target_count, meta_ref, *refs):
    sources = refs[:source_count]
    targets = refs[source_count : source_count + target_count]
    rest = refs[source_count + target_count :]
    buffers, arrived, left = rest[: len(moves)], rest[-2], rest[-1]
    incoming, outgoing = [], []
    for number, (source, row, column, target, to_row, to_column, rows, columns) in enumerate(moves):
        into = sources[source].at[pl.ds(row(meta_ref), rows), pl.ds(column, columns)]
        onto = targets[target].at[pl.ds(to_row(meta_ref), rows), pl.ds(to_column, columns)]
        incoming.append(pltpu.make_async_copy(into, buffers[number], arrived.at[number]))
        outgoing.append(pltpu.make_async_copy(buffers[number], onto, left.at[number]))
    for copy in incoming:
        copy.start()
    for copy_in, copy_out in zip(incoming, outgoing):
        copy_in.wait()
        copy_out.start()
    for copy in outgoing:
        copy.wait()


def pieces(entry):
    source, row, column, target, to_row, to_column, rows, columns = entry
    count = next((n for n in (4, 2) if rows % (16 * n) == 0 and rows * columns >= n * 2**16), 1)
    step = rows // count
    return [
        (
            source,
            functools.partial(lambda meta_ref, base, at: pl.multiple_of(base(meta_ref) + at, 16), base=row, at=i * step)
            if rows % 16 == 0
            else row,
            column,
            target,
            functools.partial(
                lambda meta_ref, base, at: pl.multiple_of(base(meta_ref) + at, 16), base=to_row, at=i * step
            )
            if rows % 16 == 0
            else to_row,
            to_column,
            step,
            columns,
        )
        for i in range(count)
    ]


def move(name, meta, sources, targets, moves):
    moves = [part for entry in moves for part in pieces(entry)]
    return call(
        functools.partial(move_kernel, moves, len(sources), len(targets)),
        name,
        meta,
        (1,),
        [(source, pl.BlockSpec(memory_space=pl.ANY)) for source in sources],
        [(shape, BF16, pl.BlockSpec(memory_space=pl.ANY)) for shape in targets],
        flops=0,
        moved=4 * sum(entry[6] * entry[7] for entry in moves),
        scratch=[pltpu.VMEM(entry[6:], BF16) for entry in moves]
        + [pltpu.SemaphoreType.DMA((len(moves),))] * 2,
    )


def fixed(row):
    return lambda meta_ref: row


def by_place(entry, rows, other=False, offset=0):
    def start(meta_ref):
        place = 1 - meta_ref[entry] if other else meta_ref[entry]
        return pl.multiple_of(place * rows + offset, 16)

    return start


def pack_qkv_kernel(blocks, meta_ref, weight_ref, whole_ref, quarter_ref, buffer, arrived, left):
    copies = []
    for kind in range(3):
        for block in range(blocks):
            number = 3 * block + kind
            copies.append(
                pltpu.make_async_copy(
                    weight_ref.at[kind, :, pl.ds(block * LANES, LANES)],
                    buffer.at[:, pl.ds(number * LANES, LANES)],
                    arrived.at[number],
                )
            )
    for copy in copies:
        copy.start()
    for copy in copies:
        copy.wait()
    quarter = quarter_ref.shape[0]
    mine = pl.ds(pl.multiple_of((2 * meta_ref[0] + meta_ref[2]) * quarter, 16), quarter)
    out = [
        pltpu.make_async_copy(buffer.at[mine], quarter_ref, left.at[0]),
        pltpu.make_async_copy(buffer, whole_ref, left.at[1]),
    ]
    for copy in out:
        copy.start()
    for copy in out:
        copy.wait()


def pack_qkv(meta, weight):
    kinds, rows, columns = weight.shape
    shapes = [(rows, kinds * columns), (rows // 4, kinds * columns)]
    return call(
        functools.partial(pack_qkv_kernel, columns // LANES),
        "pack_qkv",
        meta,
        (1,),
        [(weight, pl.BlockSpec(memory_space=pl.ANY))],
        [(shape, BF16, pl.BlockSpec(memory_space=pl.ANY)) for shape in shapes],
        flops=0,
        moved=5 * weight.size,
        scratch=[
            pltpu.VMEM(shapes[0], BF16),
            pltpu.SemaphoreType.DMA((kinds * columns // LANES,)),
            pltpu.SemaphoreType.DMA((2,)),
        ],
    )


def pack(meta, out_weight, up_weight, down_weight):
    out, up, down = [weight.shape[0] // 2 for weight in (out_weight, up_weight, down_weight)]
    width, units = out_weight.shape[1], up_weight.shape[1]
    fold = units // width
    part = out // fold
    moves = [(1, by_place(0, up), 0, 0, fixed(0), 0, up, units)]
    for i in range(fold):
        moves.append((0, by_place(0, out, offset=i * part), 0, 0, fixed(up), i * width, part, width))
    moves.append((2, by_place(0, down), 0, 1, fixed(0), 0, down, width))
    return move(
        "pack",
        meta,
        [out_weight, up_weight, down_weight],
        [(up + part, units), (down, width)],
        moves,
    )


def unpack(meta, mine, other, out_shape, up_shape):
    out, up = out_shape[0] // 2, up_shape[0] // 2
    width, units = out_shape[1], up_shape[1]
    fold = units // width
    part = out // fold
    moves = []
    for source in (0, 1):
        for i in range(fold):
            onto = by_place(0, out, other=bool(source), offset=i * part)
            moves.append((source, fixed(up), i * width, 0, onto, 0, part, width))
    for source in (0, 1):
        moves.append((source, fixed(0), 0, 1, by_place(0, up, other=bool(source)), 0, up, units))
    return move("unpack", meta, [mine, other], [out_shape, up_shape], moves)


def join(meta, entry, mine, other, name):
    rows, columns = mine[0].shape
    count = len(mine)
    moves = []
    for own in (0, 1):
        for i in range(count):
            onto = by_place(entry, rows * count, other=bool(own), offset=i * rows)
            moves.append((own * count + i, fixed(0), 0, 0, onto, 0, rows, columns))
    return move(name, meta, [*mine, *other], [(2 * count * rows, columns)], moves)[0]


def join_quarters(meta, mine, other):
    half, columns = mine.shape
    quarter = half // 2
    moves = []
    for source in (0, 1):
        for part in (0, 1):

            def onto(meta_ref, source=source, part=part):
                core = 1 - meta_ref[0] if source else meta_ref[0]
                chip = 1 - meta_ref[2] if part else meta_ref[2]
                return pl.multiple_of((2 * core + chip) * quarter, 16)

            moves.append((source, fixed(part * quarter), 0, 0, onto, 0, quarter, columns))
    return move("join_qkv", meta, [mine, other], [(2 * half, columns)], moves)[0]


def normalized(rows):
    row_mean = jnp.mean(rows, axis=-1, keepdims=True)
    centered = rows - row_mean
    variance = jnp.mean(centered * centered, axis=-1, keepdims=True)
    scale = lax.rsqrt(variance + NORM_EPSILON)
    return centered * scale, scale


def norm_back(grad, xhat, scale, gain):
    inner = grad * gain
    mean = jnp.mean(inner, axis=-1, keepdims=True)
    along = jnp.mean(inner * xhat, axis=-1, keepdims=True)
    return scale * (inner - mean - xhat * along)


def low(value):
    return value.astype(BF16).astype(F32)


def gelu_pair(value):
    cdf = 0.5 + 0.5 * lax.erf(value * HALF_ROOT)
    slope = cdf + value * (jnp.exp(-0.5 * value * value) * INVERSE_ROOT_TWO_PI)
    return (value * cdf).astype(BF16), slope.astype(BF16)


def by_lane_pair(weight):
    count, rows, columns = weight.shape
    return weight.reshape(count, rows, -1, LANES).transpose(1, 2, 0, 3).reshape(rows, -1)


def swap_tensor(block):
    return lax.ppermute(block, "tensor", [(0, 1), (1, 0)])


def swap_dp(block, devices, stride):
    return lax.ppermute(block, "dp", [(place, place ^ stride) for place in range(devices)])


def boundary(*values):
    return lax.optimization_barrier(values)


def eighths(rows):
    return jnp.sum(rows.astype(F32).reshape(-1, 8, rows.shape[1]), axis=0)


def columns_of(*sums):
    stacked = jnp.concatenate(sums) if len(sums) > 1 else sums[0]
    owner = lax.broadcasted_iota(jnp.int32, (stacked.shape[0], LANES), 0) // 8
    lane = lax.broadcasted_iota(jnp.int32, (stacked.shape[0], LANES), 1)
    return product(stacked.astype(BF16), (owner == lane).astype(BF16), TN)


def halve_kernel(sides, meta_ref, *refs):
    send_ref, keep_ref = refs[-2:]
    core = meta_ref[0]
    number = 0
    for side, parts in enumerate(sides):
        column = 0
        for width in parts:
            first, second = refs[number][:, 0], refs[number][:, 1]
            columns = slice(column, column + width)
            send_ref[side, :, :, columns] = jnp.where(core == 0, second, first)
            keep_ref[side, :, :, columns] = jnp.where(core == 0, first, second)
            number, column = number + 1, column + width


def halve(meta, sides, devices):
    parts = [part.astype(BF16) for side in sides for part in side]
    rows = parts[0].shape[0] // devices
    widths = [[part.shape[1] for part in side] for side in sides]
    shape = (len(sides), devices // 2, rows, sum(widths[0]))
    step = devices // 4
    out_spec = pl.BlockSpec((len(sides), step) + shape[2:], lambda place, meta: (0, place, 0, 0))
    return call(
        functools.partial(halve_kernel, widths),
        "halve",
        meta,
        (2,),
        [
            (
                part.reshape(devices // 2, 2, rows, part.shape[1]),
                pl.BlockSpec((step, 2, rows, part.shape[1]), lambda place, meta: (place, 0, 0, 0)),
            )
            for part in parts
        ],
        [(shape, BF16, out_spec)] * 2,
        flops=0,
        moved=1024,
    )


def total_of(terms):
    total = terms[0].astype(F32)
    for term in terms[1:]:
        total = total + term.astype(F32)
    return total


def spread_kernel(meta_ref, *refs):
    out_ref = refs[-1]
    total = sum(ref[...].astype(F32) for ref in refs[:-1])
    for block in range(total.shape[1] // (3 * LANES)):
        for kind in range(3):
            start = (3 * block + kind) * LANES
            out_ref[kind, :, block * LANES : (block + 1) * LANES] = total[:, start : start + LANES]


def spread(meta, terms, columns):
    rows = terms[0].shape[0]
    spec = pl.BlockSpec((rows, 3 * columns), lambda i, meta: (0, 0))
    shape = (3, rows, columns)
    return call(
        spread_kernel,
        "spread",
        meta,
        (1,),
        [(term, spec) for term in terms],
        [(shape, F32, pl.BlockSpec(shape, lambda i, meta: (0, 0, 0)))],
        flops=0,
        moved=1024,
    )[0]


class Reduction:
    def __init__(self, sides, devices, plan, meta=None):
        self.devices = devices
        self.plan = list(plan)
        self.left = list(range(devices.bit_length() - 2, -1, -1))
        self.sides = len(sides)
        if meta is not None:
            self.stage = self.plan.pop(0)
            self.left.remove(self.stage)
            self.send, kept = halve(meta, sides, devices)
            self.terms = [kept]
            return
        cut, here = self.halving(self.plan.pop(0))

        def pick(index):
            picked = []
            for parts in sides:
                beside = [
                    self.half(part.astype(BF16).reshape(1, devices, -1, part.shape[1]), cut, index)
                    for part in parts
                ]
                picked.append(jnp.concatenate(beside, axis=-1))
            return jnp.concatenate(picked) if len(picked) > 1 else picked[0]

        self.send, self.terms = pick(1 - here), [pick(here)]

    def halving(self, stage):
        self.stage = stage
        where = self.left.index(stage)
        self.left.remove(stage)
        return 2**where, lax.axis_index("dp") // 2**stage % 2

    def half(self, term, before, index):
        sides, places, rows, columns = term.shape
        cut = term.reshape(sides * before, 2, places // before // 2, rows, columns)
        kept = lax.dynamic_index_in_dim(cut, index, 1, keepdims=False)
        return kept.reshape(sides, places // 2, rows, columns)

    def start(self):
        if self.stage == "x":
            self.received = swap_tensor(self.send)
        else:
            self.received = swap_dp(self.send, self.devices, 2**self.stage)

    def step(self):
        self.advance()
        self.start()

    def advance(self):
        self.terms.append(self.received)
        terms, stage = self.terms, self.plan.pop(0)
        if terms[0].shape[1] == self.devices // 2:
            terms = [total_of(terms)]
        if stage == "x":
            self.stage = stage
            self.send = total_of([term[-1:] for term in terms]).astype(BF16)
            self.terms = [total_of([term[:-1] for term in terms])] if self.sides > 1 else []
            self.sides = 1
        else:
            cut, here = self.halving(stage)
            self.send = total_of([self.half(term, cut, 1 - here) for term in terms]).astype(BF16)
            self.terms = [total_of([self.half(term, cut, here) for term in terms])]

    def finish(self):
        while self.plan:
            self.step()
        self.terms.append(self.received)
        return total_of([term.reshape(term.shape[-2:]) for term in self.terms])


def body(
    hidden_in,
    pair_lengths,
    candidates,
    qkv_weight,
    qv_bias,
    out_weight,
    out_bias,
    norm1_gain,
    norm1_shift,
    up_weight,
    up_bias,
    down_weight,
    down_bias,
    norm2_gain,
    norm2_shift,
    out_cotangent,
    *,
    devices,
):
    pairs = pair_lengths.shape[0] // 2
    width = hidden_in.shape[1]
    local = qv_bias.shape[1]
    row_count = hidden_in.shape[0] // 2
    span = row_count // pairs
    place, tensor = lax.axis_index("dp"), lax.axis_index("tensor")
    meta = jnp.stack([place % 2, tensor, place // 2 % 2]).astype(jnp.int32)
    bits = list(range(1, devices.bit_length() - 1))

    def own(array, size):
        return lax.dynamic_slice_in_dim(array, tensor * size, size, 0)

    qkv_local_weight, qkv_piece = pack_qkv(meta, qkv_weight)
    qkv_mine = swap_tensor(qkv_piece)
    biases_other = swap_tensor(jnp.concatenate([qv_bias.reshape(-1), up_bias]))
    out_up_piece, down_piece = pack(meta, out_weight, up_weight, down_weight)
    out_up_mine = swap_tensor(out_up_piece)
    rows = own(hidden_in, row_count)

    def qkv_bias(bias):
        return by_lane_pair(jnp.stack([bias[0], jnp.zeros_like(bias[0]), bias[1]]).reshape(3, 1, local))

    bias_local = qkv_bias(qv_bias)
    rows, bias_local, qkv_local_weight, out_up_piece, down_piece, qkv_mine, biases_other = boundary(
        rows, bias_local, qkv_local_weight, out_up_piece, down_piece, qkv_mine, biases_other
    )
    qkv_next = swap_dp(qkv_mine, devices, 2)
    qkv_local, context_local, totals_local = attend(
        meta, pair_lengths, rows, qkv_local_weight, bias_local, pairs
    )
    context_local, qkv_next = boundary(context_local, qkv_next)
    qkv_half = jnp.concatenate([qkv_mine, qkv_next])
    qkv_remote_weight = join_quarters(meta, qkv_half, swap_dp(qkv_half, devices, 1))
    remote_bias = biases_other[: 2 * local].reshape(2, local)
    qkv_remote, context_remote, totals_remote = attend(
        meta, pair_lengths, rows, qkv_remote_weight, qkv_bias(remote_bias), pairs
    )
    context_local, context_remote, out_up_mine = boundary(context_local, context_remote, out_up_mine)
    down_mine = swap_tensor(down_piece)
    out_up_other = swap_dp(out_up_mine, devices, 1)
    part_local = product(context_local, out_weight, NN).astype(BF16)
    out_up_mine, out_up_other, part_local = boundary(out_up_mine, out_up_other, part_local)
    out_remote_weight, up_remote_weight = unpack(
        meta, out_up_mine, out_up_other, out_weight.shape, up_weight.shape
    )
    part_remote = low(product(context_remote, out_remote_weight, NN))
    residual = rows.astype(F32) + (part_local.astype(F32) + part_remote) + out_bias
    xhat_one, scale_one = normalized(residual)
    normed_one = xhat_one * norm1_gain + norm1_shift
    normed = normed_one.astype(BF16)

    def expand(weight, bias):
        return boundary(*gelu_pair(product(normed, weight, NN) + bias))

    act_local, slope_local = expand(up_weight, up_bias)
    ff_local = product(act_local, down_weight, NN).astype(BF16)
    act_remote, slope_remote = expand(up_remote_weight, biases_other[2 * local :])
    act_remote, down_mine, ff_local = boundary(act_remote, down_mine, ff_local)
    down_other = swap_dp(down_mine, devices, 1)
    down_remote_weight = join(meta, 0, [down_mine], [down_other], "join_down")
    ff_remote = low(product(act_remote, down_remote_weight, NN))
    xhat, scale = normalized(normed_one + (ff_local.astype(F32) + ff_remote) + down_bias)
    block_mine = (xhat * norm2_gain + norm2_shift).astype(BF16)

    counts = own(candidates, pairs).astype(F32)[:, None, None]
    grad_output = own(out_cotangent, row_count).astype(F32).reshape(pairs, span, width) / counts
    grad_output = grad_output.reshape(row_count, width)
    grad_two = norm_back(grad_output, xhat, scale, norm2_gain)
    grad_two_low = grad_two.astype(BF16)
    sums = [eighths(grad_two), eighths(grad_output * xhat), eighths(grad_output)]
    grad_two_low, block_mine = boundary(grad_two_low, block_mine)
    block_other = swap_tensor(block_mine)

    def weight_grad(left, right):
        return product(left, right, TN).astype(BF16)

    down_sum = Reduction(
        [[weight_grad(grad_two_low, act_local)], [weight_grad(grad_two_low, act_remote)]],
        devices,
        [0] + bits[:1] + ["x"] + bits[1:],
    )
    grad_two_low, down_sum.send = boundary(grad_two_low, down_sum.send)
    down_sum.start()
    grad_pre = []
    for weight, slope in ((down_weight, slope_local), (down_remote_weight, slope_remote)):
        grad_pre.append((product(grad_two_low, weight, NT) * slope.astype(F32)).astype(BF16))
    pre_local, pre_remote, down_sum.received = boundary(*grad_pre, down_sum.received)
    down_sum.step()
    grad_normed = (
        grad_two + product(pre_local, up_weight, NT) + product(pre_remote, up_remote_weight, NT)
    )
    grad_one = norm_back(grad_normed, xhat_one, scale_one, norm1_gain)
    grad_one_low = grad_one.astype(BF16)
    sums += [eighths(grad_one), eighths(grad_normed * xhat_one), eighths(grad_normed)]
    shared = columns_of(*sums)

    def extras(pre):
        zero = jnp.zeros((8, pre.shape[1]), F32)
        sums_up = eighths(pre)
        first = columns_of(*[zero] * len(sums), sums_up).reshape(devices, 2, -1, LANES)[:, 0]
        second = columns_of(*[zero] * len(sums), zero, sums_up).reshape(devices, 2, -1, LANES)[:, 1]
        return shared + (first + second).reshape(width, LANES)

    wide_sum = Reduction(
        [
            [weight_grad(normed, pre), weight_grad(grad_one_low, context), extras(pre)]
            for pre, context in ((pre_local, context_local), (pre_remote, context_remote))
        ],
        devices,
        [0] + bits[1:] + bits[:1] + ["x"],
    )
    grad_one_low, wide_sum.send = boundary(grad_one_low, wide_sum.send)
    wide_sum.start()
    grad_one_low, wide_sum.received = boundary(grad_one_low, wide_sum.received)
    wide_sum.advance()
    grad_one_low, wide_sum.send, wide_sum.terms, down_sum.terms = boundary(
        grad_one_low, wide_sum.send, wide_sum.terms, down_sum.terms
    )
    wide_sum.start()

    def attention_back(side, base, rows_type):
        qkv, out, totals, weight = {
            "local": (qkv_local, out_weight, totals_local, qkv_local_weight),
            "remote": (qkv_remote, out_remote_weight, totals_remote, qkv_remote_weight),
        }[side]
        return attend_back(
            meta, pair_lengths, qkv, grad_one_low, out, totals, rows, weight, base, rows_type
        )

    def qv_columns(sums_qv):
        column = columns_of(sums_qv).reshape(-1, 3, LANES, LANES)
        column = [column[:, kind].reshape(devices, -1, LANES) for kind in (0, 2)]
        return jnp.concatenate(column, axis=1).reshape(width, LANES)

    rows_part, far_grad, far_sums = attention_back("remote", grad_one, F32)
    far_sum = Reduction([[far_grad, qv_columns(far_sums)]], devices, [0, "x"], meta)
    (far_sum.send,) = boundary(far_sum.send)
    far_sum.start()
    rows_part, down_sum.received, wide_sum.received, block_other = boundary(
        rows_part, down_sum.received, wide_sum.received, block_other
    )
    down_sum.advance()
    wide_sum.advance()
    rows_part, far_sum.received, down_sum.send, wide_sum.send = boundary(
        rows_part, far_sum.received, down_sum.send, wide_sum.send
    )
    wide_sum.start()
    far_sum.advance()
    rows_part, far_sum.send = boundary(rows_part, far_sum.send)
    far_sum.start()
    down_sum.start()
    grad_in, near_grad, near_sums = attention_back("local", rows_part, BF16)
    near_grad, down_sum.received, wide_sum.received = boundary(
        near_grad, down_sum.received, wide_sum.received
    )
    down_sum.step()
    other_in = swap_tensor(grad_in)
    near_sum = Reduction([[near_grad, qv_columns(near_sums)]], devices, [0] + bits, meta)
    near_sum.send, block_mine = boundary(near_sum.send, block_mine)
    near_sum.start()
    block_out = join(meta, 1, [block_mine], [block_other], "join_block")
    near_sum.received, far_sum.received, block_out = boundary(near_sum.received, far_sum.received, block_out)
    near_sum.terms.append(far_sum.received)
    near_sum.step()
    near_sum.send, wide_sum.received, down_sum.received = boundary(
        near_sum.send, wide_sum.received, down_sum.received
    )
    wide_sum.step()
    down_sum.step()
    near_sum.received, wide_sum.send, down_sum.send = boundary(
        near_sum.received, wide_sum.send, down_sum.send
    )
    near_sum.step()
    near_sum.received, wide_sum.received = boundary(near_sum.received, wide_sum.received)
    while near_sum.plan:
        near_sum.step()
    wide_sum.step()
    near_sum.send, grad_in, down_sum.received = boundary(near_sum.send, grad_in, down_sum.received)
    share_down = down_sum.finish().T
    wide = wide_sum.finish()
    units = up_weight.shape[1]
    vectors = wide[:, units + local :].T
    near_terms = [term.reshape(term.shape[-2:]) for term in near_sum.terms + [near_sum.received]]
    share_qkv = spread(meta, near_terms, local)
    share_qv = total_of([term[:, 3 * local] for term in near_terms]).reshape(2, -1)
    return (
        block_out,
        join(meta, 1, [grad_in], [other_in], "join_in"),
        share_qkv,
        share_qv,
        wide[:, units : units + local].T,
        vectors[3],
        vectors[4],
        vectors[5],
        wide[:, :units],
        vectors[6:8].reshape(-1),
        share_down,
        vectors[0],
        vectors[1],
        vectors[2],
    )


def solution(mesh):
    devices = mesh.shape["dp"]
    in_specs = (
        P("dp", None),
        P("dp"),
        P("dp"),
        P(None, None, "tensor"),
        P(None, "tensor"),
        P("tensor", None),
        P(),
        P(),
        P(),
        P(None, "tensor"),
        P("tensor"),
        P("tensor", None),
        P(),
        P(),
        P(),
        P("dp", None),
    )
    out_specs = (
        P("dp", None),
        P("dp", None),
        P(None, "dp", "tensor"),
        P(None, ("tensor", "dp")),
        P("tensor", "dp"),
        P("dp"),
        P("dp"),
        P("dp"),
        P("dp", "tensor"),
        P(("tensor", "dp")),
        P("tensor", "dp"),
        P("dp"),
        P("dp"),
        P("dp"),
    )
    return jax.shard_map(
        functools.partial(body, devices=devices),
        mesh=mesh,
        in_specs=in_specs,
        out_specs=out_specs,
        check_vma=False,
    )
```

```python
import functools

import jax
import jax.numpy as jnp
from jax import lax
from jax.experimental import pallas as pl
from jax.experimental.pallas import tpu as pltpu
from jax.sharding import PartitionSpec as P

HEAD_DIM = 64
LANES = 128
VMEM_BYTES = 60 * 1024 * 1024
NORM_EPSILON = 1e-12
HALF_ROOT = 0.7071067811865476
INVERSE_ROOT_TWO_PI = 0.3989422804014327
SCORE_SCALE = HEAD_DIM ** (-0.5)
NT = (((1,), (1,)), ((), ()))
NN = (((1,), (0,)), ((), ()))
TN = (((0,), (0,)), ((), ()))
F32 = jnp.float32
BF16 = jnp.bfloat16


def product(left, right, dims):
    return lax.dot_general(left, right, dims, preferred_element_type=F32)


def head_halves(block):
    lane = lax.broadcasted_iota(jnp.int32, (1, LANES), 1)
    zero = jnp.zeros_like(block)
    return jnp.where(lane < HEAD_DIM, block, zero), jnp.where(lane < HEAD_DIM, zero, block)


def call(kernel, name, meta, grid, inputs, outputs, flops, moved, exps=0, scratch=()):
    return pl.pallas_call(
        kernel,
        out_shape=[jax.ShapeDtypeStruct(shape, dtype) for shape, dtype, spec in outputs],
        grid_spec=pltpu.PrefetchScalarGridSpec(
            num_scalar_prefetch=1,
            grid=grid,
            in_specs=[spec for array, spec in inputs],
            out_specs=[spec for shape, dtype, spec in outputs],
            scratch_shapes=list(scratch),
        ),
        cost_estimate=pl.CostEstimate(flops=0, bytes_accessed=1024, transcendentals=0),
        name=name,
    )(meta, *[array for array, spec in inputs])


def attend_kernel(meta_ref, length_ref, rows_ref, weight_ref, bias_ref, qkv_ref, context_ref, total_ref):
    length = length_ref[meta_ref[1] * pl.num_programs(0) + pl.program_id(0)]
    qkv = (product(rows_ref[...], weight_ref[...], NN) + bias_ref[...]).astype(BF16)
    qkv_ref[...] = qkv
    keys = qkv[:, LANES : 2 * LANES] * SCORE_SCALE
    valid = lax.broadcasted_iota(jnp.int32, (keys.shape[0], 1), 0) < length
    heads = zip(head_halves(qkv[:, :LANES]), head_halves(qkv[:, 2 * LANES :]))
    flipped = None
    for head, (query, value) in enumerate(heads):
        scores = jnp.where(valid, product(keys, query, NT), -1000000000.0)
        peak = jnp.max(scores, axis=0, keepdims=True)
        exponent = jnp.exp(scores - peak)
        total = jnp.sum(exponent, axis=0, keepdims=True)
        probs_low = (exponent * (1.0 / total)).astype(BF16)
        part = product(value, probs_low, TN)
        flipped = part if flipped is None else flipped + part
        total_ref[0, 0, head : head + 1, :] = peak + jnp.log(total)
    context_ref[...] = flipped.T.astype(BF16)


def attend(meta, lengths, rows, weight, bias, pairs):
    row_count, width = rows.shape
    columns = weight.shape[1]
    span, blocks = row_count // pairs, columns // (3 * LANES)
    work = row_count * span * blocks * LANES
    by_block = lambda pair, lanes, meta: (pair, lanes)
    return call(
        attend_kernel,
        "attend",
        meta,
        (pairs, blocks),
        [
            (lengths, pl.BlockSpec(memory_space=pltpu.SMEM)),
            (rows, pl.BlockSpec((span, width), lambda pair, lanes, meta: (pair, 0))),
            (weight, pl.BlockSpec((width, 3 * LANES), lambda pair, lanes, meta: (0, lanes))),
            (bias, pl.BlockSpec((1, 3 * LANES), lambda pair, lanes, meta: (0, lanes))),
        ],
        [
            ((row_count, columns), BF16, pl.BlockSpec((span, 3 * LANES), by_block)),
            ((row_count, blocks * LANES), BF16, pl.BlockSpec((span, LANES), by_block)),
            (
                (pairs, blocks, 2, span),
                F32,
                pl.BlockSpec((1, 1, 2, span), lambda pair, lanes, meta: (pair, lanes, 0, 0)),
            ),
        ],
        flops=16 * work,
        moved=8 * row_count * blocks * LANES,
        exps=work // HEAD_DIM,
    )


def attend_back_kernel(
    meta_ref,
    length_ref,
    qkv_ref,
    low_ref,
    out_ref,
    total_ref,
    rows_ref,
    weight_ref,
    base_ref,
    rows_grad_ref,
    weight_grad_ref,
    sums_ref,
    rows_sum,
    weight_sum,
):
    step, lanes = pl.program_id(0), pl.program_id(1)
    length = length_ref[meta_ref[1] * pl.num_programs(0) + step]
    keys = qkv_ref[:, LANES : 2 * LANES] * SCORE_SCALE
    values = qkv_ref[:, 2 * LANES :]
    valid = lax.broadcasted_iota(jnp.int32, (keys.shape[0], 1), 0) < length
    context_grad = product(low_ref[...], out_ref[...], NT).astype(BF16)
    heads = zip(head_halves(qkv_ref[:, :LANES]), head_halves(keys), head_halves(context_grad))
    sums = [None, None, None]
    for head, (query, key, grad) in enumerate(heads):
        scores = jnp.where(valid, product(keys, query, NT), -1000000000.0)
        probs = jnp.exp(scores - total_ref[0, 0, head : head + 1, :])
        grad_probs = product(values, grad, NT)
        weighted = probs * grad_probs
        inner = jnp.sum(weighted, axis=0, keepdims=True)
        grad_scores = (weighted - probs * inner).astype(BF16)
        parts = (
            product(grad_scores, key, TN),
            product(grad_scores, query, NN),
            product(probs.astype(BF16), grad, NN),
        )
        sums = [b if a is None else a + b for a, b in zip(sums, parts)]
    grads = [sums[0].astype(BF16), (sums[1] * SCORE_SCALE).astype(BF16), sums[2].astype(BF16)]
    grads = jnp.concatenate(grads, axis=1)
    rows_part = product(grads, weight_ref[...], NT)
    weight_part = product(rows_ref[...], grads, TN)
    columns = pl.ds(pl.multiple_of(lanes * 3 * LANES, LANES), 3 * LANES)
    column_sums = jnp.sum(grads.astype(F32).reshape(-1, 8, 3 * LANES), axis=0)

    @pl.when(lanes == 0)
    def _():
        rows_sum[...] = base_ref[...] + rows_part

    @pl.when(lanes > 0)
    def _():
        rows_sum[...] += rows_part

    @pl.when(lanes == pl.num_programs(1) - 1)
    def _():
        rows_grad_ref[...] = rows_sum[...].astype(rows_grad_ref.dtype)

    @pl.when(step == 0)
    def _():
        weight_sum[:, columns] = weight_part
        sums_ref[:, columns] = column_sums

    @pl.when(step > 0)
    def _():
        weight_sum[:, columns] += weight_part
        sums_ref[:, columns] += column_sums

    @pl.when(step == pl.num_programs(0) - 1)
    def _():
        weight_grad_ref[:, columns] = weight_sum[:, columns].astype(weight_grad_ref.dtype)


def attend_back(meta, lengths, qkv, low_grad, out, totals, rows, weight, base, rows_type):
    pairs = totals.shape[0]
    width, columns = weight.shape
    span, blocks = rows.shape[0] // pairs, columns // (3 * LANES)
    by_pair = lambda pair, lanes, meta: (pair, 0)
    whole = lambda pair, lanes, meta: (0, 0)
    inputs = [
        (lengths, pl.BlockSpec(memory_space=pltpu.SMEM)),
        (qkv, pl.BlockSpec((span, 3 * LANES), lambda pair, lanes, meta: (pair, lanes))),
        (low_grad, pl.BlockSpec((span, width), by_pair)),
        (out, pl.BlockSpec((LANES, width), lambda pair, lanes, meta: (lanes, 0))),
        (totals, pl.BlockSpec((1, 1, 2, span), lambda pair, lanes, meta: (pair, lanes, 0, 0))),
        (rows, pl.BlockSpec((span, width), by_pair)),
        (weight, pl.BlockSpec((width, 3 * LANES), lambda pair, lanes, meta: (0, lanes))),
        (base, pl.BlockSpec((span, width), by_pair)),
    ]
    return call(
        attend_back_kernel,
        "attend_back",
        meta,
        (pairs, blocks),
        inputs,
        [
            (rows.shape, rows_type, pl.BlockSpec((span, width), by_pair)),
            ((width, columns), BF16, pl.BlockSpec((width, columns), whole)),
            ((8, columns), F32, pl.BlockSpec((8, columns), whole)),
        ],
        flops=0,
        moved=1024,
        scratch=[pltpu.VMEM((span, width), F32), pltpu.VMEM((width, columns), F32)],
    )


def move_kernel(moves, source_count, target_count, meta_ref, *refs):
    sources = refs[:source_count]
    targets = refs[source_count : source_count + target_count]
    rest = refs[source_count + target_count :]
    buffers, arrived, left = rest[: len(moves)], rest[-2], rest[-1]
    incoming, outgoing = [], []
    for number, (source, row, column, target, to_row, to_column, rows, columns) in enumerate(moves):
        into = sources[source].at[pl.ds(row(meta_ref), rows), pl.ds(column, columns)]
        onto = targets[target].at[pl.ds(to_row(meta_ref), rows), pl.ds(to_column, columns)]
        incoming.append(pltpu.make_async_copy(into, buffers[number], arrived.at[number]))
        outgoing.append(pltpu.make_async_copy(buffers[number], onto, left.at[number]))
    for copy in incoming:
        copy.start()
    for copy_in, copy_out in zip(incoming, outgoing):
        copy_in.wait()
        copy_out.start()
    for copy in outgoing:
        copy.wait()


def pieces(entry):
    source, row, column, target, to_row, to_column, rows, columns = entry
    count = next((n for n in (4, 2) if rows % (16 * n) == 0 and rows * columns >= n * 2**16), 1)
    step = rows // count
    return [
        (
            source,
            functools.partial(lambda meta_ref, base, at: pl.multiple_of(base(meta_ref) + at, 16), base=row, at=i * step)
            if rows % 16 == 0
            else row,
            column,
            target,
            functools.partial(
                lambda meta_ref, base, at: pl.multiple_of(base(meta_ref) + at, 16), base=to_row, at=i * step
            )
            if rows % 16 == 0
            else to_row,
            to_column,
            step,
            columns,
        )
        for i in range(count)
    ]


def move(name, meta, sources, targets, moves):
    moves = [part for entry in moves for part in pieces(entry)]
    return call(
        functools.partial(move_kernel, moves, len(sources), len(targets)),
        name,
        meta,
        (1,),
        [(source, pl.BlockSpec(memory_space=pl.ANY)) for source in sources],
        [(shape, BF16, pl.BlockSpec(memory_space=pl.ANY)) for shape in targets],
        flops=0,
        moved=4 * sum(entry[6] * entry[7] for entry in moves),
        scratch=[pltpu.VMEM(entry[6:], BF16) for entry in moves]
        + [pltpu.SemaphoreType.DMA((len(moves),))] * 2,
    )


def fixed(row):
    return lambda meta_ref: row


def by_place(entry, rows, other=False, offset=0):
    def start(meta_ref):
        place = 1 - meta_ref[entry] if other else meta_ref[entry]
        return pl.multiple_of(place * rows + offset, 16)

    return start


def pack_qkv_kernel(blocks, meta_ref, weight_ref, whole_ref, quarter_ref, buffer, arrived, left):
    copies = []
    for kind in range(3):
        for block in range(blocks):
            number = 3 * block + kind
            copies.append(
                pltpu.make_async_copy(
                    weight_ref.at[kind, :, pl.ds(block * LANES, LANES)],
                    buffer.at[:, pl.ds(number * LANES, LANES)],
                    arrived.at[number],
                )
            )
    for copy in copies:
        copy.start()
    for copy in copies:
        copy.wait()
    quarter = quarter_ref.shape[0]
    mine = pl.ds(pl.multiple_of((2 * meta_ref[0] + meta_ref[2]) * quarter, 16), quarter)
    out = [
        pltpu.make_async_copy(buffer.at[mine], quarter_ref, left.at[0]),
        pltpu.make_async_copy(buffer, whole_ref, left.at[1]),
    ]
    for copy in out:
        copy.start()
    for copy in out:
        copy.wait()


def pack_qkv(meta, weight):
    kinds, rows, columns = weight.shape
    shapes = [(rows, kinds * columns), (rows // 4, kinds * columns)]
    return call(
        functools.partial(pack_qkv_kernel, columns // LANES),
        "pack_qkv",
        meta,
        (1,),
        [(weight, pl.BlockSpec(memory_space=pl.ANY))],
        [(shape, BF16, pl.BlockSpec(memory_space=pl.ANY)) for shape in shapes],
        flops=0,
        moved=5 * weight.size,
        scratch=[
            pltpu.VMEM(shapes[0], BF16),
            pltpu.SemaphoreType.DMA((kinds * columns // LANES,)),
            pltpu.SemaphoreType.DMA((2,)),
        ],
    )


def pack(meta, out_weight, up_weight, down_weight):
    out, up, down = [weight.shape[0] // 2 for weight in (out_weight, up_weight, down_weight)]
    width, units = out_weight.shape[1], up_weight.shape[1]
    fold = units // width
    part = out // fold
    moves = [(1, by_place(0, up), 0, 0, fixed(0), 0, up, units)]
    for i in range(fold):
        moves.append((0, by_place(0, out, offset=i * part), 0, 0, fixed(up), i * width, part, width))
    moves.append((2, by_place(0, down), 0, 1, fixed(0), 0, down, width))
    return move(
        "pack",
        meta,
        [out_weight, up_weight, down_weight],
        [(up + part, units), (down, width)],
        moves,
    )


def unpack(meta, mine, other, out_shape, up_shape):
    out, up = out_shape[0] // 2, up_shape[0] // 2
    width, units = out_shape[1], up_shape[1]
    fold = units // width
    part = out // fold
    moves = []
    for source in (0, 1):
        for i in range(fold):
            onto = by_place(0, out, other=bool(source), offset=i * part)
            moves.append((source, fixed(up), i * width, 0, onto, 0, part, width))
    for source in (0, 1):
        moves.append((source, fixed(0), 0, 1, by_place(0, up, other=bool(source)), 0, up, units))
    return move("unpack", meta, [mine, other], [out_shape, up_shape], moves)


def join(meta, entry, mine, other, name):
    rows, columns = mine[0].shape
    count = len(mine)
    moves = []
    for own in (0, 1):
        for i in range(count):
            onto = by_place(entry, rows * count, other=bool(own), offset=i * rows)
            moves.append((own * count + i, fixed(0), 0, 0, onto, 0, rows, columns))
    return move(name, meta, [*mine, *other], [(2 * count * rows, columns)], moves)[0]


def join_quarters(meta, mine, other):
    half, columns = mine.shape
    quarter = half // 2
    moves = []
    for source in (0, 1):
        for part in (0, 1):

            def onto(meta_ref, source=source, part=part):
                core = 1 - meta_ref[0] if source else meta_ref[0]
                chip = 1 - meta_ref[2] if part else meta_ref[2]
                return pl.multiple_of((2 * core + chip) * quarter, 16)

            moves.append((source, fixed(part * quarter), 0, 0, onto, 0, quarter, columns))
    return move("join_qkv", meta, [mine, other], [(2 * half, columns)], moves)[0]


def normalized(rows):
    row_mean = jnp.mean(rows, axis=-1, keepdims=True)
    centered = rows - row_mean
    variance = jnp.mean(centered * centered, axis=-1, keepdims=True)
    scale = lax.rsqrt(variance + NORM_EPSILON)
    return centered * scale, scale


def norm_back(grad, xhat, scale, gain):
    inner = grad * gain
    mean = jnp.mean(inner, axis=-1, keepdims=True)
    along = jnp.mean(inner * xhat, axis=-1, keepdims=True)
    return scale * (inner - mean - xhat * along)


def low(value):
    return value.astype(BF16).astype(F32)


def gelu_pair(value):
    cdf = 0.5 + 0.5 * lax.erf(value * HALF_ROOT)
    slope = cdf + value * (jnp.exp(-0.5 * value * value) * INVERSE_ROOT_TWO_PI)
    return (value * cdf).astype(BF16), slope.astype(BF16)


def by_lane_pair(weight):
    count, rows, columns = weight.shape
    return weight.reshape(count, rows, -1, LANES).transpose(1, 2, 0, 3).reshape(rows, -1)


def swap_tensor(block):
    return lax.ppermute(block, "tensor", [(0, 1), (1, 0)])


def swap_dp(block, devices, stride):
    return lax.ppermute(block, "dp", [(place, place ^ stride) for place in range(devices)])


def boundary(*values):
    return lax.optimization_barrier(values)


def eighths(rows):
    return jnp.sum(rows.astype(F32).reshape(-1, 8, rows.shape[1]), axis=0)


def columns_of(*sums):
    stacked = jnp.concatenate(sums) if len(sums) > 1 else sums[0]
    owner = lax.broadcasted_iota(jnp.int32, (stacked.shape[0], LANES), 0) // 8
    lane = lax.broadcasted_iota(jnp.int32, (stacked.shape[0], LANES), 1)
    return product(stacked.astype(BF16), (owner == lane).astype(BF16), TN)


def halve_kernel(sides, meta_ref, *refs):
    send_ref, keep_ref = refs[-2:]
    core = meta_ref[0]
    number = 0
    for side, parts in enumerate(sides):
        column = 0
        for width in parts:
            first, second = refs[number][:, 0], refs[number][:, 1]
            columns = slice(column, column + width)
            send_ref[side, :, :, columns] = jnp.where(core == 0, second, first)
            keep_ref[side, :, :, columns] = jnp.where(core == 0, first, second)
            number, column = number + 1, column + width


def halve(meta, sides, devices):
    parts = [part.astype(BF16) for side in sides for part in side]
    rows = parts[0].shape[0] // devices
    widths = [[part.shape[1] for part in side] for side in sides]
    shape = (len(sides), devices // 2, rows, sum(widths[0]))
    step = devices // 4
    out_spec = pl.BlockSpec((len(sides), step) + shape[2:], lambda place, meta: (0, place, 0, 0))
    return call(
        functools.partial(halve_kernel, widths),
        "halve",
        meta,
        (2,),
        [
            (
                part.reshape(devices // 2, 2, rows, part.shape[1]),
                pl.BlockSpec((step, 2, rows, part.shape[1]), lambda place, meta: (place, 0, 0, 0)),
            )
            for part in parts
        ],
        [(shape, BF16, out_spec)] * 2,
        flops=0,
        moved=1024,
    )


def total_of(terms):
    total = terms[0].astype(F32)
    for term in terms[1:]:
        total = total + term.astype(F32)
    return total


def spread_kernel(meta_ref, *refs):
    out_ref = refs[-1]
    total = sum(ref[...].astype(F32) for ref in refs[:-1])
    for block in range(total.shape[1] // (3 * LANES)):
        for kind in range(3):
            start = (3 * block + kind) * LANES
            out_ref[kind, :, block * LANES : (block + 1) * LANES] = total[:, start : start + LANES]


def spread(meta, terms, columns):
    rows = terms[0].shape[0]
    spec = pl.BlockSpec((rows, 3 * columns), lambda i, meta: (0, 0))
    shape = (3, rows, columns)
    return call(
        spread_kernel,
        "spread",
        meta,
        (1,),
        [(term, spec) for term in terms],
        [(shape, F32, pl.BlockSpec(shape, lambda i, meta: (0, 0, 0)))],
        flops=0,
        moved=1024,
    )[0]


class Reduction:
    def __init__(self, sides, devices, plan, meta=None):
        self.devices = devices
        self.plan = list(plan)
        self.left = list(range(devices.bit_length() - 2, -1, -1))
        self.sides = len(sides)
        if meta is not None:
            self.stage = self.plan.pop(0)
            self.left.remove(self.stage)
            self.send, kept = halve(meta, sides, devices)
            self.terms = [kept]
            return
        cut, here = self.halving(self.plan.pop(0))

        def pick(index):
            picked = []
            for parts in sides:
                beside = [
                    self.half(part.astype(BF16).reshape(1, devices, -1, part.shape[1]), cut, index)
                    for part in parts
                ]
                picked.append(jnp.concatenate(beside, axis=-1))
            return jnp.concatenate(picked) if len(picked) > 1 else picked[0]

        self.send, self.terms = pick(1 - here), [pick(here)]

    def halving(self, stage):
        self.stage = stage
        where = self.left.index(stage)
        self.left.remove(stage)
        return 2**where, lax.axis_index("dp") // 2**stage % 2

    def half(self, term, before, index):
        sides, places, rows, columns = term.shape
        cut = term.reshape(sides * before, 2, places // before // 2, rows, columns)
        kept = lax.dynamic_index_in_dim(cut, index, 1, keepdims=False)
        return kept.reshape(sides, places // 2, rows, columns)

    def start(self):
        if self.stage == "x":
            self.received = swap_tensor(self.send)
        else:
            self.received = swap_dp(self.send, self.devices, 2**self.stage)

    def step(self):
        self.advance()
        self.start()

    def advance(self):
        self.terms.append(self.received)
        terms, stage = self.terms, self.plan.pop(0)
        if terms[0].shape[1] == self.devices // 2:
            terms = [total_of(terms)]
        if stage == "x":
            self.stage = stage
            self.send = total_of([term[-1:] for term in terms]).astype(BF16)
            self.terms = [total_of([term[:-1] for term in terms])] if self.sides > 1 else []
            self.sides = 1
        else:
            cut, here = self.halving(stage)
            self.send = total_of([self.half(term, cut, 1 - here) for term in terms]).astype(BF16)
            self.terms = [total_of([self.half(term, cut, here) for term in terms])]

    def finish(self):
        while self.plan:
            self.step()
        self.terms.append(self.received)
        return total_of([term.reshape(term.shape[-2:]) for term in self.terms])


def body(
    hidden_in,
    pair_lengths,
    candidates,
    qkv_weight,
    qv_bias,
    out_weight,
    out_bias,
    norm1_gain,
    norm1_shift,
    up_weight,
    up_bias,
    down_weight,
    down_bias,
    norm2_gain,
    norm2_shift,
    out_cotangent,
    *,
    devices,
):
    pairs = pair_lengths.shape[0] // 2
    width = hidden_in.shape[1]
    local = qv_bias.shape[1]
    row_count = hidden_in.shape[0] // 2
    span = row_count // pairs
    place, tensor = lax.axis_index("dp"), lax.axis_index("tensor")
    meta = jnp.stack([place % 2, tensor, place // 2 % 2]).astype(jnp.int32)
    bits = list(range(1, devices.bit_length() - 1))

    def own(array, size):
        return lax.dynamic_slice_in_dim(array, tensor * size, size, 0)

    qkv_local_weight, qkv_piece = pack_qkv(meta, qkv_weight)
    qkv_mine = swap_tensor(qkv_piece)
    biases_other = swap_tensor(jnp.concatenate([qv_bias.reshape(-1), up_bias]))
    out_up_piece, down_piece = pack(meta, out_weight, up_weight, down_weight)
    out_up_mine = swap_tensor(out_up_piece)
    rows = own(hidden_in, row_count)

    def qkv_bias(bias):
        return by_lane_pair(jnp.stack([bias[0], jnp.zeros_like(bias[0]), bias[1]]).reshape(3, 1, local))

    bias_local = qkv_bias(qv_bias)
    rows, bias_local, qkv_local_weight, out_up_piece, down_piece, qkv_mine, biases_other = boundary(
        rows, bias_local, qkv_local_weight, out_up_piece, down_piece, qkv_mine, biases_other
    )
    qkv_next = swap_dp(qkv_mine, devices, 2)
    qkv_local, context_local, totals_local = attend(
        meta, pair_lengths, rows, qkv_local_weight, bias_local, pairs
    )
    context_local, qkv_next = boundary(context_local, qkv_next)
    qkv_half = jnp.concatenate([qkv_mine, qkv_next])
    qkv_remote_weight = join_quarters(meta, qkv_half, swap_dp(qkv_half, devices, 1))
    remote_bias = biases_other[: 2 * local].reshape(2, local)
    qkv_remote, context_remote, totals_remote = attend(
        meta, pair_lengths, rows, qkv_remote_weight, qkv_bias(remote_bias), pairs
    )
    context_local, context_remote, out_up_mine = boundary(context_local, context_remote, out_up_mine)
    down_mine = swap_tensor(down_piece)
    out_up_other = swap_dp(out_up_mine, devices, 1)
    part_local = product(context_local, out_weight, NN).astype(BF16)
    out_up_mine, out_up_other, part_local = boundary(out_up_mine, out_up_other, part_local)
    out_remote_weight, up_remote_weight = unpack(
        meta, out_up_mine, out_up_other, out_weight.shape, up_weight.shape
    )
    part_remote = low(product(context_remote, out_remote_weight, NN))
    residual = rows.astype(F32) + (part_local.astype(F32) + part_remote) + out_bias
    xhat_one, scale_one = normalized(residual)
    normed_one = xhat_one * norm1_gain + norm1_shift
    normed = normed_one.astype(BF16)

    def expand(weight, bias):
        return boundary(*gelu_pair(product(normed, weight, NN) + bias))

    act_local, slope_local = expand(up_weight, up_bias)
    ff_local = product(act_local, down_weight, NN).astype(BF16)
    act_remote, slope_remote = expand(up_remote_weight, biases_other[2 * local :])
    act_remote, down_mine, ff_local = boundary(act_remote, down_mine, ff_local)
    down_other = swap_dp(down_mine, devices, 1)
    down_remote_weight = join(meta, 0, [down_mine], [down_other], "join_down")
    ff_remote = low(product(act_remote, down_remote_weight, NN))
    xhat, scale = normalized(normed_one + (ff_local.astype(F32) + ff_remote) + down_bias)
    block_mine = (xhat * norm2_gain + norm2_shift).astype(BF16)

    counts = own(candidates, pairs).astype(F32)[:, None, None]
    grad_output = own(out_cotangent, row_count).astype(F32).reshape(pairs, span, width) / counts
    grad_output = grad_output.reshape(row_count, width)
    grad_two = norm_back(grad_output, xhat, scale, norm2_gain)
    grad_two_low = grad_two.astype(BF16)
    sums = [eighths(grad_two), eighths(grad_output * xhat), eighths(grad_output)]
    grad_two_low, block_mine = boundary(grad_two_low, block_mine)
    block_other = swap_tensor(block_mine)

    def weight_grad(left, right):
        return product(left, right, TN).astype(BF16)

    down_sum = Reduction(
        [[weight_grad(grad_two_low, act_local)], [weight_grad(grad_two_low, act_remote)]],
        devices,
        [0] + bits[:1] + ["x"] + bits[1:],
    )
    grad_two_low, down_sum.send = boundary(grad_two_low, down_sum.send)
    down_sum.start()
    grad_pre = []
    for weight, slope in ((down_weight, slope_local), (down_remote_weight, slope_remote)):
        grad_pre.append((product(grad_two_low, weight, NT) * slope.astype(F32)).astype(BF16))
    pre_local, pre_remote, down_sum.received = boundary(*grad_pre, down_sum.received)
    down_sum.step()
    grad_normed = (
        grad_two + product(pre_local, up_weight, NT) + product(pre_remote, up_remote_weight, NT)
    )
    grad_one = norm_back(grad_normed, xhat_one, scale_one, norm1_gain)
    grad_one_low = grad_one.astype(BF16)
    sums += [eighths(grad_one), eighths(grad_normed * xhat_one), eighths(grad_normed)]
    shared = columns_of(*sums)

    def extras(pre):
        zero = jnp.zeros((8, pre.shape[1]), F32)
        sums_up = eighths(pre)
        first = columns_of(*[zero] * len(sums), sums_up).reshape(devices, 2, -1, LANES)[:, 0]
        second = columns_of(*[zero] * len(sums), zero, sums_up).reshape(devices, 2, -1, LANES)[:, 1]
        return shared + (first + second).reshape(width, LANES)

    wide_sum = Reduction(
        [
            [weight_grad(normed, pre), weight_grad(grad_one_low, context), extras(pre)]
            for pre, context in ((pre_local, context_local), (pre_remote, context_remote))
        ],
        devices,
        [0] + bits[1:] + bits[:1] + ["x"],
    )
    grad_one_low, wide_sum.send = boundary(grad_one_low, wide_sum.send)
    wide_sum.start()
    grad_one_low, wide_sum.received = boundary(grad_one_low, wide_sum.received)
    wide_sum.advance()
    grad_one_low, wide_sum.send, wide_sum.terms, down_sum.terms = boundary(
        grad_one_low, wide_sum.send, wide_sum.terms, down_sum.terms
    )
    wide_sum.start()

    def attention_back(side, base, rows_type):
        qkv, out, totals, weight = {
            "local": (qkv_local, out_weight, totals_local, qkv_local_weight),
            "remote": (qkv_remote, out_remote_weight, totals_remote, qkv_remote_weight),
        }[side]
        return attend_back(
            meta, pair_lengths, qkv, grad_one_low, out, totals, rows, weight, base, rows_type
        )

    def qv_columns(sums_qv):
        column = columns_of(sums_qv).reshape(-1, 3, LANES, LANES)
        column = [column[:, kind].reshape(devices, -1, LANES) for kind in (0, 2)]
        return jnp.concatenate(column, axis=1).reshape(width, LANES)

    rows_part, far_grad, far_sums = attention_back("remote", grad_one, F32)
    far_sum = Reduction([[far_grad, qv_columns(far_sums)]], devices, [0, "x"], meta)
    (far_sum.send,) = boundary(far_sum.send)
    far_sum.start()
    rows_part, down_sum.received, wide_sum.received, block_other = boundary(
        rows_part, down_sum.received, wide_sum.received, block_other
    )
    down_sum.advance()
    wide_sum.advance()
    rows_part, far_sum.received, down_sum.send, wide_sum.send = boundary(
        rows_part, far_sum.received, down_sum.send, wide_sum.send
    )
    wide_sum.start()
    far_sum.advance()
    rows_part, far_sum.send = boundary(rows_part, far_sum.send)
    far_sum.start()
    down_sum.start()
    grad_in, near_grad, near_sums = attention_back("local", rows_part, BF16)
    near_grad, down_sum.received, wide_sum.received = boundary(
        near_grad, down_sum.received, wide_sum.received
    )
    down_sum.step()
    other_in = swap_tensor(grad_in)
    near_sum = Reduction([[near_grad, qv_columns(near_sums)]], devices, [0] + bits, meta)
    near_sum.send, block_mine = boundary(near_sum.send, block_mine)
    near_sum.start()
    near_sum.received, far_sum.received = boundary(near_sum.received, far_sum.received)
    near_sum.terms.append(far_sum.received)
    near_sum.step()
    near_sum.send, wide_sum.received, down_sum.received = boundary(
        near_sum.send, wide_sum.received, down_sum.received
    )
    wide_sum.step()
    down_sum.step()
    wide_sum.send, block_mine = boundary(wide_sum.send, block_mine)
    block_out = join(meta, 1, [block_mine], [block_other], "join_block")
    near_sum.received, wide_sum.send, down_sum.send, block_out = boundary(
        near_sum.received, wide_sum.send, down_sum.send, block_out
    )
    near_sum.step()
    near_sum.received, wide_sum.received = boundary(near_sum.received, wide_sum.received)
    while near_sum.plan:
        near_sum.step()
    wide_sum.step()
    near_sum.send, grad_in, down_sum.received = boundary(near_sum.send, grad_in, down_sum.received)
    share_down = down_sum.finish().T
    wide = wide_sum.finish()
    units = up_weight.shape[1]
    vectors = wide[:, units + local :].T
    near_terms = [term.reshape(term.shape[-2:]) for term in near_sum.terms + [near_sum.received]]
    share_qkv = spread(meta, near_terms, local)
    share_qv = total_of([term[:, 3 * local] for term in near_terms]).reshape(2, -1)
    return (
        block_out,
        join(meta, 1, [grad_in], [other_in], "join_in"),
        share_qkv,
        share_qv,
        wide[:, units : units + local].T,
        vectors[3],
        vectors[4],
        vectors[5],
        wide[:, :units],
        vectors[6:8].reshape(-1),
        share_down,
        vectors[0],
        vectors[1],
        vectors[2],
    )


def solution(mesh):
    devices = mesh.shape["dp"]
    in_specs = (
        P("dp", None),
        P("dp"),
        P("dp"),
        P(None, None, "tensor"),
        P(None, "tensor"),
        P("tensor", None),
        P(),
        P(),
        P(),
        P(None, "tensor"),
        P("tensor"),
        P("tensor", None),
        P(),
        P(),
        P(),
        P("dp", None),
    )
    out_specs = (
        P("dp", None),
        P("dp", None),
        P(None, "dp", "tensor"),
        P(None, ("tensor", "dp")),
        P("tensor", "dp"),
        P("dp"),
        P("dp"),
        P("dp"),
        P("dp", "tensor"),
        P(("tensor", "dp")),
        P("tensor", "dp"),
        P("dp"),
        P("dp"),
        P("dp"),
    )
    return jax.shard_map(
        functools.partial(body, devices=devices),
        mesh=mesh,
        in_specs=in_specs,
        out_specs=out_specs,
        check_vma=False,
    )
```

```python
import functools

import jax
import jax.numpy as jnp
from jax import lax
from jax.experimental import pallas as pl
from jax.experimental.pallas import tpu as pltpu
from jax.sharding import PartitionSpec as P

HEAD_DIM = 64
LANES = 128
VMEM_BYTES = 60 * 1024 * 1024
NORM_EPSILON = 1e-12
HALF_ROOT = 0.7071067811865476
INVERSE_ROOT_TWO_PI = 0.3989422804014327
SCORE_SCALE = HEAD_DIM ** (-0.5)
NT = (((1,), (1,)), ((), ()))
NN = (((1,), (0,)), ((), ()))
TN = (((0,), (0,)), ((), ()))
F32 = jnp.float32
BF16 = jnp.bfloat16


def product(left, right, dims):
    return lax.dot_general(left, right, dims, preferred_element_type=F32)


def head_halves(block):
    lane = lax.broadcasted_iota(jnp.int32, (1, LANES), 1)
    zero = jnp.zeros_like(block)
    return jnp.where(lane < HEAD_DIM, block, zero), jnp.where(lane < HEAD_DIM, zero, block)


def call(kernel, name, meta, grid, inputs, outputs, flops, moved, exps=0, scratch=()):
    return pl.pallas_call(
        kernel,
        out_shape=[jax.ShapeDtypeStruct(shape, dtype) for shape, dtype, spec in outputs],
        grid_spec=pltpu.PrefetchScalarGridSpec(
            num_scalar_prefetch=1,
            grid=grid,
            in_specs=[spec for array, spec in inputs],
            out_specs=[spec for shape, dtype, spec in outputs],
            scratch_shapes=list(scratch),
        ),
        cost_estimate=pl.CostEstimate(flops=0, bytes_accessed=1024, transcendentals=0),
        name=name,
    )(meta, *[array for array, spec in inputs])


def attend_kernel(meta_ref, length_ref, rows_ref, weight_ref, bias_ref, qkv_ref, context_ref, total_ref):
    length = length_ref[meta_ref[1] * pl.num_programs(0) + pl.program_id(0)]
    qkv = (product(rows_ref[...], weight_ref[...], NN) + bias_ref[...]).astype(BF16)
    qkv_ref[...] = qkv
    keys = qkv[:, LANES : 2 * LANES] * SCORE_SCALE
    valid = lax.broadcasted_iota(jnp.int32, (keys.shape[0], 1), 0) < length
    heads = zip(head_halves(qkv[:, :LANES]), head_halves(qkv[:, 2 * LANES :]))
    flipped = None
    for head, (query, value) in enumerate(heads):
        scores = jnp.where(valid, product(keys, query, NT), -1000000000.0)
        peak = jnp.max(scores, axis=0, keepdims=True)
        exponent = jnp.exp(scores - peak)
        total = jnp.sum(exponent, axis=0, keepdims=True)
        probs_low = (exponent * (1.0 / total)).astype(BF16)
        part = product(value, probs_low, TN)
        flipped = part if flipped is None else flipped + part
        total_ref[0, 0, head : head + 1, :] = peak + jnp.log(total)
    context_ref[...] = flipped.T.astype(BF16)


def attend(meta, lengths, rows, weight, bias, pairs):
    row_count, width = rows.shape
    columns = weight.shape[1]
    span, blocks = row_count // pairs, columns // (3 * LANES)
    work = row_count * span * blocks * LANES
    by_block = lambda pair, lanes, meta: (pair, lanes)
    return call(
        attend_kernel,
        "attend",
        meta,
        (pairs, blocks),
        [
            (lengths, pl.BlockSpec(memory_space=pltpu.SMEM)),
            (rows, pl.BlockSpec((span, width), lambda pair, lanes, meta: (pair, 0))),
            (weight, pl.BlockSpec((width, 3 * LANES), lambda pair, lanes, meta: (0, lanes))),
            (bias, pl.BlockSpec((1, 3 * LANES), lambda pair, lanes, meta: (0, lanes))),
        ],
        [
            ((row_count, columns), BF16, pl.BlockSpec((span, 3 * LANES), by_block)),
            ((row_count, blocks * LANES), BF16, pl.BlockSpec((span, LANES), by_block)),
            (
                (pairs, blocks, 2, span),
                F32,
                pl.BlockSpec((1, 1, 2, span), lambda pair, lanes, meta: (pair, lanes, 0, 0)),
            ),
        ],
        flops=16 * work,
        moved=8 * row_count * blocks * LANES,
        exps=work // HEAD_DIM,
    )


def attend_back_kernel(
    meta_ref,
    length_ref,
    qkv_ref,
    low_ref,
    out_ref,
    total_ref,
    rows_ref,
    weight_ref,
    base_ref,
    rows_grad_ref,
    weight_grad_ref,
    sums_ref,
    rows_sum,
    weight_sum,
):
    step, lanes = pl.program_id(0), pl.program_id(1)
    length = length_ref[meta_ref[1] * pl.num_programs(0) + step]
    keys = qkv_ref[:, LANES : 2 * LANES] * SCORE_SCALE
    values = qkv_ref[:, 2 * LANES :]
    valid = lax.broadcasted_iota(jnp.int32, (keys.shape[0], 1), 0) < length
    context_grad = product(low_ref[...], out_ref[...], NT).astype(BF16)
    heads = zip(head_halves(qkv_ref[:, :LANES]), head_halves(keys), head_halves(context_grad))
    sums = [None, None, None]
    for head, (query, key, grad) in enumerate(heads):
        scores = jnp.where(valid, product(keys, query, NT), -1000000000.0)
        probs = jnp.exp(scores - total_ref[0, 0, head : head + 1, :])
        grad_probs = product(values, grad, NT)
        weighted = probs * grad_probs
        inner = jnp.sum(weighted, axis=0, keepdims=True)
        grad_scores = (weighted - probs * inner).astype(BF16)
        parts = (
            product(grad_scores, key, TN),
            product(grad_scores, query, NN),
            product(probs.astype(BF16), grad, NN),
        )
        sums = [b if a is None else a + b for a, b in zip(sums, parts)]
    grads = [sums[0].astype(BF16), (sums[1] * SCORE_SCALE).astype(BF16), sums[2].astype(BF16)]
    grads = jnp.concatenate(grads, axis=1)
    rows_part = product(grads, weight_ref[...], NT)
    weight_part = product(rows_ref[...], grads, TN)
    columns = pl.ds(pl.multiple_of(lanes * 3 * LANES, LANES), 3 * LANES)
    column_sums = jnp.sum(grads.astype(F32).reshape(-1, 8, 3 * LANES), axis=0)

    @pl.when(lanes == 0)
    def _():
        rows_sum[...] = base_ref[...] + rows_part

    @pl.when(lanes > 0)
    def _():
        rows_sum[...] += rows_part

    @pl.when(lanes == pl.num_programs(1) - 1)
    def _():
        rows_grad_ref[...] = rows_sum[...].astype(rows_grad_ref.dtype)

    @pl.when(step == 0)
    def _():
        weight_sum[:, columns] = weight_part
        sums_ref[:, columns] = column_sums

    @pl.when(step > 0)
    def _():
        weight_sum[:, columns] += weight_part
        sums_ref[:, columns] += column_sums

    @pl.when(step == pl.num_programs(0) - 1)
    def _():
        weight_grad_ref[:, columns] = weight_sum[:, columns].astype(weight_grad_ref.dtype)


def attend_back(meta, lengths, qkv, low_grad, out, totals, rows, weight, base, rows_type):
    pairs = totals.shape[0]
    width, columns = weight.shape
    span, blocks = rows.shape[0] // pairs, columns // (3 * LANES)
    by_pair = lambda pair, lanes, meta: (pair, 0)
    whole = lambda pair, lanes, meta: (0, 0)
    inputs = [
        (lengths, pl.BlockSpec(memory_space=pltpu.SMEM)),
        (qkv, pl.BlockSpec((span, 3 * LANES), lambda pair, lanes, meta: (pair, lanes))),
        (low_grad, pl.BlockSpec((span, width), by_pair)),
        (out, pl.BlockSpec((LANES, width), lambda pair, lanes, meta: (lanes, 0))),
        (totals, pl.BlockSpec((1, 1, 2, span), lambda pair, lanes, meta: (pair, lanes, 0, 0))),
        (rows, pl.BlockSpec((span, width), by_pair)),
        (weight, pl.BlockSpec((width, 3 * LANES), lambda pair, lanes, meta: (0, lanes))),
        (base, pl.BlockSpec((span, width), by_pair)),
    ]
    return call(
        attend_back_kernel,
        "attend_back",
        meta,
        (pairs, blocks),
        inputs,
        [
            (rows.shape, rows_type, pl.BlockSpec((span, width), by_pair)),
            ((width, columns), BF16, pl.BlockSpec((width, columns), whole)),
            ((8, columns), F32, pl.BlockSpec((8, columns), whole)),
        ],
        flops=0,
        moved=1024,
        scratch=[pltpu.VMEM((span, width), F32), pltpu.VMEM((width, columns), F32)],
    )


def move_kernel(moves, source_count, target_count, meta_ref, *refs):
    sources = refs[:source_count]
    targets = refs[source_count : source_count + target_count]
    rest = refs[source_count + target_count :]
    buffers, arrived, left = rest[: len(moves)], rest[-2], rest[-1]
    incoming, outgoing = [], []
    for number, (source, row, column, target, to_row, to_column, rows, columns) in enumerate(moves):
        into = sources[source].at[pl.ds(row(meta_ref), rows), pl.ds(column, columns)]
        onto = targets[target].at[pl.ds(to_row(meta_ref), rows), pl.ds(to_column, columns)]
        incoming.append(pltpu.make_async_copy(into, buffers[number], arrived.at[number]))
        outgoing.append(pltpu.make_async_copy(buffers[number], onto, left.at[number]))
    for copy in incoming:
        copy.start()
    for copy_in, copy_out in zip(incoming, outgoing):
        copy_in.wait()
        copy_out.start()
    for copy in outgoing:
        copy.wait()


def pieces(entry):
    source, row, column, target, to_row, to_column, rows, columns = entry
    count = next((n for n in (4, 2) if rows % (16 * n) == 0 and rows * columns >= n * 2**16), 1)
    step = rows // count
    return [
        (
            source,
            functools.partial(lambda meta_ref, base, at: pl.multiple_of(base(meta_ref) + at, 16), base=row, at=i * step)
            if rows % 16 == 0
            else row,
            column,
            target,
            functools.partial(
                lambda meta_ref, base, at: pl.multiple_of(base(meta_ref) + at, 16), base=to_row, at=i * step
            )
            if rows % 16 == 0
            else to_row,
            to_column,
            step,
            columns,
        )
        for i in range(count)
    ]


def move(name, meta, sources, targets, moves):
    moves = [part for entry in moves for part in pieces(entry)]
    return call(
        functools.partial(move_kernel, moves, len(sources), len(targets)),
        name,
        meta,
        (1,),
        [(source, pl.BlockSpec(memory_space=pl.ANY)) for source in sources],
        [(shape, BF16, pl.BlockSpec(memory_space=pl.ANY)) for shape in targets],
        flops=0,
        moved=4 * sum(entry[6] * entry[7] for entry in moves),
        scratch=[pltpu.VMEM(entry[6:], BF16) for entry in moves]
        + [pltpu.SemaphoreType.DMA((len(moves),))] * 2,
    )


def fixed(row):
    return lambda meta_ref: row


def by_place(entry, rows, other=False, offset=0):
    def start(meta_ref):
        place = 1 - meta_ref[entry] if other else meta_ref[entry]
        return pl.multiple_of(place * rows + offset, 16)

    return start


def pack_qkv_kernel(blocks, meta_ref, weight_ref, whole_ref, quarter_ref, buffer, arrived, left):
    copies = []
    for kind in range(3):
        for block in range(blocks):
            number = 3 * block + kind
            copies.append(
                pltpu.make_async_copy(
                    weight_ref.at[kind, :, pl.ds(block * LANES, LANES)],
                    buffer.at[:, pl.ds(number * LANES, LANES)],
                    arrived.at[number],
                )
            )
    for copy in copies:
        copy.start()
    for copy in copies:
        copy.wait()
    quarter = quarter_ref.shape[0]
    mine = pl.ds(pl.multiple_of((2 * meta_ref[0] + meta_ref[2]) * quarter, 16), quarter)
    out = [
        pltpu.make_async_copy(buffer.at[mine], quarter_ref, left.at[0]),
        pltpu.make_async_copy(buffer, whole_ref, left.at[1]),
    ]
    for copy in out:
        copy.start()
    for copy in out:
        copy.wait()


def pack_qkv(meta, weight):
    kinds, rows, columns = weight.shape
    shapes = [(rows, kinds * columns), (rows // 4, kinds * columns)]
    return call(
        functools.partial(pack_qkv_kernel, columns // LANES),
        "pack_qkv",
        meta,
        (1,),
        [(weight, pl.BlockSpec(memory_space=pl.ANY))],
        [(shape, BF16, pl.BlockSpec(memory_space=pl.ANY)) for shape in shapes],
        flops=0,
        moved=5 * weight.size,
        scratch=[
            pltpu.VMEM(shapes[0], BF16),
            pltpu.SemaphoreType.DMA((kinds * columns // LANES,)),
            pltpu.SemaphoreType.DMA((2,)),
        ],
    )


def pack(meta, out_weight, up_weight, down_weight):
    out, up, down = [weight.shape[0] // 2 for weight in (out_weight, up_weight, down_weight)]
    width, units = out_weight.shape[1], up_weight.shape[1]
    fold = units // width
    part = out // fold
    moves = [(1, by_place(0, up), 0, 0, fixed(0), 0, up, units)]
    for i in range(fold):
        moves.append((0, by_place(0, out, offset=i * part), 0, 0, fixed(up), i * width, part, width))
    moves.append((2, by_place(0, down), 0, 1, fixed(0), 0, down, width))
    return move(
        "pack",
        meta,
        [out_weight, up_weight, down_weight],
        [(up + part, units), (down, width)],
        moves,
    )


def unpack(meta, mine, other, out_shape, up_shape):
    out, up = out_shape[0] // 2, up_shape[0] // 2
    width, units = out_shape[1], up_shape[1]
    fold = units // width
    part = out // fold
    moves = []
    for source in (0, 1):
        for i in range(fold):
            onto = by_place(0, out, other=bool(source), offset=i * part)
            moves.append((source, fixed(up), i * width, 0, onto, 0, part, width))
    for source in (0, 1):
        moves.append((source, fixed(0), 0, 1, by_place(0, up, other=bool(source)), 0, up, units))
    return move("unpack", meta, [mine, other], [out_shape, up_shape], moves)


def join(meta, entry, mine, other, name):
    rows, columns = mine[0].shape
    count = len(mine)
    moves = []
    for own in (0, 1):
        for i in range(count):
            onto = by_place(entry, rows * count, other=bool(own), offset=i * rows)
            moves.append((own * count + i, fixed(0), 0, 0, onto, 0, rows, columns))
    return move(name, meta, [*mine, *other], [(2 * count * rows, columns)], moves)[0]


def join_quarters(meta, mine, other):
    half, columns = mine.shape
    quarter = half // 2
    moves = []
    for source in (0, 1):
        for part in (0, 1):

            def onto(meta_ref, source=source, part=part):
                core = 1 - meta_ref[0] if source else meta_ref[0]
                chip = 1 - meta_ref[2] if part else meta_ref[2]
                return pl.multiple_of((2 * core + chip) * quarter, 16)

            moves.append((source, fixed(part * quarter), 0, 0, onto, 0, quarter, columns))
    return move("join_qkv", meta, [mine, other], [(2 * half, columns)], moves)[0]


def normalized(rows):
    row_mean = jnp.mean(rows, axis=-1, keepdims=True)
    centered = rows - row_mean
    variance = jnp.mean(centered * centered, axis=-1, keepdims=True)
    scale = lax.rsqrt(variance + NORM_EPSILON)
    return centered * scale, scale


def norm_back(grad, xhat, scale, gain):
    inner = grad * gain
    mean = jnp.mean(inner, axis=-1, keepdims=True)
    along = jnp.mean(inner * xhat, axis=-1, keepdims=True)
    return scale * (inner - mean - xhat * along)


def low(value):
    return value.astype(BF16).astype(F32)


def gelu_pair(value):
    cdf = 0.5 + 0.5 * lax.erf(value * HALF_ROOT)
    slope = cdf + value * (jnp.exp(-0.5 * value * value) * INVERSE_ROOT_TWO_PI)
    return (value * cdf).astype(BF16), slope.astype(BF16)


def by_lane_pair(weight):
    count, rows, columns = weight.shape
    return weight.reshape(count, rows, -1, LANES).transpose(1, 2, 0, 3).reshape(rows, -1)


def swap_tensor(block):
    return lax.ppermute(block, "tensor", [(0, 1), (1, 0)])


def swap_dp(block, devices, stride):
    return lax.ppermute(block, "dp", [(place, place ^ stride) for place in range(devices)])


def boundary(*values):
    return lax.optimization_barrier(values)


def eighths(rows):
    return jnp.sum(rows.astype(F32).reshape(-1, 8, rows.shape[1]), axis=0)


def columns_of(*sums):
    stacked = jnp.concatenate(sums) if len(sums) > 1 else sums[0]
    owner = lax.broadcasted_iota(jnp.int32, (stacked.shape[0], LANES), 0) // 8
    lane = lax.broadcasted_iota(jnp.int32, (stacked.shape[0], LANES), 1)
    return product(stacked.astype(BF16), (owner == lane).astype(BF16), TN)


def halve_kernel(sides, meta_ref, *refs):
    send_ref, keep_ref = refs[-2:]
    core = meta_ref[0]
    number = 0
    for side, parts in enumerate(sides):
        column = 0
        for width in parts:
            first, second = refs[number][:, 0], refs[number][:, 1]
            columns = slice(column, column + width)
            send_ref[side, :, :, columns] = jnp.where(core == 0, second, first)
            keep_ref[side, :, :, columns] = jnp.where(core == 0, first, second)
            number, column = number + 1, column + width


def halve(meta, sides, devices):
    parts = [part.astype(BF16) for side in sides for part in side]
    rows = parts[0].shape[0] // devices
    widths = [[part.shape[1] for part in side] for side in sides]
    shape = (len(sides), devices // 2, rows, sum(widths[0]))
    step = devices // 4
    out_spec = pl.BlockSpec((len(sides), step) + shape[2:], lambda place, meta: (0, place, 0, 0))
    return call(
        functools.partial(halve_kernel, widths),
        "halve",
        meta,
        (2,),
        [
            (
                part.reshape(devices // 2, 2, rows, part.shape[1]),
                pl.BlockSpec((step, 2, rows, part.shape[1]), lambda place, meta: (place, 0, 0, 0)),
            )
            for part in parts
        ],
        [(shape, BF16, out_spec)] * 2,
        flops=0,
        moved=1024,
    )


def total_of(terms):
    total = terms[0].astype(F32)
    for term in terms[1:]:
        total = total + term.astype(F32)
    return total


def spread_kernel(meta_ref, *refs):
    out_ref = refs[-1]
    total = sum(ref[...].astype(F32) for ref in refs[:-1])
    for block in range(total.shape[1] // (3 * LANES)):
        for kind in range(3):
            start = (3 * block + kind) * LANES
            out_ref[kind, :, block * LANES : (block + 1) * LANES] = total[:, start : start + LANES]


def spread(meta, terms, columns):
    rows = terms[0].shape[0]
    spec = pl.BlockSpec((rows, 3 * columns), lambda i, meta: (0, 0))
    shape = (3, rows, columns)
    return call(
        spread_kernel,
        "spread",
        meta,
        (1,),
        [(term, spec) for term in terms],
        [(shape, F32, pl.BlockSpec(shape, lambda i, meta: (0, 0, 0)))],
        flops=0,
        moved=1024,
    )[0]


class Reduction:
    def __init__(self, sides, devices, plan, meta=None):
        self.devices = devices
        self.plan = list(plan)
        self.left = list(range(devices.bit_length() - 2, -1, -1))
        self.sides = len(sides)
        if meta is not None:
            self.stage = self.plan.pop(0)
            self.left.remove(self.stage)
            self.send, kept = halve(meta, sides, devices)
            self.terms = [kept]
            return
        cut, here = self.halving(self.plan.pop(0))

        def pick(index):
            picked = []
            for parts in sides:
                beside = [
                    self.half(part.astype(BF16).reshape(1, devices, -1, part.shape[1]), cut, index)
                    for part in parts
                ]
                picked.append(jnp.concatenate(beside, axis=-1))
            return jnp.concatenate(picked) if len(picked) > 1 else picked[0]

        self.send, self.terms = pick(1 - here), [pick(here)]

    def halving(self, stage):
        self.stage = stage
        where = self.left.index(stage)
        self.left.remove(stage)
        return 2**where, lax.axis_index("dp") // 2**stage % 2

    def half(self, term, before, index):
        sides, places, rows, columns = term.shape
        cut = term.reshape(sides * before, 2, places // before // 2, rows, columns)
        kept = lax.dynamic_index_in_dim(cut, index, 1, keepdims=False)
        return kept.reshape(sides, places // 2, rows, columns)

    def start(self):
        if self.stage == "x":
            self.received = swap_tensor(self.send)
        else:
            self.received = swap_dp(self.send, self.devices, 2**self.stage)

    def step(self):
        self.advance()
        self.start()

    def advance(self):
        self.terms.append(self.received)
        terms, stage = self.terms, self.plan.pop(0)
        if terms[0].shape[1] == self.devices // 2:
            terms = [total_of(terms)]
        if stage == "x":
            self.stage = stage
            self.send = total_of([term[-1:] for term in terms]).astype(BF16)
            self.terms = [total_of([term[:-1] for term in terms])] if self.sides > 1 else []
            self.sides = 1
        else:
            cut, here = self.halving(stage)
            self.send = total_of([self.half(term, cut, 1 - here) for term in terms]).astype(BF16)
            self.terms = [total_of([self.half(term, cut, here) for term in terms])]

    def finish(self):
        while self.plan:
            self.step()
        self.terms.append(self.received)
        return total_of([term.reshape(term.shape[-2:]) for term in self.terms])


def body(
    hidden_in,
    pair_lengths,
    candidates,
    qkv_weight,
    qv_bias,
    out_weight,
    out_bias,
    norm1_gain,
    norm1_shift,
    up_weight,
    up_bias,
    down_weight,
    down_bias,
    norm2_gain,
    norm2_shift,
    out_cotangent,
    *,
    devices,
):
    pairs = pair_lengths.shape[0] // 2
    width = hidden_in.shape[1]
    local = qv_bias.shape[1]
    row_count = hidden_in.shape[0] // 2
    span = row_count // pairs
    place, tensor = lax.axis_index("dp"), lax.axis_index("tensor")
    meta = jnp.stack([place % 2, tensor, place // 2 % 2]).astype(jnp.int32)
    bits = list(range(1, devices.bit_length() - 1))

    def own(array, size):
        return lax.dynamic_slice_in_dim(array, tensor * size, size, 0)

    qkv_local_weight, qkv_piece = pack_qkv(meta, qkv_weight)
    qkv_mine = swap_tensor(qkv_piece)
    biases_other = swap_tensor(jnp.concatenate([qv_bias.reshape(-1), up_bias]))
    out_up_piece, down_piece = pack(meta, out_weight, up_weight, down_weight)
    out_up_mine = swap_tensor(out_up_piece)
    rows = own(hidden_in, row_count)

    def qkv_bias(bias):
        return by_lane_pair(jnp.stack([bias[0], jnp.zeros_like(bias[0]), bias[1]]).reshape(3, 1, local))

    bias_local = qkv_bias(qv_bias)
    rows, bias_local, qkv_local_weight, out_up_piece, down_piece, qkv_mine, biases_other = boundary(
        rows, bias_local, qkv_local_weight, out_up_piece, down_piece, qkv_mine, biases_other
    )
    qkv_next = swap_dp(qkv_mine, devices, 2)
    qkv_local, context_local, totals_local = attend(
        meta, pair_lengths, rows, qkv_local_weight, bias_local, pairs
    )
    context_local, qkv_next = boundary(context_local, qkv_next)
    qkv_half = jnp.concatenate([qkv_mine, qkv_next])
    qkv_remote_weight = join_quarters(meta, qkv_half, swap_dp(qkv_half, devices, 1))
    remote_bias = biases_other[: 2 * local].reshape(2, local)
    qkv_remote, context_remote, totals_remote = attend(
        meta, pair_lengths, rows, qkv_remote_weight, qkv_bias(remote_bias), pairs
    )
    context_local, context_remote, out_up_mine = boundary(context_local, context_remote, out_up_mine)
    down_mine = swap_tensor(down_piece)
    out_up_other = swap_dp(out_up_mine, devices, 1)
    part_local = product(context_local, out_weight, NN).astype(BF16)
    out_up_mine, out_up_other, part_local = boundary(out_up_mine, out_up_other, part_local)
    out_remote_weight, up_remote_weight = unpack(
        meta, out_up_mine, out_up_other, out_weight.shape, up_weight.shape
    )
    part_remote = low(product(context_remote, out_remote_weight, NN))
    residual = rows.astype(F32) + (part_local.astype(F32) + part_remote) + out_bias
    xhat_one, scale_one = normalized(residual)
    normed_one = xhat_one * norm1_gain + norm1_shift
    normed = normed_one.astype(BF16)

    def expand(weight, bias):
        return boundary(*gelu_pair(product(normed, weight, NN) + bias))

    act_local, slope_local = expand(up_weight, up_bias)
    ff_local = product(act_local, down_weight, NN).astype(BF16)
    act_remote, slope_remote = expand(up_remote_weight, biases_other[2 * local :])
    act_remote, down_mine, ff_local = boundary(act_remote, down_mine, ff_local)
    down_other = swap_dp(down_mine, devices, 1)
    down_remote_weight = join(meta, 0, [down_mine], [down_other], "join_down")
    ff_remote = low(product(act_remote, down_remote_weight, NN))
    xhat, scale = normalized(normed_one + (ff_local.astype(F32) + ff_remote) + down_bias)
    block_mine = (xhat * norm2_gain + norm2_shift).astype(BF16)

    counts = own(candidates, pairs).astype(F32)[:, None, None]
    grad_output = own(out_cotangent, row_count).astype(F32).reshape(pairs, span, width) / counts
    grad_output = grad_output.reshape(row_count, width)
    grad_two = norm_back(grad_output, xhat, scale, norm2_gain)
    grad_two_low = grad_two.astype(BF16)
    sums = [eighths(grad_two), eighths(grad_output * xhat), eighths(grad_output)]
    grad_two_low, block_mine = boundary(grad_two_low, block_mine)
    block_other = swap_tensor(block_mine)

    def weight_grad(left, right):
        return product(left, right, TN).astype(BF16)

    down_sum = Reduction(
        [[weight_grad(grad_two_low, act_local)], [weight_grad(grad_two_low, act_remote)]],
        devices,
        [0] + bits[:1] + ["x"] + bits[1:],
    )
    grad_two_low, down_sum.send = boundary(grad_two_low, down_sum.send)
    down_sum.start()
    grad_pre = []
    for weight, slope in ((down_weight, slope_local), (down_remote_weight, slope_remote)):
        grad_pre.append((product(grad_two_low, weight, NT) * slope.astype(F32)).astype(BF16))
    pre_local, pre_remote, down_sum.received = boundary(*grad_pre, down_sum.received)
    down_sum.step()
    grad_normed = (
        grad_two + product(pre_local, up_weight, NT) + product(pre_remote, up_remote_weight, NT)
    )
    grad_one = norm_back(grad_normed, xhat_one, scale_one, norm1_gain)
    grad_one_low = grad_one.astype(BF16)
    sums += [eighths(grad_one), eighths(grad_normed * xhat_one), eighths(grad_normed)]
    shared = columns_of(*sums)

    def extras(pre):
        zero = jnp.zeros((8, pre.shape[1]), F32)
        sums_up = eighths(pre)
        first = columns_of(*[zero] * len(sums), sums_up).reshape(devices, 2, -1, LANES)[:, 0]
        second = columns_of(*[zero] * len(sums), zero, sums_up).reshape(devices, 2, -1, LANES)[:, 1]
        return shared + (first + second).reshape(width, LANES)

    wide_sum = Reduction(
        [
            [weight_grad(normed, pre), weight_grad(grad_one_low, context), extras(pre)]
            for pre, context in ((pre_local, context_local), (pre_remote, context_remote))
        ],
        devices,
        [0] + bits[1:] + bits[:1] + ["x"],
    )
    grad_one_low, wide_sum.send = boundary(grad_one_low, wide_sum.send)
    wide_sum.start()
    grad_one_low, wide_sum.received = boundary(grad_one_low, wide_sum.received)
    wide_sum.advance()
    grad_one_low, wide_sum.send, wide_sum.terms, down_sum.terms = boundary(
        grad_one_low, wide_sum.send, wide_sum.terms, down_sum.terms
    )
    wide_sum.start()

    def attention_back(side, base, rows_type):
        qkv, out, totals, weight = {
            "local": (qkv_local, out_weight, totals_local, qkv_local_weight),
            "remote": (qkv_remote, out_remote_weight, totals_remote, qkv_remote_weight),
        }[side]
        return attend_back(
            meta, pair_lengths, qkv, grad_one_low, out, totals, rows, weight, base, rows_type
        )

    def qv_columns(sums_qv):
        column = columns_of(sums_qv).reshape(-1, 3, LANES, LANES)
        column = [column[:, kind].reshape(devices, -1, LANES) for kind in (0, 2)]
        return jnp.concatenate(column, axis=1).reshape(width, LANES)

    rows_part, far_grad, far_sums = attention_back("remote", grad_one, F32)
    far_sum = Reduction([[far_grad, qv_columns(far_sums)]], devices, [0, "x"], meta)
    (far_sum.send,) = boundary(far_sum.send)
    far_sum.start()
    rows_part, down_sum.received, wide_sum.received, block_other = boundary(
        rows_part, down_sum.received, wide_sum.received, block_other
    )
    down_sum.advance()
    wide_sum.advance()
    rows_part, far_sum.received, down_sum.send, wide_sum.send = boundary(
        rows_part, far_sum.received, down_sum.send, wide_sum.send
    )
    wide_sum.start()
    far_sum.advance()
    rows_part, far_sum.send = boundary(rows_part, far_sum.send)
    far_sum.start()
    down_sum.start()
    grad_in, near_grad, near_sums = attention_back("local", rows_part, BF16)
    near_grad, down_sum.received, wide_sum.received = boundary(
        near_grad, down_sum.received, wide_sum.received
    )
    down_sum.step()
    other_in = swap_tensor(grad_in)
    near_sum = Reduction([[near_grad, qv_columns(near_sums)]], devices, [0] + bits, meta)
    near_sum.send, block_mine = boundary(near_sum.send, block_mine)
    near_sum.start()
    near_sum.received, far_sum.received = boundary(near_sum.received, far_sum.received)
    near_sum.terms.append(far_sum.received)
    near_sum.step()
    near_sum.send, wide_sum.received, down_sum.received = boundary(
        near_sum.send, wide_sum.received, down_sum.received
    )
    wide_sum.step()
    down_sum.step()
    wide_sum.send, block_mine = boundary(wide_sum.send, block_mine)
    block_out = join(meta, 1, [block_mine], [block_other], "join_block")
    near_sum.received, wide_sum.send, down_sum.send, block_out = boundary(
        near_sum.received, wide_sum.send, down_sum.send, block_out
    )
    near_sum.step()
    near_sum.received, wide_sum.received = boundary(near_sum.received, wide_sum.received)
    while near_sum.plan:
        near_sum.step()
    wide_sum.step()
    near_sum.send, grad_in, down_sum.received = boundary(near_sum.send, grad_in, down_sum.received)
    share_down = down_sum.finish().T
    wide = wide_sum.finish()
    units = up_weight.shape[1]
    vectors = wide[:, units + local :].T
    near_terms = [term.reshape(term.shape[-2:]) for term in near_sum.terms + [near_sum.received]]
    share_qkv = spread(meta, near_terms, local)
    share_qv = total_of([term[:, 3 * local] for term in near_terms]).reshape(2, -1)
    share_qkv, share_qv, grad_in = boundary(share_qkv, share_qv, grad_in)
    return (
        block_out,
        join(meta, 1, [grad_in], [other_in], "join_in"),
        share_qkv,
        share_qv,
        wide[:, units : units + local].T,
        vectors[3],
        vectors[4],
        vectors[5],
        wide[:, :units],
        vectors[6:8].reshape(-1),
        share_down,
        vectors[0],
        vectors[1],
        vectors[2],
    )


def solution(mesh):
    devices = mesh.shape["dp"]
    in_specs = (
        P("dp", None),
        P("dp"),
        P("dp"),
        P(None, None, "tensor"),
        P(None, "tensor"),
        P("tensor", None),
        P(),
        P(),
        P(),
        P(None, "tensor"),
        P("tensor"),
        P("tensor", None),
        P(),
        P(),
        P(),
        P("dp", None),
    )
    out_specs = (
        P("dp", None),
        P("dp", None),
        P(None, "dp", "tensor"),
        P(None, ("tensor", "dp")),
        P("tensor", "dp"),
        P("dp"),
        P("dp"),
        P("dp"),
        P("dp", "tensor"),
        P(("tensor", "dp")),
        P("tensor", "dp"),
        P("dp"),
        P("dp"),
        P("dp"),
    )
    return jax.shard_map(
        functools.partial(body, devices=devices),
        mesh=mesh,
        in_specs=in_specs,
        out_specs=out_specs,
        check_vma=False,
    )
```
